32 devices in a mesh: groups: 2 (over y), frame: 16 (over z, x, core).
Axes of the slice: x: 2, y: 2, z: 4, core: 2. Of those that a mesh axis runs over, the one named last changes fastest.
Arguments:
- queries: bfloat16 [8192, 1536], P(('groups', 'frame')), parts along dimension 0, may hold values from -14 to 14
- key_heads: bfloat16 [8192, 1536], P(('groups', 'frame')), parts along dimension 0, may hold values from -14 to 14
- value_heads: bfloat16 [8192, 1536], P(('groups', 'frame')), parts along dimension 0, may hold values from -6 to 6
- tile_lists: int32 [16, 8], P('frame'), may hold values from 0 to 1
Outputs:
- attended: bfloat16 [8192, 1536], P(('groups', 'frame')), parts along dimension 0
The draws below stay inside these ranges and needn't reach their ends.
There are 2 independent parts, one for each index of `groups`. The reference program is written for one: setup_inputs(seed, part) draws one part's arguments, and reference() takes and returns one part's arrays. A program takes and returns all parts, laid end to end along the dimension named above; an argument that names none is the same for every part. Nothing has to cross between parts.
Inputs may be any that keep to these rules, and one draw needn't show every extreme that they name: `tile_lists`: entry l of a frame's row names a block of the frame 2^l before it, entry 4 + l one of the frame 2^l after it; entries for frames outside the video are not read.
All inputs are finite; a program needn't handle non-finite values.
Results may differ from the reference program's by a relative error of at most 0.0049.
Values may be sent and summed in bfloat16 or wider, within the bound.
A program may use at most 64 MiB of HBM per device.

```python
import math
import jax
import jax.numpy as jnp
from jax import lax

HEADS = 12
HD = 128
TILE = 128
TF = 2
LEVELS = 4
FRAMES = 16
TOKENS = 4096
HC = 1536


def pair_draw(key):
    shape = (TOKENS, HEADS * HD)
    query_base = 1.4 * jnp.clip(jax.random.normal(jax.random.fold_in(key, 11), shape, jnp.float32), -4.0, 4.0)
    key_base = 1.4 * jnp.clip(jax.random.normal(jax.random.fold_in(key, 12), shape, jnp.float32), -4.0, 4.0)
    return (query_base, key_base)


def draw_queries(key, part):
    return pair_draw(key)[0].astype(jnp.bfloat16)


def draw_key_heads(key, part):
    return pair_draw(key)[1].astype(jnp.bfloat16)


def place_ends(entries, stream_key, smallest, high):
    longest = entries.shape.index(max(entries.shape))
    spots = []
    for shift in (0, 1):
        where = [jax.random.randint(jax.random.fold_in(stream_key, axis), (), 0, length) for axis, length in enumerate(entries.shape)]
        where[longest] = (where[longest] + shift) % entries.shape[longest]
        spots.append(tuple(where))
    return entries.at[spots[0]].set(smallest).at[spots[1]].set(high)


def steps_of(rng, shape, split, least, largest):
    def one(dim, blocks):
        heights = jax.random.uniform(jax.random.fold_in(jax.random.fold_in(rng, 6), dim), (blocks,), jnp.float32, least / len(split), largest / len(split))
        return jnp.repeat(jnp.exp(heights), shape[dim] // blocks).reshape((-1,) + (1,) * (len(shape) - dim - 1))

    gain = one(*split[0])
    for cut in split[1:]:
        gain = gain * one(*cut)
    return gain


def centred(key, dims, scale, bound, shards=(), kind=jnp.bfloat16):
    result = scale * jax.random.normal(key, dims, jnp.float32)
    if shards:
        result = result * steps_of(key, dims, shards, -0.22, 0.18)
    return jnp.clip(result, -bound, bound).astype(kind)


def setup_inputs(seed: int = 0, part: int = 0) -> dict:
    seeds = jax.random.split(jax.random.key(seed), 5)
    own_keys = jax.random.split(jax.random.fold_in(seeds[4], part), 5)
    return {
        "queries": draw_queries(jax.random.fold_in(jax.random.fold_in(seeds[4], part), 71), part),
        "key_heads": draw_key_heads(jax.random.fold_in(jax.random.fold_in(seeds[4], part), 71), part),
        "value_heads": centred(own_keys[2], (TOKENS, HC), 1.5, 6.0, ((0, 16),)),
        "tile_lists": place_ends(jax.random.randint(seeds[3], (FRAMES, 2 * LEVELS), 0, TF), jax.random.fold_in(seeds[3], 1), 0, TF - 1).astype(jnp.int32),
    }


def attend_block(block_queries, block_keys, block_values, usable):
    scale = 1.0 / math.sqrt(HD)

    def one_head(head):
        offset = head * HD
        head_queries = lax.dynamic_slice_in_dim(block_queries, offset, HD, 1)
        head_keys = lax.dynamic_slice_in_dim(block_keys, offset, HD, 1)
        head_values = lax.dynamic_slice_in_dim(block_values, offset, HD, 1)
        scores = lax.dot_general(head_queries, head_keys, (((1,), (1,)), ((), ())), preferred_element_type=jnp.float32) * scale
        scores = jnp.where(usable[None, :], scores, -jnp.inf)
        peak = lax.optimization_barrier(jnp.max(scores, axis=1, keepdims=True))
        raised = jnp.exp(scores - peak)
        weights = (raised / lax.optimization_barrier(jnp.sum(raised, axis=1, keepdims=True))).astype(jnp.bfloat16)
        return jnp.dot(weights, head_values, preferred_element_type=jnp.float32).astype(jnp.bfloat16)
    per_head = lax.map(one_head, jnp.arange(HEADS, dtype=jnp.int32))
    return jnp.transpose(per_head, (1, 0, 2)).reshape(block_queries.shape[0], HEADS * HD)

def reference(queries, key_heads, value_heads, tile_lists):
    frame_len = TF * TILE
    width = HEADS * HD
    query_frames = queries.reshape(FRAMES, frame_len, width)
    key_frames = key_heads.reshape(FRAMES, frame_len, width)
    value_frames = value_heads.reshape(FRAMES, frame_len, width)

    def per_frame(frame_no):
        own_queries = lax.dynamic_index_in_dim(query_frames, frame_no, 0, keepdims=False)
        own_lists = lax.dynamic_index_in_dim(tile_lists, frame_no, 0, keepdims=False)
        key_parts = [lax.dynamic_index_in_dim(key_frames, frame_no, 0, keepdims=False)]
        value_parts = [lax.dynamic_index_in_dim(value_frames, frame_no, 0, keepdims=False)]
        usable_parts = [jnp.ones((frame_len,), dtype=bool)]
        for upward in (0, 1):
            for level in range(LEVELS):
                distance = 2 ** level
                if upward:
                    source = frame_no + distance
                else:
                    source = frame_no - distance
                inside = (source >= 0) & (source < FRAMES)
                clipped = jnp.clip(source, 0, FRAMES - 1).astype(jnp.int32)
                first_row = (own_lists[upward * LEVELS + level] * TILE).astype(jnp.int32)
                start_index = (clipped, first_row, jnp.int32(0))
                key_parts.append(lax.dynamic_slice(key_frames, start_index, (1, TILE, width))[0])
                value_parts.append(lax.dynamic_slice(value_frames, start_index, (1, TILE, width))[0])
                usable_parts.append(jnp.broadcast_to(inside, (TILE,)))
        return attend_block(own_queries, jnp.concatenate(key_parts, axis=0), jnp.concatenate(value_parts, axis=0), jnp.concatenate(usable_parts, axis=0))
    attended = lax.map(per_frame, jnp.arange(FRAMES, dtype=jnp.int32))
    return attended.reshape(FRAMES * frame_len, width)
```

```python
import functools
import math

import jax
import jax.numpy as jnp
from jax import lax
from jax.experimental import pallas as pl
from jax.experimental.pallas import tpu as pltpu
from jax.sharding import PartitionSpec as P

HD = 128
TILE = 128
PER = 1
MESH = pl.DeviceIdType.MESH
ABSENT = -1e30

CORE, MIRROR, RELAYED, BELOW8, ABOVE8 = range(5)
NEAR = 5
ACROSS, INNER = NEAR, NEAR + 1
OUT_NEAR = NEAR + 2


def kernel(n, levels, heads, q_hbm, k_hbm, v_hbm, own_list, out_ref,
           q_v, k_v, v_v, whole, inside, stage, landed, lists_s, top, total, acc,
           w_send, w_recv, i_send, i_recv, t_send, t_recv, l_send, l_recv, in_sem):
    me = lax.axis_index("frame")
    quarter = me % 4
    x = quarter // 2
    core = me % 2
    core_peer = me + 1 - 2 * core
    across = me + 2 - 4 * x
    mirror = me + 3 - 2 * quarter
    inner = (quarter == 1) | (quarter == 2)
    outer = (quarter == 0) | (quarter == 3)
    has_low, has_high = me >= 4, me + 4 < n
    chunks = heads // PER
    width = PER * HD
    tiles = k_v.shape[0]
    far = [1 << level for level in range(4, levels)]
    yes = me >= 0

    loads = [
        pltpu.make_async_copy(source, target, in_sem.at[i])
        for i, (source, target) in enumerate(((k_hbm, k_v), (v_hbm, v_v), (q_hbm, q_v)))
    ]
    for load in loads:
        load.start()

    partners = [
        (core_peer, yes, 0, 0),
        (across, yes, 1, 1),
        (mirror, yes, 2, 2),
        (me - 4, has_low, 3, 4),
        (me + 4, has_high, 4, 3),
    ]
    for j, d in enumerate(far):
        partners.append((me - d, me >= d, 5 + 2 * j, 6 + 2 * j))
        partners.append((me + d, me + d < n, 6 + 2 * j, 5 + 2 * j))

    barrier = pltpu.get_barrier_semaphore()
    for device, exists, _, _ in partners:
        @pl.when(exists)
        def _():
            pl.semaphore_signal(barrier, inc=1, device_id={"frame": device}, device_id_type=MESH)
    pl.semaphore_wait(barrier, sum(jnp.where(exists, 1, 0) for _, exists, _, _ in partners))

    def columns_of(chunk):
        return pl.ds(pl.multiple_of(chunk * width, width), width)

    def whole_copy(side, chunk, kv):
        source = (k_hbm, v_hbm)[kv]
        return pltpu.make_async_remote_copy(
            src_ref=source.at[:, :, columns_of(chunk)], dst_ref=whole.at[side, chunk, kv],
            send_sem=w_send.at[side, chunk, kv], recv_sem=w_recv.at[side, chunk, kv],
            device_id={"frame": me + 4 if side == 0 else me - 4}, device_id_type=MESH)

    def inner_copy(chunk, kv):
        source = (k_hbm, v_hbm)[kv]
        return pltpu.make_async_remote_copy(
            src_ref=source.at[:, :, columns_of(chunk)], dst_ref=inside.at[chunk, kv],
            send_sem=i_send.at[chunk, kv], recv_sem=i_recv.at[chunk, kv],
            device_id={"frame": across}, device_id_type=MESH)

    def list_copy(device, here, there):
        return pltpu.make_async_remote_copy(
            src_ref=own_list, dst_ref=lists_s.at[there],
            send_sem=l_send.at[here], recv_sem=l_recv.at[there],
            device_id={"frame": device}, device_id_type=MESH)

    def tile_copy(slot, there, chunk, device):
        return pltpu.make_async_remote_copy(
            src_ref=stage.at[slot, chunk], dst_ref=landed.at[there, chunk],
            send_sem=t_send.at[slot, chunk], recv_sem=t_recv.at[there, chunk],
            device_id={"frame": device}, device_id_type=MESH)

    def across_copy(chunk):
        return pltpu.make_async_remote_copy(
            src_ref=stage.at[ACROSS, chunk], dst_ref=inside.at[chunk, :, 0],
            send_sem=t_send.at[ACROSS, chunk], recv_sem=i_recv.at[chunk, 0],
            device_id={"frame": across}, device_id_type=MESH)

    sides = ((has_high, has_low), (has_low, has_high))

    def send_wholes(chunk, carry):
        @pl.when(inner)
        def _():
            for kv in range(2):
                inner_copy(chunk, kv).start()
        for side in range(2):
            @pl.when(sides[side][0])
            def _():
                for kv in range(2):
                    whole_copy(side, chunk, kv).start()
        return carry

    send_wholes(0, 0)
    for device, exists, here, there in partners:
        @pl.when(exists)
        def _():
            list_copy(device, here, there).start()
    lax.fori_loop(1, chunks, send_wholes, 0)

    landings = [
        (MIRROR, inner | ((quarter == 0) & has_low) | ((quarter == 3) & has_high)),
        (RELAYED, ((x == 0) & has_low) | ((x == 1) & has_high)),
        (BELOW8, me >= 8),
        (ABOVE8, me + 8 < n),
    ]
    for j, d in enumerate(far):
        landings.append((NEAR + 2 * j, me >= d))
        landings.append((NEAR + 2 * j + 1, me + d < n))
    for slot, exists in landings:
        @pl.when(jnp.logical_not(exists))
        def _():
            landed[slot] = jnp.zeros(landed.shape[1:], landed.dtype)
    for side in range(2):
        @pl.when(jnp.logical_not(sides[side][1]))
        def _():
            whole[side] = jnp.zeros(whole.shape[1:], whole.dtype)

    for load in loads:
        load.wait()
    for _, exists, here, _ in partners:
        @pl.when(exists)
        def _():
            list_copy(core_peer, here, here).wait_recv()

    def stage_own(slot, chunk, wanted):
        stage[slot, chunk, 0] = k_v[wanted, :, columns_of(chunk)]
        stage[slot, chunk, 1] = v_v[wanted, :, columns_of(chunk)]

    far_sends = []
    for j, d in enumerate(far):
        far_sends.append((OUT_NEAR + 2 * j, NEAR + 2 * j, me + d, me + d < n, 6 + 2 * j, 4 + j))
        far_sends.append((OUT_NEAR + 2 * j + 1, NEAR + 2 * j + 1, me - d, me >= d, 5 + 2 * j, levels + 4 + j))

    def send_own(chunk, carry):
        @pl.when(outer)
        def _():
            stage_own(ACROSS, chunk, lists_s[1, 0, 1 + levels * x])
            across_copy(chunk).start()
        stage_own(CORE, chunk, lists_s[0, 0, levels * core])
        tile_copy(CORE, CORE, chunk, core_peer).start()
        for slot, there, device, exists, here, entry in far_sends:
            @pl.when(exists)
            def _():
                stage_own(slot, chunk, lists_s[here, 0, entry])
                tile_copy(slot, there, chunk, device).start()
        return carry

    lax.fori_loop(0, chunks, send_own, 0)

    factor = math.log2(math.e) / math.sqrt(HD)

    def bias_of(parts):
        return jnp.concatenate(
            [jnp.full((1, size), jnp.where(exists, 0.0, ABSENT), jnp.float32) for size, exists in parts], axis=1)

    near_bias = bias_of([(4 * TILE, yes), (TILE, has_low), (TILE, has_high)])
    late_bias = bias_of([(TILE, exists) for _, exists in landings])

    relays = [
        (RELAYED, RELAYED, across, (x == 0) & has_high, 1, 1, levels + 1),
        (RELAYED, RELAYED, across, (x == 1) & has_low, 0, 1, 1),
        (MIRROR, MIRROR, mirror, (quarter == 0) & has_high, 1, 2, levels),
        (MIRROR, MIRROR, mirror, (quarter == 3) & has_low, 0, 2, 0),
        (BELOW8, BELOW8, me + 4, has_low & has_high, 0, 4, 3),
        (ABOVE8, ABOVE8, me - 4, has_low & has_high, 1, 3, levels + 3),
    ]

    def chosen(blocks, wanted):
        block = blocks(0)
        for tile in range(1, tiles):
            block = jnp.where(wanted == tile, blocks(tile), block)
        return block

    def heads_of(chunk):
        for local in range(PER):
            h = chunk * PER + local
            yield h, pl.ds(local * HD, HD), pl.ds(pl.multiple_of(h * HD, HD), HD)

    def early(chunk, carry):
        for side in range(2):
            @pl.when(sides[side][1])
            def _():
                for kv in range(2):
                    whole_copy(side, chunk, kv).wait_recv()
        for slot, there, device, exists, side, here, entry in relays:
            @pl.when(exists)
            def _():
                wanted = lists_s[here, 0, entry]
                for kv in range(2):
                    stage[slot, chunk, kv] = chosen(lambda tile: whole[side, chunk, kv, tile], wanted)
                tile_copy(slot, there, chunk, device).start()

        @pl.when(outer)
        def _():
            for kv in range(2):
                inner_copy(chunk, kv).wait_recv()
            wanted = lists_s[0, 0, levels * (1 - core)]
            for kv in range(2):
                stage[INNER, chunk, kv] = chosen(lambda tile: inside[chunk, kv, tile], wanted)
            tile_copy(INNER, MIRROR, chunk, core_peer).start()

        @pl.when(inner)
        def _():
            across_copy(chunk).wait_recv()

        tile_copy(CORE, CORE, chunk, core_peer).wait_recv()
        low, high = own_list[0, 2], own_list[0, levels + 2]
        beside = jnp.where(outer, own_list[0, 1 + levels * (1 - x)], 0)
        for h, local, columns in heads_of(chunk):
            def gather(kv):
                own = (k_v, v_v)[kv]
                return jnp.concatenate([
                    own[0, :, columns], own[1, :, columns], landed[CORE, chunk, kv, :, local],
                    chosen(lambda tile: inside[chunk, kv, tile, :, local], beside),
                    chosen(lambda tile: whole[0, chunk, kv, tile, :, local], low),
                    chosen(lambda tile: whole[1, chunk, kv, tile, :, local], high)], axis=0)
            scores = lax.dot_general(
                q_v[:, columns], gather(0), (((1,), (1,)), ((), ())), preferred_element_type=jnp.float32)
            scores = scores + near_bias
            peak = jnp.max(scores, axis=1, keepdims=True)
            raised = jnp.exp2((scores - peak) * factor)
            added = jnp.sum(raised, axis=1, keepdims=True)
            acc[h] = jnp.dot(raised.astype(jnp.bfloat16), gather(1), preferred_element_type=jnp.float32)
            top[h] = jnp.broadcast_to(peak, (peak.shape[0], HD))
            total[h] = jnp.broadcast_to(added, (peak.shape[0], HD))
        return carry

    lax.fori_loop(0, chunks, early, 0)

    def late(chunk, carry):
        for slot, exists in landings:
            @pl.when(exists)
            def _():
                tile_copy(CORE, slot, chunk, core_peer).wait_recv()
        for h, local, columns in heads_of(chunk):
            def gather(kv):
                return jnp.concatenate([landed[slot, chunk, kv, :, local] for slot, _ in landings], axis=0)
            scores = lax.dot_general(
                q_v[:, columns], gather(0), (((1,), (1,)), ((), ())), preferred_element_type=jnp.float32)
            scores = scores + late_bias
            old = top[h][:, :1]
            peak = jnp.maximum(old, jnp.max(scores, axis=1, keepdims=True))
            raised = jnp.exp2((scores - peak) * factor)
            fade = jnp.exp2((old - peak) * factor)
            added = jnp.sum(raised, axis=1, keepdims=True) + fade * total[h][:, :1]
            mixed = jnp.dot(raised.astype(jnp.bfloat16), gather(1), preferred_element_type=jnp.float32)
            mixed = mixed + fade * acc[h]
            out_ref[:, columns] = (mixed / added).astype(out_ref.dtype)
        return carry

    lax.fori_loop(0, chunks, late, 0)

    for _, exists, here, _ in partners:
        @pl.when(exists)
        def _():
            list_copy(core_peer, here, here).wait_send()

    def drain(chunk, carry):
        @pl.when(inner)
        def _():
            for kv in range(2):
                inner_copy(chunk, kv).wait_send()
        for side in range(2):
            @pl.when(sides[side][0])
            def _():
                for kv in range(2):
                    whole_copy(side, chunk, kv).wait_send()
        sent = [(CORE, yes), (ACROSS, outer), (INNER, outer)]
        sent += [(slot, exists) for slot, _, _, exists, _, _ in far_sends]
        sent += [(slot, exists) for slot, _, _, exists, _, _, _ in relays]
        for slot, exists in sent:
            @pl.when(exists)
            def _():
                tile_copy(slot, CORE, chunk, core_peer).wait_send()
        return carry

    lax.fori_loop(0, chunks, drain, 0)


def write_out(in_ref, out_ref, sem):
    copy = pltpu.make_async_copy(in_ref, out_ref, sem)
    copy.start()
    copy.wait()


def solution(mesh):
    n = mesh.shape["frame"]

    def body(queries, key_heads, value_heads, tile_lists):
        rows, channels = queries.shape
        heads = channels // HD
        tiles = rows // TILE
        levels = tile_lists.shape[1] // 2
        far = max(levels - 4, 0)
        chunks = heads // PER
        width = PER * HD
        lists = 5 + 2 * far
        bf16, f32 = jnp.bfloat16, jnp.float32
        hbm = pl.BlockSpec(memory_space=pltpu.HBM)
        dma = pltpu.SemaphoreType.DMA
        out_slots, in_slots = OUT_NEAR + 2 * far, NEAR + 2 * far
        result = pl.pallas_call(
            functools.partial(kernel, n, levels, heads),
            out_shape=pltpu.VMEM((rows, channels), bf16),
            in_specs=[hbm, hbm, hbm, pl.BlockSpec(memory_space=pltpu.SMEM)],
            out_specs=pl.BlockSpec(memory_space=pltpu.VMEM),
            scratch_shapes=[
                pltpu.VMEM((rows, channels), bf16),
                pltpu.VMEM((tiles, TILE, channels), bf16),
                pltpu.VMEM((tiles, TILE, channels), bf16),
                pltpu.VMEM((2, chunks, 2, tiles, TILE, width), bf16),
                pltpu.VMEM((chunks, 2, tiles, TILE, width), bf16),
                pltpu.VMEM((out_slots, chunks, 2, TILE, width), bf16),
                pltpu.VMEM((in_slots, chunks, 2, TILE, width), bf16),
                pltpu.SMEM((lists, 1, 2 * levels), jnp.int32),
                pltpu.VMEM((heads, rows, HD), f32),
                pltpu.VMEM((heads, rows, HD), f32),
                pltpu.VMEM((heads, rows, HD), f32),
                dma((2, chunks, 2)),
                dma((2, chunks, 2)),
                dma((chunks, 2)),
                dma((chunks, 2)),
                dma((out_slots, chunks)),
                dma((in_slots, chunks)),
                dma((lists,)),
                dma((lists,)),
                dma((3,)),
            ],
            compiler_params=pltpu.CompilerParams(
                collective_id=0, has_side_effects=True, vmem_limit_bytes=61 << 20
            ),
        )(
            queries,
            key_heads.reshape(tiles, TILE, channels),
            value_heads.reshape(tiles, TILE, channels),
            tile_lists,
        )
        return pl.pallas_call(
            write_out,
            out_shape=jax.ShapeDtypeStruct((rows, channels), bf16),
            in_specs=[pl.BlockSpec(memory_space=pltpu.VMEM)],
            out_specs=pl.BlockSpec(memory_space=pl.ANY),
            scratch_shapes=[dma],
            compiler_params=pltpu.CompilerParams(vmem_limit_bytes=4 << 20),
        )(result)

    in_specs = (
        P(("groups", "frame"), None),
        P(("groups", "frame"), None),
        P(("groups", "frame"), None),
        P("frame", None),
    )
    return jax.shard_map(
        body, mesh=mesh, in_specs=in_specs, out_specs=P(("groups", "frame"), None), check_vma=False
    )
```

```python
import functools
import math

import jax
import jax.numpy as jnp
from jax import lax
from jax.experimental import pallas as pl
from jax.experimental.pallas import tpu as pltpu
from jax.sharding import PartitionSpec as P

HD = 128
TILE = 128
MESH = pl.DeviceIdType.MESH
ABSENT = -1e30

WHOLE_PIECES = (4, 4, 4)
RELAY_PIECES = (2, 2, 2, 2, 2, 1, 1)

CORE, MIRROR, RELAYED, BELOW8, ABOVE8 = range(5)
NEAR = 5
ACROSS, INNER = NEAR, NEAR + 1
OUT_NEAR = NEAR + 2


def pieces_of(sizes, heads):
    unit = heads // sum(sizes)
    pieces, first = [], 0
    for size in sizes:
        pieces.append((first, size * unit))
        first += size * unit
    return pieces


def kernel(n, levels, heads, q_hbm, k_hbm, v_hbm, own_list, out_ref,
           q_v, k_v, v_v, whole, inside, stage, landed, lists_s, top, total, acc,
           w_send, w_recv, i_send, i_recv, t_send, t_recv, l_send, l_recv, in_sem):
    me = lax.axis_index("frame")
    quarter = me % 4
    x = quarter // 2
    core = me % 2
    core_peer = me + 1 - 2 * core
    across = me + 2 - 4 * x
    mirror = me + 3 - 2 * quarter
    inner = (quarter == 1) | (quarter == 2)
    outer = (quarter == 0) | (quarter == 3)
    has_low, has_high = me >= 4, me + 4 < n
    tiles = k_v.shape[0]
    far = [1 << level for level in range(4, levels)]
    yes = me >= 0
    wholes = pieces_of(WHOLE_PIECES, heads)
    relayed = pieces_of(RELAY_PIECES, heads)

    partners = [
        (core_peer, yes, 0, 0),
        (across, yes, 1, 1),
        (mirror, yes, 2, 2),
        (me - 4, has_low, 3, 4),
        (me + 4, has_high, 4, 3),
    ]
    for j, d in enumerate(far):
        partners.append((me - d, me >= d, 5 + 2 * j, 6 + 2 * j))
        partners.append((me + d, me + d < n, 6 + 2 * j, 5 + 2 * j))

    barrier = pltpu.get_barrier_semaphore()
    for device, exists, _, _ in partners:
        @pl.when(exists)
        def _():
            pl.semaphore_signal(barrier, inc=1, device_id={"frame": device}, device_id_type=MESH)
    loads = [
        pltpu.make_async_copy(source, target, in_sem.at[i])
        for i, (source, target) in enumerate(((k_hbm, k_v), (v_hbm, v_v), (q_hbm, q_v)))
    ]
    for load in loads:
        load.start()
    pl.semaphore_wait(barrier, sum(jnp.where(exists, 1, 0) for _, exists, _, _ in partners))

    def span(piece):
        return pl.ds(piece[0] * HD, piece[1] * HD)

    def whole_copy(side, i, kv):
        columns = span(wholes[i])
        return pltpu.make_async_remote_copy(
            src_ref=(k_hbm, v_hbm)[kv].at[:, :, columns], dst_ref=whole.at[side, kv, :, :, columns],
            send_sem=w_send.at[side, i, kv], recv_sem=w_recv.at[side, i, kv],
            device_id={"frame": me + 4 if side == 0 else me - 4}, device_id_type=MESH)

    def inner_copy(i, kv):
        columns = span(wholes[i])
        return pltpu.make_async_remote_copy(
            src_ref=(k_hbm, v_hbm)[kv].at[:, :, columns], dst_ref=inside.at[kv, :, :, columns],
            send_sem=i_send.at[i, kv], recv_sem=i_recv.at[i, kv],
            device_id={"frame": across}, device_id_type=MESH)

    def across_copy(i):
        columns = span(wholes[i])
        return pltpu.make_async_remote_copy(
            src_ref=stage.at[ACROSS, :, :, columns], dst_ref=inside.at[:, 0, :, columns],
            send_sem=t_send.at[ACROSS, i], recv_sem=i_recv.at[i, 0],
            device_id={"frame": across}, device_id_type=MESH)

    def list_copy(device, here, there):
        return pltpu.make_async_remote_copy(
            src_ref=own_list, dst_ref=lists_s.at[there],
            send_sem=l_send.at[here], recv_sem=l_recv.at[there],
            device_id={"frame": device}, device_id_type=MESH)

    def tile_copy(slot, there, pieces, i, device):
        columns = span(pieces[i])
        return pltpu.make_async_remote_copy(
            src_ref=stage.at[slot, :, :, columns], dst_ref=landed.at[there, :, :, columns],
            send_sem=t_send.at[slot, i], recv_sem=t_recv.at[there, i],
            device_id={"frame": device}, device_id_type=MESH)

    sides = ((has_high, has_low), (has_low, has_high))

    def send_wholes(i):
        for side in range(2):
            @pl.when(sides[side][0])
            def _():
                for kv in range(2):
                    whole_copy(side, i, kv).start()
        @pl.when(inner)
        def _():
            for kv in range(2):
                inner_copy(i, kv).start()

    for i in range(len(wholes)):
        send_wholes(i)
        if i == 0:
            for device, exists, here, there in partners:
                @pl.when(exists)
                def _():
                    list_copy(device, here, there).start()

    landings = [
        (MIRROR, inner | ((quarter == 0) & has_low) | ((quarter == 3) & has_high)),
        (RELAYED, ((x == 0) & has_low) | ((x == 1) & has_high)),
        (BELOW8, me >= 8),
        (ABOVE8, me + 8 < n),
    ]
    for j, d in enumerate(far):
        landings.append((NEAR + 2 * j, me >= d))
        landings.append((NEAR + 2 * j + 1, me + d < n))
    for slot, exists in landings:
        @pl.when(jnp.logical_not(exists))
        def _():
            landed[slot] = jnp.zeros(landed.shape[1:], landed.dtype)
    for side in range(2):
        @pl.when(jnp.logical_not(sides[side][1]))
        def _():
            whole[side] = jnp.zeros(whole.shape[1:], whole.dtype)

    for load in loads:
        load.wait()
    for _, exists, here, _ in partners:
        @pl.when(exists)
        def _():
            list_copy(core_peer, here, here).wait_recv()

    def stage_own(slot, columns, wanted):
        stage[slot, 0, :, columns] = k_v[wanted, :, columns]
        stage[slot, 1, :, columns] = v_v[wanted, :, columns]

    far_sends = []
    for j, d in enumerate(far):
        far_sends.append((OUT_NEAR + 2 * j, NEAR + 2 * j, me + d, me + d < n, 6 + 2 * j, 4 + j))
        far_sends.append((OUT_NEAR + 2 * j + 1, NEAR + 2 * j + 1, me - d, me >= d, 5 + 2 * j, levels + 4 + j))

    for i, piece in enumerate(wholes):
        @pl.when(outer)
        def _():
            stage_own(ACROSS, span(piece), lists_s[1, 0, 1 + levels * x])
            across_copy(i).start()
        stage_own(CORE, span(piece), lists_s[0, 0, levels * core])
        tile_copy(CORE, CORE, wholes, i, core_peer).start()
    for slot, there, device, exists, here, entry in far_sends:
        @pl.when(exists)
        def _():
            for i, piece in enumerate(relayed):
                stage_own(slot, span(piece), lists_s[here, 0, entry])
                tile_copy(slot, there, relayed, i, device).start()

    factor = math.log2(math.e) / math.sqrt(HD)

    def bias_of(parts):
        return jnp.concatenate(
            [jnp.full((1, size), jnp.where(exists, 0.0, ABSENT), jnp.float32) for size, exists in parts], axis=1)

    near_bias = bias_of([((tiles + 2) * TILE, yes), (TILE, has_low), (TILE, has_high)])
    late_bias = bias_of([(TILE, exists) for _, exists in landings])

    relays = [
        (RELAYED, RELAYED, across, (x == 0) & has_high, 1, 1, levels + 1),
        (RELAYED, RELAYED, across, (x == 1) & has_low, 0, 1, 1),
        (MIRROR, MIRROR, mirror, (quarter == 0) & has_high, 1, 2, levels),
        (MIRROR, MIRROR, mirror, (quarter == 3) & has_low, 0, 2, 0),
        (BELOW8, BELOW8, me + 4, has_low & has_high, 0, 4, 3),
        (ABOVE8, ABOVE8, me - 4, has_low & has_high, 1, 3, levels + 3),
    ]

    def chosen(block_of, wanted):
        block = block_of(0)
        for tile in range(1, tiles):
            block = jnp.where(wanted == tile, block_of(tile), block)
        return block

    low, high = own_list[0, 2], own_list[0, levels + 2]
    beside = jnp.where(outer, own_list[0, 1 + levels * (1 - x)], 0)

    def early(h, carry):
        columns = pl.ds(pl.multiple_of(h * HD, HD), HD)

        def gather(kv):
            own = (k_v, v_v)[kv]
            return jnp.concatenate(
                [own[tile, :, columns] for tile in range(tiles)] + [
                    landed[CORE, kv, :, columns],
                    chosen(lambda tile: inside[kv, tile, :, columns], beside),
                    chosen(lambda tile: whole[0, kv, tile, :, columns], low),
                    chosen(lambda tile: whole[1, kv, tile, :, columns], high)], axis=0)
        scores = lax.dot_general(
            q_v[:, columns], gather(0), (((1,), (1,)), ((), ())), preferred_element_type=jnp.float32)
        scores = scores + near_bias
        peak = jnp.max(scores, axis=1, keepdims=True)
        raised = jnp.exp2((scores - peak) * factor)
        added = jnp.sum(raised, axis=1, keepdims=True)
        acc[h] = jnp.dot(raised.astype(jnp.bfloat16), gather(1), preferred_element_type=jnp.float32)
        top[h] = jnp.broadcast_to(peak, (peak.shape[0], HD))
        total[h] = jnp.broadcast_to(added, (peak.shape[0], HD))
        return carry

    for w, (first, size) in enumerate(wholes):
        inside_piece = [r for r, piece in enumerate(relayed) if first <= piece[0] < first + size]
        for side in range(2):
            @pl.when(sides[side][1])
            def _():
                for kv in range(2):
                    whole_copy(side, w, kv).wait_recv()
        for r in inside_piece:
            columns = span(relayed[r])
            for slot, there, device, exists, side, here, entry in relays:
                @pl.when(exists)
                def _():
                    wanted = lists_s[here, 0, entry]
                    for kv in range(2):
                        stage[slot, kv, :, columns] = chosen(lambda tile: whole[side, kv, tile, :, columns], wanted)
                    tile_copy(slot, there, relayed, r, device).start()

        @pl.when(outer)
        def _():
            for kv in range(2):
                inner_copy(w, kv).wait_recv()
            wanted = lists_s[0, 0, levels * (1 - core)]
            for r in inside_piece:
                columns = span(relayed[r])
                for kv in range(2):
                    stage[INNER, kv, :, columns] = chosen(lambda tile: inside[kv, tile, :, columns], wanted)
                tile_copy(INNER, MIRROR, relayed, r, core_peer).start()

        @pl.when(inner)
        def _():
            across_copy(w).wait_recv()

        tile_copy(CORE, CORE, wholes, w, core_peer).wait_recv()
        lax.fori_loop(first, first + size, early, 0)

    def late(h, carry):
        columns = pl.ds(pl.multiple_of(h * HD, HD), HD)

        def gather(kv):
            return jnp.concatenate([landed[slot, kv, :, columns] for slot, _ in landings], axis=0)
        scores = lax.dot_general(
            q_v[:, columns], gather(0), (((1,), (1,)), ((), ())), preferred_element_type=jnp.float32)
        scores = scores + late_bias
        old = top[h][:, :1]
        peak = jnp.maximum(old, jnp.max(scores, axis=1, keepdims=True))
        raised = jnp.exp2((scores - peak) * factor)
        fade = jnp.exp2((old - peak) * factor)
        added = jnp.sum(raised, axis=1, keepdims=True) + fade * total[h][:, :1]
        mixed = jnp.dot(raised.astype(jnp.bfloat16), gather(1), preferred_element_type=jnp.float32)
        mixed = mixed + fade * acc[h]
        out_ref[:, columns] = (mixed / added).astype(out_ref.dtype)
        return carry

    def drain_early():
        for _, exists, here, _ in partners:
            @pl.when(exists)
            def _():
                list_copy(core_peer, here, here).wait_send()
        for i in range(len(wholes)):
            @pl.when(inner)
            def _():
                for kv in range(2):
                    inner_copy(i, kv).wait_send()
            for side in range(2):
                @pl.when(sides[side][0])
                def _():
                    for kv in range(2):
                        whole_copy(side, i, kv).wait_send()
            @pl.when(outer)
            def _():
                across_copy(i).wait_send()
            tile_copy(CORE, CORE, wholes, i, core_peer).wait_send()

    def drain(r):
        sent = [(INNER, outer)]
        sent += [(slot, exists) for slot, _, _, exists, _, _ in far_sends]
        sent += [(slot, exists) for slot, _, _, exists, _, _, _ in relays]
        for slot, exists in sent:
            @pl.when(exists)
            def _():
                tile_copy(slot, CORE, relayed, r, core_peer).wait_send()

    for r, (first, size) in enumerate(relayed):
        for slot, exists in landings:
            @pl.when(exists)
            def _():
                tile_copy(CORE, slot, relayed, r, core_peer).wait_recv()
        lax.fori_loop(first, first + size, late, 0)
        if r == 1:
            drain_early()
        if r >= 2:
            drain(r - 2)
    for r in range(len(relayed) - 2, len(relayed)):
        drain(r)


def write_out(in_ref, out_ref, sem):
    copy = pltpu.make_async_copy(in_ref, out_ref, sem)
    copy.start()
    copy.wait()


def solution(mesh):
    n = mesh.shape["frame"]

    def body(queries, key_heads, value_heads, tile_lists):
        rows, channels = queries.shape
        heads = channels // HD
        tiles = rows // TILE
        levels = tile_lists.shape[1] // 2
        far = max(levels - 4, 0)
        lists = 5 + 2 * far
        bf16, f32 = jnp.bfloat16, jnp.float32
        hbm = pl.BlockSpec(memory_space=pltpu.HBM)
        dma = pltpu.SemaphoreType.DMA
        out_slots, in_slots = OUT_NEAR + 2 * far, NEAR + 2 * far
        result = pl.pallas_call(
            functools.partial(kernel, n, levels, heads),
            out_shape=pltpu.VMEM((rows, channels), bf16),
            in_specs=[hbm, hbm, hbm, pl.BlockSpec(memory_space=pltpu.SMEM)],
            out_specs=pl.BlockSpec(memory_space=pltpu.VMEM),
            scratch_shapes=[
                pltpu.VMEM((rows, channels), bf16),
                pltpu.VMEM((tiles, TILE, channels), bf16),
                pltpu.VMEM((tiles, TILE, channels), bf16),
                pltpu.VMEM((2, 2, tiles, TILE, channels), bf16),
                pltpu.VMEM((2, tiles, TILE, channels), bf16),
                pltpu.VMEM((out_slots, 2, TILE, channels), bf16),
                pltpu.VMEM((in_slots, 2, TILE, channels), bf16),
                pltpu.SMEM((lists, 1, 2 * levels), jnp.int32),
                pltpu.VMEM((heads, rows, HD), f32),
                pltpu.VMEM((heads, rows, HD), f32),
                pltpu.VMEM((heads, rows, HD), f32),
                dma((2, len(WHOLE_PIECES), 2)),
                dma((2, len(WHOLE_PIECES), 2)),
                dma((len(WHOLE_PIECES), 2)),
                dma((len(WHOLE_PIECES), 2)),
                dma((out_slots, len(RELAY_PIECES))),
                dma((in_slots, len(RELAY_PIECES))),
                dma((lists,)),
                dma((lists,)),
                dma((3,)),
            ],
            compiler_params=pltpu.CompilerParams(
                collective_id=0, has_side_effects=True, vmem_limit_bytes=61 << 20
            ),
        )(
            queries,
            key_heads.reshape(tiles, TILE, channels),
            value_heads.reshape(tiles, TILE, channels),
            tile_lists,
        )
        return pl.pallas_call(
            write_out,
            out_shape=jax.ShapeDtypeStruct((rows, channels), bf16),
            in_specs=[pl.BlockSpec(memory_space=pltpu.VMEM)],
            out_specs=pl.BlockSpec(memory_space=pl.ANY),
            scratch_shapes=[dma],
            compiler_params=pltpu.CompilerParams(vmem_limit_bytes=4 << 20),
        )(result)

    in_specs = (
        P(("groups", "frame"), None),
        P(("groups", "frame"), None),
        P(("groups", "frame"), None),
        P("frame", None),
    )
    return jax.shard_map(
        body, mesh=mesh, in_specs=in_specs, out_specs=P(("groups", "frame"), None), check_vma=False
    )
```

```python
import functools
import math

import jax
import jax.numpy as jnp
from jax import lax
from jax.experimental import pallas as pl
from jax.experimental.pallas import tpu as pltpu
from jax.sharding import PartitionSpec as P

HD = 128
TILE = 128
MESH = pl.DeviceIdType.MESH
ABSENT = -1e30

WHOLE_PIECES = (4, 4, 4)
RELAY_PIECES = (4, 4, 2, 1, 1)

CORE, MIRROR, RELAYED, BELOW8, ABOVE8 = range(5)
NEAR = 5
ACROSS, INNER, TO_LOW_END, TO_HIGH_END, END_RELAYED = range(NEAR, NEAR + 5)
OUT_NEAR = NEAR + 5


def pieces_of(sizes, heads):
    unit = heads // sum(sizes)
    pieces, first = [], 0
    for size in sizes:
        pieces.append((first, size * unit))
        first += size * unit
    return pieces


def kernel(n, levels, heads, q_hbm, k_hbm, v_hbm, own_list, out_ref,
           q_v, k_v, v_v, whole, inside, stage, landed, lists_s, top, total, acc,
           w_send, w_recv, i_send, i_recv, t_send, t_recv, l_send, l_recv, in_sem):
    me = lax.axis_index("frame")
    quarter = me % 4
    x = quarter // 2
    core = me % 2
    core_peer = me + 1 - 2 * core
    across = me + 2 - 4 * x
    mirror = me + 3 - 2 * quarter
    inner = (quarter == 1) | (quarter == 2)
    outer = (quarter == 0) | (quarter == 3)
    has_low, has_high = me >= 4, me + 4 < n
    low_corner, high_corner = quarter == 0, quarter == 3
    to_low_end, to_high_end = has_low & (me < 8), has_high & (me + 8 >= n)
    chosen_down, chosen_up = to_low_end & ~low_corner, to_high_end & ~high_corner
    low_chosen, high_chosen = (me + 4 >= n) & ~high_corner, (me < 4) & ~low_corner
    tiles = k_v.shape[0]
    far = [1 << level for level in range(4, levels)]
    yes = me >= 0
    wholes = pieces_of(WHOLE_PIECES, heads)
    relayed = pieces_of(RELAY_PIECES, heads)

    partners = [
        (core_peer, yes, 0, 0),
        (across, yes, 1, 1),
        (mirror, yes, 2, 2),
        (me - 4, has_low, 3, 4),
        (me + 4, has_high, 4, 3),
    ]
    for j, d in enumerate(far):
        partners.append((me - d, me >= d, 5 + 2 * j, 6 + 2 * j))
        partners.append((me + d, me + d < n, 6 + 2 * j, 5 + 2 * j))

    barrier = pltpu.get_barrier_semaphore()
    for device, exists, _, _ in partners:
        @pl.when(exists)
        def _():
            pl.semaphore_signal(barrier, inc=1, device_id={"frame": device}, device_id_type=MESH)
    loads = [
        pltpu.make_async_copy(source, target, in_sem.at[i])
        for i, (source, target) in enumerate(((k_hbm, k_v), (v_hbm, v_v), (q_hbm, q_v)))
    ]
    for load in loads:
        load.start()
    pl.semaphore_wait(barrier, sum(jnp.where(exists, 1, 0) for _, exists, _, _ in partners))

    def span(piece):
        return pl.ds(piece[0] * HD, piece[1] * HD)

    def whole_copy(side, i, kv):
        columns = span(wholes[i])
        return pltpu.make_async_remote_copy(
            src_ref=(k_hbm, v_hbm)[kv].at[:, :, columns], dst_ref=whole.at[side, kv, :, :, columns],
            send_sem=w_send.at[side, i, kv], recv_sem=w_recv.at[side, i, kv],
            device_id={"frame": me + 4 if side == 0 else me - 4}, device_id_type=MESH)

    def inner_copy(i, kv):
        columns = span(wholes[i])
        return pltpu.make_async_remote_copy(
            src_ref=(k_hbm, v_hbm)[kv].at[:, :, columns], dst_ref=inside.at[kv, :, :, columns],
            send_sem=i_send.at[i, kv], recv_sem=i_recv.at[i, kv],
            device_id={"frame": across}, device_id_type=MESH)

    def across_copy(i):
        columns = span(wholes[i])
        return pltpu.make_async_remote_copy(
            src_ref=stage.at[ACROSS, :, :, columns], dst_ref=inside.at[:, 0, :, columns],
            send_sem=t_send.at[ACROSS, i], recv_sem=i_recv.at[i, 0],
            device_id={"frame": across}, device_id_type=MESH)

    def end_copy(slot, side, i):
        columns = span(wholes[i])
        return pltpu.make_async_remote_copy(
            src_ref=stage.at[slot, :, :, columns], dst_ref=whole.at[side, :, 0, :, columns],
            send_sem=t_send.at[slot, i], recv_sem=w_recv.at[side, i, 0],
            device_id={"frame": me + 4 if side == 0 else me - 4}, device_id_type=MESH)

    def list_copy(device, here, there):
        return pltpu.make_async_remote_copy(
            src_ref=own_list, dst_ref=lists_s.at[there],
            send_sem=l_send.at[here], recv_sem=l_recv.at[there],
            device_id={"frame": device}, device_id_type=MESH)

    def tile_copy(slot, there, pieces, i, device):
        columns = span(pieces[i])
        return pltpu.make_async_remote_copy(
            src_ref=stage.at[slot, :, :, columns], dst_ref=landed.at[there, :, :, columns],
            send_sem=t_send.at[slot, i], recv_sem=t_recv.at[there, i],
            device_id={"frame": device}, device_id_type=MESH)

    sides = (
        (has_high & ~chosen_up, has_low & ~low_chosen, has_low & low_chosen),
        (has_low & ~chosen_down, has_high & ~high_chosen, has_high & high_chosen),
    )
    end_sends = [(TO_HIGH_END, 0, chosen_up, 4, 2), (TO_LOW_END, 1, chosen_down, 3, levels + 2)]

    def send_wholes(i):
        for side in range(2):
            @pl.when(sides[side][0])
            def _():
                for kv in range(2):
                    whole_copy(side, i, kv).start()
        @pl.when(inner)
        def _():
            for kv in range(2):
                inner_copy(i, kv).start()

    for device, exists, here, there in partners:
        @pl.when(exists)
        def _():
            list_copy(device, here, there).start()
    for i in range(len(wholes)):
        send_wholes(i)

    landings = [
        (MIRROR, inner | ((quarter == 0) & has_low) | ((quarter == 3) & has_high)),
        (RELAYED, ((x == 0) & has_low) | ((x == 1) & has_high)),
        (BELOW8, me >= 8),
        (ABOVE8, me + 8 < n),
    ]
    for j, d in enumerate(far):
        landings.append((NEAR + 2 * j, me >= d))
        landings.append((NEAR + 2 * j + 1, me + d < n))
    for slot, exists in landings:
        @pl.when(jnp.logical_not(exists))
        def _():
            landed[slot] = jnp.zeros(landed.shape[1:], landed.dtype)
    for side in range(2):
        @pl.when(jnp.logical_not((has_low, has_high)[side]))
        def _():
            whole[side] = jnp.zeros(whole.shape[1:], whole.dtype)

    for load in loads:
        load.wait()
    for _, exists, here, _ in partners:
        @pl.when(exists)
        def _():
            list_copy(core_peer, here, here).wait_recv()

    def stage_own(slot, columns, wanted):
        stage[slot, 0, :, columns] = k_v[wanted, :, columns]
        stage[slot, 1, :, columns] = v_v[wanted, :, columns]

    far_sends = []
    for j, d in enumerate(far):
        far_sends.append((OUT_NEAR + 2 * j, NEAR + 2 * j, me + d, me + d < n, 6 + 2 * j, 4 + j))
        far_sends.append((OUT_NEAR + 2 * j + 1, NEAR + 2 * j + 1, me - d, me >= d, 5 + 2 * j, levels + 4 + j))

    for i, piece in enumerate(wholes):
        for slot, side, exists, here, entry in end_sends:
            @pl.when(exists)
            def _():
                stage_own(slot, span(piece), lists_s[here, 0, entry])
                end_copy(slot, side, i).start()
        @pl.when(outer)
        def _():
            stage_own(ACROSS, span(piece), lists_s[1, 0, 1 + levels * x])
            across_copy(i).start()
        stage_own(CORE, span(piece), lists_s[0, 0, levels * core])
        tile_copy(CORE, CORE, wholes, i, core_peer).start()
    for slot, there, device, exists, here, entry in far_sends:
        @pl.when(exists)
        def _():
            for i, piece in enumerate(relayed):
                stage_own(slot, span(piece), lists_s[here, 0, entry])
                tile_copy(slot, there, relayed, i, device).start()

    factor = math.log2(math.e) / math.sqrt(HD)

    def bias_of(parts):
        return jnp.concatenate(
            [jnp.full((1, size), jnp.where(exists, 0.0, ABSENT), jnp.float32) for size, exists in parts], axis=1)

    near_bias = bias_of([((tiles + 2) * TILE, yes), (TILE, has_low), (TILE, has_high)])
    late_bias = bias_of([(TILE, exists) for _, exists in landings])

    relays = [
        (RELAYED, RELAYED, across, (x == 0) & has_high & ((me >= 4) | low_corner), 1, 1, levels + 1),
        (RELAYED, RELAYED, across, (x == 1) & has_low & ((me + 4 < n) | high_corner), 0, 1, 1),
        (MIRROR, MIRROR, mirror, (quarter == 0) & has_high, 1, 2, levels),
        (MIRROR, MIRROR, mirror, (quarter == 3) & has_low, 0, 2, 0),
        (BELOW8, BELOW8, me + 4, has_low & has_high, 0, 4, 3),
        (ABOVE8, ABOVE8, me - 4, has_low & has_high, 1, 3, levels + 3),
    ]

    end_relays = [
        (END_RELAYED, me - 4, to_low_end & high_corner, 3, levels + 1),
        (END_RELAYED, me + 4, to_high_end & low_corner, 4, 1),
    ]

    relays_to_end = (to_low_end & high_corner) | (to_high_end & low_corner)

    def chosen(block_of, wanted):
        block = block_of(0)
        for tile in range(1, tiles):
            block = jnp.where(wanted == tile, block_of(tile), block)
        return block

    low = jnp.where(low_chosen, 0, own_list[0, 2])
    high = jnp.where(high_chosen, 0, own_list[0, levels + 2])
    beside = jnp.where(outer, own_list[0, 1 + levels * (1 - x)], 0)

    def early(h, carry):
        columns = pl.ds(pl.multiple_of(h * HD, HD), HD)

        def gather(kv):
            own = (k_v, v_v)[kv]
            return jnp.concatenate(
                [own[tile, :, columns] for tile in range(tiles)] + [
                    landed[CORE, kv, :, columns],
                    chosen(lambda tile: inside[kv, tile, :, columns], beside),
                    chosen(lambda tile: whole[0, kv, tile, :, columns], low),
                    chosen(lambda tile: whole[1, kv, tile, :, columns], high)], axis=0)
        scores = lax.dot_general(
            q_v[:, columns], gather(0), (((1,), (1,)), ((), ())), preferred_element_type=jnp.float32)
        scores = scores + near_bias
        peak = jnp.max(scores, axis=1, keepdims=True)
        raised = jnp.exp2((scores - peak) * factor)
        added = jnp.sum(raised, axis=1, keepdims=True)
        acc[h] = jnp.dot(raised.astype(jnp.bfloat16), gather(1), preferred_element_type=jnp.float32)
        top[h] = jnp.broadcast_to(peak, (peak.shape[0], HD))
        total[h] = jnp.broadcast_to(added, (peak.shape[0], HD))
        return carry

    for w, (first, size) in enumerate(wholes):
        inside_piece = [r for r, piece in enumerate(relayed) if first <= piece[0] < first + size]
        for side in range(2):
            @pl.when(sides[side][1])
            def _():
                for kv in range(2):
                    whole_copy(side, w, kv).wait_recv()
            @pl.when(sides[side][2])
            def _():
                end_copy(TO_LOW_END, side, w).wait_recv()

        for slot, device, exists, here, entry in end_relays:
            @pl.when(exists)
            def _():
                for kv in range(2):
                    inner_copy(w, kv).wait_recv()
                wanted = lists_s[here, 0, entry]
                for r in inside_piece:
                    columns = span(relayed[r])
                    for kv in range(2):
                        stage[slot, kv, :, columns] = chosen(lambda tile: inside[kv, tile, :, columns], wanted)
                    tile_copy(slot, RELAYED, relayed, r, device).start()

        for r in inside_piece:
            columns = span(relayed[r])
            for slot, there, device, exists, side, here, entry in relays:
                @pl.when(exists)
                def _():
                    wanted = lists_s[here, 0, entry]
                    for kv in range(2):
                        stage[slot, kv, :, columns] = chosen(lambda tile: whole[side, kv, tile, :, columns], wanted)
                    tile_copy(slot, there, relayed, r, device).start()

        @pl.when(outer & ~relays_to_end)
        def _():
            for kv in range(2):
                inner_copy(w, kv).wait_recv()

        @pl.when(outer)
        def _():
            wanted = lists_s[0, 0, levels * (1 - core)]
            for r in inside_piece:
                columns = span(relayed[r])
                for kv in range(2):
                    stage[INNER, kv, :, columns] = chosen(lambda tile: inside[kv, tile, :, columns], wanted)
                tile_copy(INNER, MIRROR, relayed, r, core_peer).start()

        @pl.when(inner)
        def _():
            across_copy(w).wait_recv()

        tile_copy(CORE, CORE, wholes, w, core_peer).wait_recv()
        lax.fori_loop(first, first + size, early, 0)

    def late(h, carry):
        columns = pl.ds(pl.multiple_of(h * HD, HD), HD)

        def gather(kv):
            return jnp.concatenate([landed[slot, kv, :, columns] for slot, _ in landings], axis=0)
        scores = lax.dot_general(
            q_v[:, columns], gather(0), (((1,), (1,)), ((), ())), preferred_element_type=jnp.float32)
        scores = scores + late_bias
        old = top[h][:, :1]
        peak = jnp.maximum(old, jnp.max(scores, axis=1, keepdims=True))
        raised = jnp.exp2((scores - peak) * factor)
        fade = jnp.exp2((old - peak) * factor)
        added = jnp.sum(raised, axis=1, keepdims=True) + fade * total[h][:, :1]
        mixed = jnp.dot(raised.astype(jnp.bfloat16), gather(1), preferred_element_type=jnp.float32)
        mixed = mixed + fade * acc[h]
        out_ref[:, columns] = (mixed / added).astype(out_ref.dtype)
        return carry

    def drain_early():
        for _, exists, here, _ in partners:
            @pl.when(exists)
            def _():
                list_copy(core_peer, here, here).wait_send()
        for i in range(len(wholes)):
            @pl.when(inner)
            def _():
                for kv in range(2):
                    inner_copy(i, kv).wait_send()
            for side in range(2):
                @pl.when(sides[side][0])
                def _():
                    for kv in range(2):
                        whole_copy(side, i, kv).wait_send()
            @pl.when(outer)
            def _():
                across_copy(i).wait_send()
            tile_copy(CORE, CORE, wholes, i, core_peer).wait_send()
            for slot, side, exists, _, _ in end_sends:
                @pl.when(exists)
                def _():
                    end_copy(slot, side, i).wait_send()

    def drain(r):
        sent = [(INNER, outer)]
        sent += [(slot, exists) for slot, _, _, exists, _, _ in far_sends]
        sent += [(slot, exists) for slot, _, _, exists, _, _, _ in relays]
        sent += [(slot, exists) for slot, _, exists, _, _ in end_relays]
        for slot, exists in sent:
            @pl.when(exists)
            def _():
                tile_copy(slot, CORE, relayed, r, core_peer).wait_send()

    for r, (first, size) in enumerate(relayed):
        for slot, exists in landings:
            @pl.when(exists)
            def _():
                tile_copy(CORE, slot, relayed, r, core_peer).wait_recv()
        lax.fori_loop(first, first + size, late, 0)
        if r == 0:
            drain_early()
        if r >= 1:
            drain(r - 1)
    drain(len(relayed) - 1)


def write_out(in_ref, out_ref, sem):
    copy = pltpu.make_async_copy(in_ref, out_ref, sem)
    copy.start()
    copy.wait()


def solution(mesh):
    n = mesh.shape["frame"]

    def body(queries, key_heads, value_heads, tile_lists):
        rows, channels = queries.shape
        heads = channels // HD
        tiles = rows // TILE
        levels = tile_lists.shape[1] // 2
        far = max(levels - 4, 0)
        lists = 5 + 2 * far
        bf16, f32 = jnp.bfloat16, jnp.float32
        hbm = pl.BlockSpec(memory_space=pltpu.HBM)
        dma = pltpu.SemaphoreType.DMA
        out_slots, in_slots = OUT_NEAR + 2 * far, NEAR + 2 * far
        result = pl.pallas_call(
            functools.partial(kernel, n, levels, heads),
            out_shape=pltpu.VMEM((rows, channels), bf16),
            in_specs=[hbm, hbm, hbm, pl.BlockSpec(memory_space=pltpu.SMEM)],
            out_specs=pl.BlockSpec(memory_space=pltpu.VMEM),
            scratch_shapes=[
                pltpu.VMEM((rows, channels), bf16),
                pltpu.VMEM((tiles, TILE, channels), bf16),
                pltpu.VMEM((tiles, TILE, channels), bf16),
                pltpu.VMEM((2, 2, tiles, TILE, channels), bf16),
                pltpu.VMEM((2, tiles, TILE, channels), bf16),
                pltpu.VMEM((out_slots, 2, TILE, channels), bf16),
                pltpu.VMEM((in_slots, 2, TILE, channels), bf16),
                pltpu.SMEM((lists, 1, 2 * levels), jnp.int32),
                pltpu.VMEM((heads, rows, HD), f32),
                pltpu.VMEM((heads, rows, HD), f32),
                pltpu.VMEM((heads, rows, HD), f32),
                dma((2, len(WHOLE_PIECES), 2)),
                dma((2, len(WHOLE_PIECES), 2)),
                dma((len(WHOLE_PIECES), 2)),
                dma((len(WHOLE_PIECES), 2)),
                dma((out_slots, len(RELAY_PIECES))),
                dma((in_slots, len(RELAY_PIECES))),
                dma((lists,)),
                dma((lists,)),
                dma((3,)),
            ],
            compiler_params=pltpu.CompilerParams(
                collective_id=0, has_side_effects=True, vmem_limit_bytes=61 << 20
            ),
        )(
            queries,
            key_heads.reshape(tiles, TILE, channels),
            value_heads.reshape(tiles, TILE, channels),
            tile_lists,
        )
        return pl.pallas_call(
            write_out,
            out_shape=jax.ShapeDtypeStruct((rows, channels), bf16),
            in_specs=[pl.BlockSpec(memory_space=pltpu.VMEM)],
            out_specs=pl.BlockSpec(memory_space=pl.ANY),
            scratch_shapes=[dma],
            compiler_params=pltpu.CompilerParams(vmem_limit_bytes=4 << 20),
        )(result)

    in_specs = (
        P(("groups", "frame"), None),
        P(("groups", "frame"), None),
        P(("groups", "frame"), None),
        P("frame", None),
    )
    return jax.shard_map(
        body, mesh=mesh, in_specs=in_specs, out_specs=P(("groups", "frame"), None), check_vma=False
    )
```

```python
import functools
import math

import jax
import jax.numpy as jnp
from jax import lax
from jax.experimental import pallas as pl
from jax.experimental.pallas import tpu as pltpu
from jax.sharding import PartitionSpec as P

HD = 128
TILE = 128
MESH = pl.DeviceIdType.MESH
ABSENT = -1e30

WHOLE_PIECES = (4, 4, 4)
RELAY_PIECES = (4, 4, 2, 1, 1)

CORE, MIRROR, RELAYED, BELOW8, ABOVE8 = range(5)
NEAR = 5
ACROSS, INNER, TO_LOW_END, TO_HIGH_END, END_RELAYED = range(NEAR, NEAR + 5)
OUT_NEAR = NEAR + 5


def pieces_of(sizes, heads):
    unit = heads // sum(sizes)
    pieces, first = [], 0
    for size in sizes:
        pieces.append((first, size * unit))
        first += size * unit
    return pieces


def kernel(n, levels, heads, q_hbm, k_hbm, v_hbm, own_list, out_ref,
           q_v, k_v, v_v, whole, inside, stage, landed, lists_s, top, total, acc,
           w_send, w_recv, i_send, i_recv, t_send, t_recv, l_send, l_recv, in_sem):
    me = lax.axis_index("frame")
    quarter = me % 4
    x = quarter // 2
    core = me % 2
    core_peer = me + 1 - 2 * core
    across = me + 2 - 4 * x
    mirror = me + 3 - 2 * quarter
    inner = (quarter == 1) | (quarter == 2)
    outer = (quarter == 0) | (quarter == 3)
    has_low, has_high = me >= 4, me + 4 < n
    low_corner, high_corner = quarter == 0, quarter == 3
    to_low_end, to_high_end = has_low & (me < 8), has_high & (me + 8 >= n)
    chosen_down, chosen_up = to_low_end & ~low_corner, to_high_end & ~high_corner
    low_chosen, high_chosen = (me + 4 >= n) & ~high_corner, (me < 4) & ~low_corner
    tiles = k_v.shape[0]
    far = [1 << level for level in range(4, levels)]
    yes = me >= 0
    wholes = pieces_of(WHOLE_PIECES, heads)
    relayed = pieces_of(RELAY_PIECES, heads)

    partners = [
        (core_peer, yes, 0, 0),
        (across, yes, 1, 1),
        (mirror, yes, 2, 2),
        (me - 4, has_low, 3, 4),
        (me + 4, has_high, 4, 3),
    ]
    for j, d in enumerate(far):
        partners.append((me - d, me >= d, 5 + 2 * j, 6 + 2 * j))
        partners.append((me + d, me + d < n, 6 + 2 * j, 5 + 2 * j))

    barrier = pltpu.get_barrier_semaphore()
    for device, exists, _, _ in partners:
        @pl.when(exists)
        def _():
            pl.semaphore_signal(barrier, inc=1, device_id={"frame": device}, device_id_type=MESH)
    loads = [
        pltpu.make_async_copy(source, target, in_sem.at[i])
        for i, (source, target) in enumerate(((k_hbm, k_v), (v_hbm, v_v), (q_hbm, q_v)))
    ]
    for load in loads:
        load.start()
    pl.semaphore_wait(barrier, sum(jnp.where(exists, 1, 0) for _, exists, _, _ in partners))

    def span(piece):
        return pl.ds(piece[0] * HD, piece[1] * HD)

    def whole_copy(side, i, kv):
        columns = span(wholes[i])
        return pltpu.make_async_remote_copy(
            src_ref=(k_hbm, v_hbm)[kv].at[:, :, columns], dst_ref=whole.at[side, kv, :, :, columns],
            send_sem=w_send.at[side, kv], recv_sem=w_recv.at[side, i, kv],
            device_id={"frame": me + 4 if side == 0 else me - 4}, device_id_type=MESH)

    def inner_copy(i, kv):
        columns = span(wholes[i])
        return pltpu.make_async_remote_copy(
            src_ref=(k_hbm, v_hbm)[kv].at[:, :, columns], dst_ref=inside.at[kv, :, :, columns],
            send_sem=i_send.at[kv], recv_sem=i_recv.at[i, kv],
            device_id={"frame": across}, device_id_type=MESH)

    def across_copy(i):
        columns = span(wholes[i])
        return pltpu.make_async_remote_copy(
            src_ref=stage.at[ACROSS, :, :, columns], dst_ref=inside.at[:, 0, :, columns],
            send_sem=t_send.at[ACROSS], recv_sem=i_recv.at[i, 0],
            device_id={"frame": across}, device_id_type=MESH)

    def end_copy(slot, side, i):
        columns = span(wholes[i])
        return pltpu.make_async_remote_copy(
            src_ref=stage.at[slot, :, :, columns], dst_ref=whole.at[side, :, 0, :, columns],
            send_sem=t_send.at[slot], recv_sem=w_recv.at[side, i, 0],
            device_id={"frame": me + 4 if side == 0 else me - 4}, device_id_type=MESH)

    def list_copy(device, here, there):
        return pltpu.make_async_remote_copy(
            src_ref=own_list, dst_ref=lists_s.at[there],
            send_sem=l_send.at[here], recv_sem=l_recv.at[there],
            device_id={"frame": device}, device_id_type=MESH)

    def tile_copy(slot, there, pieces, i, device):
        columns = span(pieces[i])
        return pltpu.make_async_remote_copy(
            src_ref=stage.at[slot, :, :, columns], dst_ref=landed.at[there, :, :, columns],
            send_sem=t_send.at[slot], recv_sem=t_recv.at[there, i],
            device_id={"frame": device}, device_id_type=MESH)

    def parts_of(r):
        return (0, 1) if r == len(relayed) - 1 else (None,)

    def part_copy(slot, there, r, part, device):
        columns = span(relayed[r])
        at = slice(None) if part is None else part
        i = r + (part or 0)
        return pltpu.make_async_remote_copy(
            src_ref=stage.at[slot, at, :, columns], dst_ref=landed.at[there, at, :, columns],
            send_sem=t_send.at[slot], recv_sem=t_recv.at[there, i],
            device_id={"frame": device}, device_id_type=MESH)

    sides = (
        (has_high & ~chosen_up, has_low & ~low_chosen, has_low & low_chosen),
        (has_low & ~chosen_down, has_high & ~high_chosen, has_high & high_chosen),
    )
    end_sends = [(TO_HIGH_END, 0, chosen_up, 4, 2), (TO_LOW_END, 1, chosen_down, 3, levels + 2)]

    def send_lists(chosen_partners):
        for device, exists, here, there in chosen_partners:
            @pl.when(exists)
            def _():
                list_copy(device, here, there).start()

    def send_wholes(i):
        for side in range(2):
            @pl.when(sides[side][0])
            def _():
                for kv in range(2):
                    whole_copy(side, i, kv).start()

    def send_inner(i):
        @pl.when(inner)
        def _():
            for kv in range(2):
                inner_copy(i, kv).start()

    send_lists(partners[3:])
    send_wholes(0)
    send_lists(partners[:3])
    send_inner(0)
    for i in range(1, len(wholes)):
        send_wholes(i)
        send_inner(i)

    landings = [
        (MIRROR, inner | ((quarter == 0) & has_low) | ((quarter == 3) & has_high)),
        (RELAYED, ((x == 0) & has_low) | ((x == 1) & has_high)),
        (BELOW8, me >= 8),
        (ABOVE8, me + 8 < n),
    ]
    for j, d in enumerate(far):
        landings.append((NEAR + 2 * j, me >= d))
        landings.append((NEAR + 2 * j + 1, me + d < n))
    for slot, exists in landings:
        @pl.when(jnp.logical_not(exists))
        def _():
            landed[slot] = jnp.zeros(landed.shape[1:], landed.dtype)
    for side in range(2):
        @pl.when(jnp.logical_not((has_low, has_high)[side]))
        def _():
            whole[side] = jnp.zeros(whole.shape[1:], whole.dtype)

    for load in loads:
        load.wait()
    for _, exists, here, _ in partners:
        @pl.when(exists)
        def _():
            list_copy(core_peer, here, here).wait_recv()

    def stage_own(slot, columns, wanted):
        stage[slot, 0, :, columns] = k_v[wanted, :, columns]
        stage[slot, 1, :, columns] = v_v[wanted, :, columns]

    far_sends = []
    for j, d in enumerate(far):
        far_sends.append((OUT_NEAR + 2 * j, NEAR + 2 * j, me + d, me + d < n, 6 + 2 * j, 4 + j))
        far_sends.append((OUT_NEAR + 2 * j + 1, NEAR + 2 * j + 1, me - d, me >= d, 5 + 2 * j, levels + 4 + j))

    for i, piece in enumerate(wholes):
        for slot, side, exists, here, entry in end_sends:
            @pl.when(exists)
            def _():
                stage_own(slot, span(piece), lists_s[here, 0, entry])
                end_copy(slot, side, i).start()
        @pl.when(outer)
        def _():
            stage_own(ACROSS, span(piece), lists_s[1, 0, 1 + levels * x])
            across_copy(i).start()
        stage_own(CORE, span(piece), lists_s[0, 0, levels * core])
        tile_copy(CORE, CORE, wholes, i, core_peer).start()
    for slot, there, device, exists, here, entry in far_sends:
        @pl.when(exists)
        def _():
            for i, piece in enumerate(relayed):
                stage_own(slot, span(piece), lists_s[here, 0, entry])
                for part in parts_of(i):
                    part_copy(slot, there, i, part, device).start()

    factor = math.log2(math.e) / math.sqrt(HD)

    def bias_of(parts):
        return jnp.concatenate(
            [jnp.full((1, size), jnp.where(exists, 0.0, ABSENT), jnp.float32) for size, exists in parts], axis=1)

    near_bias = bias_of([((tiles + 2) * TILE, yes), (TILE, has_low), (TILE, has_high)])
    late_bias = bias_of([(TILE, exists) for _, exists in landings])

    relays = [
        (BELOW8, BELOW8, me + 4, has_low & has_high, 0, 4, 3),
        (ABOVE8, ABOVE8, me - 4, has_low & has_high, 1, 3, levels + 3),
        (RELAYED, RELAYED, across, (x == 0) & has_high & ((me >= 4) | low_corner), 1, 1, levels + 1),
        (RELAYED, RELAYED, across, (x == 1) & has_low & ((me + 4 < n) | high_corner), 0, 1, 1),
        (MIRROR, MIRROR, mirror, (quarter == 0) & has_high, 1, 2, levels),
        (MIRROR, MIRROR, mirror, (quarter == 3) & has_low, 0, 2, 0),
    ]
    end_relays = [
        (END_RELAYED, me - 4, to_low_end & high_corner, 3, levels + 1),
        (END_RELAYED, me + 4, to_high_end & low_corner, 4, 1),
    ]

    relays_to_end = (to_low_end & high_corner) | (to_high_end & low_corner)

    def chosen(block_of, wanted):
        block = block_of(0)
        for tile in range(1, tiles):
            block = jnp.where(wanted == tile, block_of(tile), block)
        return block

    low = jnp.where(low_chosen, 0, own_list[0, 2])
    high = jnp.where(high_chosen, 0, own_list[0, levels + 2])
    beside = jnp.where(outer, own_list[0, 1 + levels * (1 - x)], 0)

    def early(h, carry):
        columns = pl.ds(pl.multiple_of(h * HD, HD), HD)

        def gather(kv):
            own = (k_v, v_v)[kv]
            return jnp.concatenate(
                [own[tile, :, columns] for tile in range(tiles)] + [
                    landed[CORE, kv, :, columns],
                    chosen(lambda tile: inside[kv, tile, :, columns], beside),
                    chosen(lambda tile: whole[0, kv, tile, :, columns], low),
                    chosen(lambda tile: whole[1, kv, tile, :, columns], high)], axis=0)
        scores = lax.dot_general(
            q_v[:, columns], gather(0), (((1,), (1,)), ((), ())), preferred_element_type=jnp.float32)
        scores = scores + near_bias
        peak = jnp.max(scores, axis=1, keepdims=True)
        raised = jnp.exp2((scores - peak) * factor)
        added = jnp.sum(raised, axis=1, keepdims=True)
        acc[h] = jnp.dot(raised.astype(jnp.bfloat16), gather(1), preferred_element_type=jnp.float32)
        top[h] = jnp.broadcast_to(peak, (peak.shape[0], HD))
        total[h] = jnp.broadcast_to(added, (peak.shape[0], HD))
        return carry

    for w, (first, size) in enumerate(wholes):
        inside_piece = [r for r, piece in enumerate(relayed) if first <= piece[0] < first + size]
        for side in range(2):
            @pl.when(sides[side][1])
            def _():
                for kv in range(2):
                    whole_copy(side, w, kv).wait_recv()
            @pl.when(sides[side][2])
            def _():
                end_copy(TO_LOW_END, side, w).wait_recv()

        for slot, device, exists, here, entry in end_relays:
            @pl.when(exists)
            def _():
                for kv in range(2):
                    inner_copy(w, kv).wait_recv()
                wanted = lists_s[here, 0, entry]
                for r in inside_piece:
                    columns = span(relayed[r])
                    for kv in range(2):
                        stage[slot, kv, :, columns] = chosen(lambda tile: inside[kv, tile, :, columns], wanted)
                    for part in parts_of(r):
                        part_copy(slot, RELAYED, r, part, device).start()

        for r in inside_piece:
            columns = span(relayed[r])
            for slot, there, device, exists, side, here, entry in relays:
                @pl.when(exists)
                def _():
                    wanted = lists_s[here, 0, entry]
                    for kv in range(2):
                        stage[slot, kv, :, columns] = chosen(lambda tile: whole[side, kv, tile, :, columns], wanted)
            for part in parts_of(r):
                for slot, there, device, exists, _, _, _ in relays:
                    @pl.when(exists)
                    def _():
                        part_copy(slot, there, r, part, device).start()

        @pl.when(outer & ~relays_to_end)
        def _():
            for kv in range(2):
                inner_copy(w, kv).wait_recv()

        @pl.when(outer)
        def _():
            wanted = lists_s[0, 0, levels * (1 - core)]
            for r in inside_piece:
                columns = span(relayed[r])
                for kv in range(2):
                    stage[INNER, kv, :, columns] = chosen(lambda tile: inside[kv, tile, :, columns], wanted)
                for part in parts_of(r):
                    part_copy(INNER, MIRROR, r, part, core_peer).start()

        @pl.when(inner)
        def _():
            across_copy(w).wait_recv()

        tile_copy(CORE, CORE, wholes, w, core_peer).wait_recv()
        lax.fori_loop(first, first + size, early, 0)

    def landed_at(kv, columns):
        return jnp.concatenate([landed[slot, kv, :, columns] for slot, _ in landings], axis=0)

    def weigh(h, columns):
        scores = lax.dot_general(
            q_v[:, columns], landed_at(0, columns), (((1,), (1,)), ((), ())), preferred_element_type=jnp.float32)
        scores = scores + late_bias
        old = top[h][:, :1]
        peak = jnp.maximum(old, jnp.max(scores, axis=1, keepdims=True))
        raised = jnp.exp2((scores - peak) * factor)
        fade = jnp.exp2((old - peak) * factor)
        added = jnp.sum(raised, axis=1, keepdims=True) + fade * total[h][:, :1]
        return raised.astype(jnp.bfloat16), fade * acc[h], added

    def finish(columns, raised, faded, added):
        mixed = jnp.dot(raised, landed_at(1, columns), preferred_element_type=jnp.float32) + faded
        out_ref[:, columns] = (mixed / added).astype(out_ref.dtype)

    def late(h, carry):
        columns = pl.ds(pl.multiple_of(h * HD, HD), HD)
        finish(columns, *weigh(h, columns))
        return carry

    def sent(source, target, semaphore):
        pltpu.make_async_remote_copy(
            src_ref=source, dst_ref=target, send_sem=semaphore, recv_sem=semaphore,
            device_id={"frame": core_peer}, device_id_type=MESH).wait_send()

    def drain_early():
        for _, exists, here, _ in partners:
            @pl.when(exists)
            def _():
                list_copy(core_peer, here, here).wait_send()
        for kv in range(2):
            @pl.when(inner)
            def _():
                sent((k_hbm, v_hbm)[kv], inside.at[kv], i_send.at[kv])
            for side in range(2):
                @pl.when(sides[side][0])
                def _():
                    sent((k_hbm, v_hbm)[kv], whole.at[side, kv], w_send.at[side, kv])
        early_slots = [(CORE, yes), (ACROSS, outer)] + [(slot, exists) for slot, _, exists, _, _ in end_sends]
        for slot, exists in early_slots:
            @pl.when(exists)
            def _():
                sent(stage.at[slot], landed.at[CORE], t_send.at[slot])

    def drain():
        late_slots = [(INNER, outer)]
        late_slots += [(slot, exists) for slot, _, _, exists, _, _ in far_sends]
        late_slots += [(slot, exists) for slot, _, _, exists, _, _, _ in relays]
        late_slots += [(slot, exists) for slot, _, exists, _, _ in end_relays]
        for slot, exists in late_slots:
            @pl.when(exists)
            def _():
                sent(stage.at[slot], landed.at[CORE], t_send.at[slot])

    def wait_landed(r, part):
        for slot, exists in landings:
            @pl.when(exists)
            def _():
                part_copy(CORE, slot, r, part, core_peer).wait_recv()

    last = len(relayed) - 1
    for r in range(last):
        first, size = relayed[r]
        wait_landed(r, None)
        lax.fori_loop(first, first + size, late, 0)
        if r == 0:
            drain_early()
    first, size = relayed[last]
    wait_landed(last, 0)
    weighed = [weigh(h, span((h, 1))) for h in range(first, first + size)]
    wait_landed(last, 1)
    for h, ready in zip(range(first, first + size), weighed):
        finish(span((h, 1)), *ready)
    drain()


def write_out(in_ref, out_ref, sem):
    copy = pltpu.make_async_copy(in_ref, out_ref, sem)
    copy.start()
    copy.wait()


def solution(mesh):
    n = mesh.shape["frame"]

    def body(queries, key_heads, value_heads, tile_lists):
        rows, channels = queries.shape
        heads = channels // HD
        tiles = rows // TILE
        levels = tile_lists.shape[1] // 2
        far = max(levels - 4, 0)
        lists = 5 + 2 * far
        bf16, f32 = jnp.bfloat16, jnp.float32
        hbm = pl.BlockSpec(memory_space=pltpu.HBM)
        dma = pltpu.SemaphoreType.DMA
        out_slots, in_slots = OUT_NEAR + 2 * far, NEAR + 2 * far
        result = pl.pallas_call(
            functools.partial(kernel, n, levels, heads),
            out_shape=pltpu.VMEM((rows, channels), bf16),
            in_specs=[hbm, hbm, hbm, pl.BlockSpec(memory_space=pltpu.SMEM)],
            out_specs=pl.BlockSpec(memory_space=pltpu.VMEM),
            scratch_shapes=[
                pltpu.VMEM((rows, channels), bf16),
                pltpu.VMEM((tiles, TILE, channels), bf16),
                pltpu.VMEM((tiles, TILE, channels), bf16),
                pltpu.VMEM((2, 2, tiles, TILE, channels), bf16),
                pltpu.VMEM((2, tiles, TILE, channels), bf16),
                pltpu.VMEM((out_slots, 2, TILE, channels), bf16),
                pltpu.VMEM((in_slots, 2, TILE, channels), bf16),
                pltpu.SMEM((lists, 1, 2 * levels), jnp.int32),
                pltpu.VMEM((heads, rows, HD), f32),
                pltpu.VMEM((heads, rows, HD), f32),
                pltpu.VMEM((heads, rows, HD), f32),
                dma((2, 2)),
                dma((2, len(WHOLE_PIECES), 2)),
                dma((2,)),
                dma((len(WHOLE_PIECES), 2)),
                dma((out_slots,)),
                dma((in_slots, len(RELAY_PIECES) + 1)),
                dma((lists,)),
                dma((lists,)),
                dma((3,)),
            ],
            compiler_params=pltpu.CompilerParams(
                collective_id=0, has_side_effects=True, vmem_limit_bytes=61 << 20
            ),
        )(
            queries,
            key_heads.reshape(tiles, TILE, channels),
            value_heads.reshape(tiles, TILE, channels),
            tile_lists,
        )
        return pl.pallas_call(
            write_out,
            out_shape=jax.ShapeDtypeStruct((rows, channels), bf16),
            in_specs=[pl.BlockSpec(memory_space=pltpu.VMEM)],
            out_specs=pl.BlockSpec(memory_space=pl.ANY),
            scratch_shapes=[dma],
            compiler_params=pltpu.CompilerParams(vmem_limit_bytes=4 << 20),
        )(result)

    in_specs = (
        P(("groups", "frame"), None),
        P(("groups", "frame"), None),
        P(("groups", "frame"), None),
        P("frame", None),
    )
    return jax.shard_map(
        body, mesh=mesh, in_specs=in_specs, out_specs=P(("groups", "frame"), None), check_vma=False
    )
```

```python
import functools
import math

import jax
import jax.numpy as jnp
from jax import lax
from jax.experimental import pallas as pl
from jax.experimental.pallas import tpu as pltpu
from jax.sharding import PartitionSpec as P

HD = 128
TILE = 128
MESH = pl.DeviceIdType.MESH
ABSENT = -1e30

WHOLE_PIECES = (4, 4, 4)
RELAY_PIECES = (4, 4, 2, 2)

CORE, MIRROR, RELAYED, BELOW8, ABOVE8 = range(5)
NEAR = 5
ACROSS, INNER, TO_LOW_END, TO_HIGH_END, END_RELAYED = range(NEAR, NEAR + 5)
OUT_NEAR = NEAR + 5


def pieces_of(sizes, heads):
    unit = heads // sum(sizes)
    pieces, first = [], 0
    for size in sizes:
        pieces.append((first, size * unit))
        first += size * unit
    return pieces


def kernel(n, levels, heads, q_hbm, k_hbm, v_hbm, own_list, out_ref,
           q_v, k_v, v_v, whole, inside, stage, landed, lists_s, top, total, acc,
           w_send, w_recv, i_send, i_recv, t_send, t_recv, l_send, l_recv, in_sem):
    me = lax.axis_index("frame")
    quarter = me % 4
    x = quarter // 2
    core = me % 2
    core_peer = me + 1 - 2 * core
    across = me + 2 - 4 * x
    mirror = me + 3 - 2 * quarter
    inner = (quarter == 1) | (quarter == 2)
    outer = (quarter == 0) | (quarter == 3)
    has_low, has_high = me >= 4, me + 4 < n
    low_corner, high_corner = quarter == 0, quarter == 3
    to_low_end, to_high_end = has_low & (me < 8), has_high & (me + 8 >= n)
    chosen_down, chosen_up = to_low_end & ~low_corner, to_high_end & ~high_corner
    low_chosen, high_chosen = (me + 4 >= n) & ~high_corner, (me < 4) & ~low_corner
    tiles = k_v.shape[0]
    far = [1 << level for level in range(4, levels)]
    yes = me >= 0
    wholes = pieces_of(WHOLE_PIECES, heads)
    relayed = pieces_of(RELAY_PIECES, heads)

    partners = [
        (core_peer, yes, 0, 0),
        (across, yes, 1, 1),
        (mirror, yes, 2, 2),
        (me - 4, has_low, 3, 4),
        (me + 4, has_high, 4, 3),
    ]
    for j, d in enumerate(far):
        partners.append((me - d, me >= d, 5 + 2 * j, 6 + 2 * j))
        partners.append((me + d, me + d < n, 6 + 2 * j, 5 + 2 * j))

    barrier = pltpu.get_barrier_semaphore()
    for device, exists, _, _ in partners:
        @pl.when(exists)
        def _():
            pl.semaphore_signal(barrier, inc=1, device_id={"frame": device}, device_id_type=MESH)
    loads = [
        pltpu.make_async_copy(source, target, in_sem.at[i])
        for i, (source, target) in enumerate(((k_hbm, k_v), (v_hbm, v_v), (q_hbm, q_v)))
    ]
    for load in loads:
        load.start()
    pl.semaphore_wait(barrier, sum(jnp.where(exists, 1, 0) for _, exists, _, _ in partners))

    def span(piece):
        return pl.ds(piece[0] * HD, piece[1] * HD)

    def whole_copy(side, i, kv):
        columns = span(wholes[i])
        return pltpu.make_async_remote_copy(
            src_ref=(k_hbm, v_hbm)[kv].at[:, :, columns], dst_ref=whole.at[side, kv, :, :, columns],
            send_sem=w_send.at[side, kv], recv_sem=w_recv.at[side, i],
            device_id={"frame": me + 4 if side == 0 else me - 4}, device_id_type=MESH)

    def inner_copy(i, kv):
        columns = span(wholes[i])
        return pltpu.make_async_remote_copy(
            src_ref=(k_hbm, v_hbm)[kv].at[:, :, columns], dst_ref=inside.at[kv, :, :, columns],
            send_sem=i_send.at[kv], recv_sem=i_recv.at[i],
            device_id={"frame": across}, device_id_type=MESH)

    def across_copy(i):
        columns = span(wholes[i])
        return pltpu.make_async_remote_copy(
            src_ref=stage.at[ACROSS, :, :, columns], dst_ref=inside.at[:, 0, :, columns],
            send_sem=t_send.at[ACROSS], recv_sem=i_recv.at[i],
            device_id={"frame": across}, device_id_type=MESH)

    def end_copy(slot, side, i):
        columns = span(wholes[i])
        return pltpu.make_async_remote_copy(
            src_ref=stage.at[slot, :, :, columns], dst_ref=whole.at[side, :, 0, :, columns],
            send_sem=t_send.at[slot], recv_sem=w_recv.at[side, i],
            device_id={"frame": me + 4 if side == 0 else me - 4}, device_id_type=MESH)

    def list_copy(device, here, there):
        return pltpu.make_async_remote_copy(
            src_ref=own_list, dst_ref=lists_s.at[there],
            send_sem=l_send.at[here], recv_sem=l_recv.at[there],
            device_id={"frame": device}, device_id_type=MESH)

    def tile_copy(slot, there, pieces, i, device):
        columns = span(pieces[i])
        return pltpu.make_async_remote_copy(
            src_ref=stage.at[slot, :, :, columns], dst_ref=landed.at[there, :, :, columns],
            send_sem=t_send.at[slot], recv_sem=t_recv.at[there, i],
            device_id={"frame": device}, device_id_type=MESH)

    def parts_of(r):
        return (0, 1) if r == len(relayed) - 1 else (None,)

    def part_copy(slot, there, r, part, device):
        columns = span(relayed[r])
        at = slice(None) if part is None else part
        i = r + (part or 0)
        return pltpu.make_async_remote_copy(
            src_ref=stage.at[slot, at, :, columns], dst_ref=landed.at[there, at, :, columns],
            send_sem=t_send.at[slot], recv_sem=t_recv.at[there, i],
            device_id={"frame": device}, device_id_type=MESH)

    sides = (
        (has_high & ~chosen_up, has_low & ~low_chosen, has_low & low_chosen),
        (has_low & ~chosen_down, has_high & ~high_chosen, has_high & high_chosen),
    )
    end_sends = [(TO_HIGH_END, 0, chosen_up, 4, 2), (TO_LOW_END, 1, chosen_down, 3, levels + 2)]

    def send_lists(chosen_partners):
        for device, exists, here, there in chosen_partners:
            @pl.when(exists)
            def _():
                list_copy(device, here, there).start()

    def send_wholes(i):
        for side in range(2):
            @pl.when(sides[side][0])
            def _():
                for kv in range(2):
                    whole_copy(side, i, kv).start()

    def send_inner(i):
        @pl.when(inner)
        def _():
            for kv in range(2):
                inner_copy(i, kv).start()

    send_lists(partners[1:3])
    send_inner(0)
    send_lists(partners[3:])
    send_wholes(0)
    send_lists(partners[:1])
    for i in range(1, len(wholes)):
        send_inner(i)
        send_wholes(i)

    landings = [
        (MIRROR, inner | ((quarter == 0) & has_low) | ((quarter == 3) & has_high)),
        (RELAYED, ((x == 0) & has_low) | ((x == 1) & has_high)),
        (BELOW8, me >= 8),
        (ABOVE8, me + 8 < n),
    ]
    for j, d in enumerate(far):
        landings.append((NEAR + 2 * j, me >= d))
        landings.append((NEAR + 2 * j + 1, me + d < n))
    for slot, exists in landings:
        @pl.when(jnp.logical_not(exists))
        def _():
            landed[slot] = jnp.zeros(landed.shape[1:], landed.dtype)
    for side in range(2):
        @pl.when(jnp.logical_not((has_low, has_high)[side]))
        def _():
            whole[side] = jnp.zeros(whole.shape[1:], whole.dtype)

    for load in loads:
        load.wait()
    for _, exists, here, _ in partners:
        @pl.when(exists)
        def _():
            list_copy(core_peer, here, here).wait_recv()

    def stage_own(slot, columns, wanted):
        stage[slot, 0, :, columns] = k_v[wanted, :, columns]
        stage[slot, 1, :, columns] = v_v[wanted, :, columns]

    far_sends = []
    for j, d in enumerate(far):
        far_sends.append((OUT_NEAR + 2 * j, NEAR + 2 * j, me + d, me + d < n, 6 + 2 * j, 4 + j))
        far_sends.append((OUT_NEAR + 2 * j + 1, NEAR + 2 * j + 1, me - d, me >= d, 5 + 2 * j, levels + 4 + j))

    for i, piece in enumerate(wholes):
        for slot, side, exists, here, entry in end_sends:
            @pl.when(exists)
            def _():
                stage_own(slot, span(piece), lists_s[here, 0, entry])
                end_copy(slot, side, i).start()
        @pl.when(outer)
        def _():
            stage_own(ACROSS, span(piece), lists_s[1, 0, 1 + levels * x])
            across_copy(i).start()
        stage_own(CORE, span(piece), lists_s[0, 0, levels * core])
        tile_copy(CORE, CORE, wholes, i, core_peer).start()
    for slot, there, device, exists, here, entry in far_sends:
        @pl.when(exists)
        def _():
            for i, piece in enumerate(relayed):
                stage_own(slot, span(piece), lists_s[here, 0, entry])
                for part in parts_of(i):
                    part_copy(slot, there, i, part, device).start()

    factor = math.log2(math.e) / math.sqrt(HD)

    def bias_of(parts):
        return jnp.concatenate(
            [jnp.full((1, size), jnp.where(exists, 0.0, ABSENT), jnp.float32) for size, exists in parts], axis=1)

    near_bias = bias_of([((tiles + 2) * TILE, yes), (TILE, has_low), (TILE, has_high)])
    late_bias = bias_of([(TILE, exists) for _, exists in landings])

    relays = [
        (MIRROR, MIRROR, mirror, (quarter == 0) & has_high, 1, 2, levels),
        (MIRROR, MIRROR, mirror, (quarter == 3) & has_low, 0, 2, 0),
        (RELAYED, RELAYED, across, (x == 0) & has_high & ((me >= 4) | low_corner), 1, 1, levels + 1),
        (RELAYED, RELAYED, across, (x == 1) & has_low & ((me + 4 < n) | high_corner), 0, 1, 1),
        (BELOW8, BELOW8, me + 4, has_low & has_high, 0, 4, 3),
        (ABOVE8, ABOVE8, me - 4, has_low & has_high, 1, 3, levels + 3),
    ]
    end_relays = [
        (END_RELAYED, me - 4, to_low_end & high_corner, 3, levels + 1),
        (END_RELAYED, me + 4, to_high_end & low_corner, 4, 1),
    ]

    relays_to_end = (to_low_end & high_corner) | (to_high_end & low_corner)

    def chosen(block_of, wanted):
        block = block_of(0)
        for tile in range(1, tiles):
            block = jnp.where(wanted == tile, block_of(tile), block)
        return block

    low = jnp.where(low_chosen, 0, own_list[0, 2])
    high = jnp.where(high_chosen, 0, own_list[0, levels + 2])
    beside = jnp.where(outer, own_list[0, 1 + levels * (1 - x)], 0)

    def early(h, carry):
        columns = pl.ds(pl.multiple_of(h * HD, HD), HD)

        def gather(kv):
            own = (k_v, v_v)[kv]
            return jnp.concatenate(
                [own[tile, :, columns] for tile in range(tiles)] + [
                    landed[CORE, kv, :, columns],
                    chosen(lambda tile: inside[kv, tile, :, columns], beside),
                    chosen(lambda tile: whole[0, kv, tile, :, columns], low),
                    chosen(lambda tile: whole[1, kv, tile, :, columns], high)], axis=0)
        scores = lax.dot_general(
            q_v[:, columns], gather(0), (((1,), (1,)), ((), ())), preferred_element_type=jnp.float32)
        scores = scores + near_bias
        peak = jnp.max(scores, axis=1, keepdims=True)
        raised = jnp.exp2((scores - peak) * factor)
        added = jnp.sum(raised, axis=1, keepdims=True)
        acc[h] = jnp.dot(raised.astype(jnp.bfloat16), gather(1), preferred_element_type=jnp.float32)
        top[h] = jnp.broadcast_to(peak, (peak.shape[0], HD))
        total[h] = jnp.broadcast_to(added, (peak.shape[0], HD))
        return carry

    def arrived(target, semaphore):
        pltpu.make_async_remote_copy(
            src_ref=target, dst_ref=target, send_sem=semaphore, recv_sem=semaphore,
            device_id={"frame": core_peer}, device_id_type=MESH).wait_recv()

    for w, (first, size) in enumerate(wholes):
        inside_piece = [r for r, piece in enumerate(relayed) if first <= piece[0] < first + size]
        for side in range(2):
            @pl.when(sides[side][1])
            def _():
                arrived(whole.at[side, :, :, :, span(wholes[w])], w_recv.at[side, w])
            @pl.when(sides[side][2])
            def _():
                end_copy(TO_LOW_END, side, w).wait_recv()

        for slot, device, exists, here, entry in end_relays:
            @pl.when(exists)
            def _():
                arrived(inside.at[:, :, :, span(wholes[w])], i_recv.at[w])
                wanted = lists_s[here, 0, entry]
                for r in inside_piece:
                    columns = span(relayed[r])
                    for kv in range(2):
                        stage[slot, kv, :, columns] = chosen(lambda tile: inside[kv, tile, :, columns], wanted)
                    for part in parts_of(r):
                        part_copy(slot, RELAYED, r, part, device).start()

        for r in inside_piece:
            columns = span(relayed[r])
            for slot, there, device, exists, side, here, entry in relays:
                @pl.when(exists)
                def _():
                    wanted = lists_s[here, 0, entry]
                    for kv in range(2):
                        stage[slot, kv, :, columns] = chosen(lambda tile: whole[side, kv, tile, :, columns], wanted)
            for part in parts_of(r):
                for slot, there, device, exists, _, _, _ in relays:
                    @pl.when(exists)
                    def _():
                        part_copy(slot, there, r, part, device).start()

        @pl.when(outer & ~relays_to_end)
        def _():
            arrived(inside.at[:, :, :, span(wholes[w])], i_recv.at[w])

        @pl.when(outer)
        def _():
            wanted = lists_s[0, 0, levels * (1 - core)]
            for r in inside_piece:
                columns = span(relayed[r])
                for kv in range(2):
                    stage[INNER, kv, :, columns] = chosen(lambda tile: inside[kv, tile, :, columns], wanted)
                for part in parts_of(r):
                    part_copy(INNER, MIRROR, r, part, core_peer).start()

        @pl.when(inner)
        def _():
            across_copy(w).wait_recv()

        tile_copy(CORE, CORE, wholes, w, core_peer).wait_recv()
        lax.fori_loop(first, first + size, early, 0)

    def landed_at(kv, columns):
        return jnp.concatenate([landed[slot, kv, :, columns] for slot, _ in landings], axis=0)

    def weigh(h, columns):
        scores = lax.dot_general(
            q_v[:, columns], landed_at(0, columns), (((1,), (1,)), ((), ())), preferred_element_type=jnp.float32)
        scores = scores + late_bias
        old = top[h][:, :1]
        peak = jnp.maximum(old, jnp.max(scores, axis=1, keepdims=True))
        raised = jnp.exp2((scores - peak) * factor)
        fade = jnp.exp2((old - peak) * factor)
        added = jnp.sum(raised, axis=1, keepdims=True) + fade * total[h][:, :1]
        return raised.astype(jnp.bfloat16), fade * acc[h], added

    def finish(columns, raised, faded, added):
        mixed = jnp.dot(raised, landed_at(1, columns), preferred_element_type=jnp.float32) + faded
        out_ref[:, columns] = (mixed / added).astype(out_ref.dtype)

    def late(h, carry):
        columns = pl.ds(pl.multiple_of(h * HD, HD), HD)
        finish(columns, *weigh(h, columns))
        return carry

    def sent(source, target, semaphore):
        pltpu.make_async_remote_copy(
            src_ref=source, dst_ref=target, send_sem=semaphore, recv_sem=semaphore,
            device_id={"frame": core_peer}, device_id_type=MESH).wait_send()

    def drain_early():
        for _, exists, here, _ in partners:
            @pl.when(exists)
            def _():
                list_copy(core_peer, here, here).wait_send()
        for kv in range(2):
            @pl.when(inner)
            def _():
                sent((k_hbm, v_hbm)[kv], inside.at[kv], i_send.at[kv])
            for side in range(2):
                @pl.when(sides[side][0])
                def _():
                    sent((k_hbm, v_hbm)[kv], whole.at[side, kv], w_send.at[side, kv])
        early_slots = [(CORE, yes), (ACROSS, outer)] + [(slot, exists) for slot, _, exists, _, _ in end_sends]
        for slot, exists in early_slots:
            @pl.when(exists)
            def _():
                sent(stage.at[slot], landed.at[CORE], t_send.at[slot])

    def drain():
        late_slots = [(INNER, outer)]
        late_slots += [(slot, exists) for slot, _, _, exists, _, _ in far_sends]
        late_slots += [(slot, exists) for slot, _, _, exists, _, _, _ in relays]
        late_slots += [(slot, exists) for slot, _, exists, _, _ in end_relays]
        for slot, exists in late_slots:
            @pl.when(exists)
            def _():
                sent(stage.at[slot], landed.at[CORE], t_send.at[slot])

    def wait_landed(r, part):
        for slot, exists in landings:
            @pl.when(exists)
            def _():
                part_copy(CORE, slot, r, part, core_peer).wait_recv()

    last = len(relayed) - 1
    for r in range(last):
        first, size = relayed[r]
        wait_landed(r, None)
        lax.fori_loop(first, first + size, late, 0)
        if r == 0:
            drain_early()
    first, size = relayed[last]
    wait_landed(last, 0)
    weighed = [weigh(h, span((h, 1))) for h in range(first, first + size)]
    drain()
    wait_landed(last, 1)
    for h, ready in zip(range(first, first + size), weighed):
        finish(span((h, 1)), *ready)


def write_out(in_ref, out_ref, sem):
    copy = pltpu.make_async_copy(in_ref, out_ref, sem)
    copy.start()
    copy.wait()


def solution(mesh):
    n = mesh.shape["frame"]

    def body(queries, key_heads, value_heads, tile_lists):
        rows, channels = queries.shape
        heads = channels // HD
        tiles = rows // TILE
        levels = tile_lists.shape[1] // 2
        far = max(levels - 4, 0)
        lists = 5 + 2 * far
        bf16, f32 = jnp.bfloat16, jnp.float32
        hbm = pl.BlockSpec(memory_space=pltpu.HBM)
        dma = pltpu.SemaphoreType.DMA
        out_slots, in_slots = OUT_NEAR + 2 * far, NEAR + 2 * far
        result = pl.pallas_call(
            functools.partial(kernel, n, levels, heads),
            out_shape=pltpu.VMEM((rows, channels), bf16),
            in_specs=[hbm, hbm, hbm, pl.BlockSpec(memory_space=pltpu.SMEM)],
            out_specs=pl.BlockSpec(memory_space=pltpu.VMEM),
            scratch_shapes=[
                pltpu.VMEM((rows, channels), bf16),
                pltpu.VMEM((tiles, TILE, channels), bf16),
                pltpu.VMEM((tiles, TILE, channels), bf16),
                pltpu.VMEM((2, 2, tiles, TILE, channels), bf16),
                pltpu.VMEM((2, tiles, TILE, channels), bf16),
                pltpu.VMEM((out_slots, 2, TILE, channels), bf16),
                pltpu.VMEM((in_slots, 2, TILE, channels), bf16),
                pltpu.SMEM((lists, 1, 2 * levels), jnp.int32),
                pltpu.VMEM((heads, rows, HD), f32),
                pltpu.VMEM((heads, rows, HD), f32),
                pltpu.VMEM((heads, rows, HD), f32),
                dma((2, 2)),
                dma((2, len(WHOLE_PIECES))),
                dma((2,)),
                dma((len(WHOLE_PIECES),)),
                dma((out_slots,)),
                dma((in_slots, len(RELAY_PIECES) + 1)),
                dma((lists,)),
                dma((lists,)),
                dma((3,)),
            ],
            compiler_params=pltpu.CompilerParams(
                collective_id=0, has_side_effects=True, vmem_limit_bytes=61 << 20
            ),
        )(
            queries,
            key_heads.reshape(tiles, TILE, channels),
            value_heads.reshape(tiles, TILE, channels),
            tile_lists,
        )
        return pl.pallas_call(
            write_out,
            out_shape=jax.ShapeDtypeStruct((rows, channels), bf16),
            in_specs=[pl.BlockSpec(memory_space=pltpu.VMEM)],
            out_specs=pl.BlockSpec(memory_space=pl.ANY),
            scratch_shapes=[dma],
            compiler_params=pltpu.CompilerParams(vmem_limit_bytes=4 << 20),
        )(result)

    in_specs = (
        P(("groups", "frame"), None),
        P(("groups", "frame"), None),
        P(("groups", "frame"), None),
        P("frame", None),
    )
    return jax.shard_map(
        body, mesh=mesh, in_specs=in_specs, out_specs=P(("groups", "frame"), None), check_vma=False
    )
```

```python
import functools
import math

import jax
import jax.numpy as jnp
from jax import lax
from jax.experimental import pallas as pl
from jax.experimental.pallas import tpu as pltpu
from jax.sharding import PartitionSpec as P

HD = 128
TILE = 128
MESH = pl.DeviceIdType.MESH
ABSENT = -1e30

WHOLE_PIECES = (4, 4, 4)
RELAY_PIECES = (4, 4, 2, 2)

CORE, MIRROR, RELAYED, BELOW8, ABOVE8 = range(5)
NEAR = 5
ACROSS, INNER, TO_LOW_END, TO_HIGH_END, END_DOWN, END_UP = range(NEAR, NEAR + 6)
OUT_NEAR = NEAR + 6


def pieces_of(sizes, heads):
    unit = heads // sum(sizes)
    pieces, first = [], 0
    for size in sizes:
        pieces.append((first, size * unit))
        first += size * unit
    return pieces


def kernel(n, levels, heads, q_hbm, k_hbm, v_hbm, own_list, out_ref,
           q_v, k_v, v_v, whole, inside, stage, landed, lists_s, top, total, acc,
           w_send, w_recv, i_send, i_recv, t_send, t_recv, l_send, l_recv, in_sem):
    me = lax.axis_index("frame")
    quarter = me % 4
    x = quarter // 2
    core = me % 2
    core_peer = me + 1 - 2 * core
    across = me + 2 - 4 * x
    mirror = me + 3 - 2 * quarter
    inner = (quarter == 1) | (quarter == 2)
    outer = (quarter == 0) | (quarter == 3)
    has_low, has_high = me >= 4, me + 4 < n
    low_corner, high_corner = quarter == 0, quarter == 3
    to_low_end, to_high_end = has_low & (me < 8), has_high & (me + 8 >= n)
    chosen_down, chosen_up = to_low_end & ~low_corner, to_high_end & ~high_corner
    low_chosen, high_chosen = (me + 4 >= n) & ~high_corner, (me < 4) & ~low_corner
    tiles = k_v.shape[0]
    far = [1 << level for level in range(4, levels)]
    yes = me >= 0
    wholes = pieces_of(WHOLE_PIECES, heads)
    relayed = pieces_of(RELAY_PIECES, heads)

    partners = [
        (core_peer, yes, 0, 0),
        (across, yes, 1, 1),
        (mirror, yes, 2, 2),
        (me - 4, has_low, 3, 4),
        (me + 4, has_high, 4, 3),
    ]
    for j, d in enumerate(far):
        partners.append((me - d, me >= d, 5 + 2 * j, 6 + 2 * j))
        partners.append((me + d, me + d < n, 6 + 2 * j, 5 + 2 * j))

    barrier = pltpu.get_barrier_semaphore()
    for device, exists, _, _ in partners:
        @pl.when(exists)
        def _():
            pl.semaphore_signal(barrier, inc=1, device_id={"frame": device}, device_id_type=MESH)
    loads = [
        pltpu.make_async_copy(source, target, in_sem.at[i])
        for i, (source, target) in enumerate(((k_hbm, k_v), (v_hbm, v_v), (q_hbm, q_v)))
    ]
    for load in loads:
        load.start()
    pl.semaphore_wait(barrier, sum(jnp.where(exists, 1, 0) for _, exists, _, _ in partners))

    def span(piece):
        return pl.ds(piece[0] * HD, piece[1] * HD)

    def whole_copy(side, i, kv):
        columns = span(wholes[i])
        return pltpu.make_async_remote_copy(
            src_ref=(k_hbm, v_hbm)[kv].at[:, :, columns], dst_ref=whole.at[side, kv, :, :, columns],
            send_sem=w_send.at[side, kv], recv_sem=w_recv.at[side, i],
            device_id={"frame": me + 4 if side == 0 else me - 4}, device_id_type=MESH)

    def inner_copy(i, kv):
        columns = span(wholes[i])
        return pltpu.make_async_remote_copy(
            src_ref=(k_hbm, v_hbm)[kv].at[:, :, columns], dst_ref=inside.at[kv, :, :, columns],
            send_sem=i_send.at[kv], recv_sem=i_recv.at[i],
            device_id={"frame": across}, device_id_type=MESH)

    def across_copy(i):
        columns = span(wholes[i])
        return pltpu.make_async_remote_copy(
            src_ref=stage.at[ACROSS, :, :, columns], dst_ref=inside.at[:, 0, :, columns],
            send_sem=t_send.at[ACROSS], recv_sem=i_recv.at[i],
            device_id={"frame": across}, device_id_type=MESH)

    def end_copy(slot, side, i):
        columns = span(wholes[i])
        return pltpu.make_async_remote_copy(
            src_ref=stage.at[slot, :, :, columns], dst_ref=whole.at[side, :, 0, :, columns],
            send_sem=t_send.at[slot], recv_sem=w_recv.at[side, i],
            device_id={"frame": me + 4 if side == 0 else me - 4}, device_id_type=MESH)

    def list_copy(device, here, there):
        return pltpu.make_async_remote_copy(
            src_ref=own_list, dst_ref=lists_s.at[there],
            send_sem=l_send.at[here], recv_sem=l_recv.at[there],
            device_id={"frame": device}, device_id_type=MESH)

    def tile_copy(slot, there, pieces, i, device):
        columns = span(pieces[i])
        return pltpu.make_async_remote_copy(
            src_ref=stage.at[slot, :, :, columns], dst_ref=landed.at[there, :, :, columns],
            send_sem=t_send.at[slot], recv_sem=t_recv.at[there, i],
            device_id={"frame": device}, device_id_type=MESH)

    def parts_of(r):
        return (0, 1) if r == len(relayed) - 1 else (None,)

    def part_copy(slot, there, r, part, device):
        columns = span(relayed[r])
        at = slice(None) if part is None else part
        i = r + (part or 0)
        return pltpu.make_async_remote_copy(
            src_ref=stage.at[slot, at, :, columns], dst_ref=landed.at[there, at, :, columns],
            send_sem=t_send.at[slot], recv_sem=t_recv.at[there, i],
            device_id={"frame": device}, device_id_type=MESH)

    sides = (
        (has_high & ~chosen_up, has_low & ~low_chosen, has_low & low_chosen),
        (has_low & ~chosen_down, has_high & ~high_chosen, has_high & high_chosen),
    )
    end_sends = [(TO_HIGH_END, 0, chosen_up, 4, 2), (TO_LOW_END, 1, chosen_down, 3, levels + 2)]

    def send_lists(chosen_partners):
        for device, exists, here, there in chosen_partners:
            @pl.when(exists)
            def _():
                list_copy(device, here, there).start()

    def send_wholes(i):
        for side in range(2):
            @pl.when(sides[side][0])
            def _():
                for kv in range(2):
                    whole_copy(side, i, kv).start()

    def send_inner(i):
        @pl.when(inner)
        def _():
            for kv in range(2):
                inner_copy(i, kv).start()

    send_lists(partners[1:3])
    send_inner(0)
    send_lists(partners[3:])
    send_wholes(0)
    send_lists(partners[:1])
    for i in range(1, len(wholes)):
        send_inner(i)
        send_wholes(i)

    landings = [
        (MIRROR, inner | ((quarter == 0) & has_low) | ((quarter == 3) & has_high)),
        (RELAYED, ((x == 0) & has_low) | ((x == 1) & has_high)),
        (BELOW8, me >= 8),
        (ABOVE8, me + 8 < n),
    ]
    for j, d in enumerate(far):
        landings.append((NEAR + 2 * j, me >= d))
        landings.append((NEAR + 2 * j + 1, me + d < n))
    for slot, exists in landings:
        @pl.when(jnp.logical_not(exists))
        def _():
            landed[slot] = jnp.zeros(landed.shape[1:], landed.dtype)
    for side in range(2):
        @pl.when(jnp.logical_not((has_low, has_high)[side]))
        def _():
            whole[side] = jnp.zeros(whole.shape[1:], whole.dtype)

    for load in loads:
        load.wait()
    for _, exists, here, _ in partners:
        @pl.when(exists)
        def _():
            list_copy(core_peer, here, here).wait_recv()

    def stage_own(slot, columns, wanted):
        stage[slot, 0, :, columns] = k_v[wanted, :, columns]
        stage[slot, 1, :, columns] = v_v[wanted, :, columns]

    far_sends = []
    for j, d in enumerate(far):
        far_sends.append((OUT_NEAR + 2 * j, NEAR + 2 * j, me + d, me + d < n, 6 + 2 * j, 4 + j))
        far_sends.append((OUT_NEAR + 2 * j + 1, NEAR + 2 * j + 1, me - d, me >= d, 5 + 2 * j, levels + 4 + j))

    for i, piece in enumerate(wholes):
        for slot, side, exists, here, entry in end_sends:
            @pl.when(exists)
            def _():
                stage_own(slot, span(piece), lists_s[here, 0, entry])
                end_copy(slot, side, i).start()
        @pl.when(outer)
        def _():
            stage_own(ACROSS, span(piece), lists_s[1, 0, 1 + levels * x])
            across_copy(i).start()
        stage_own(CORE, span(piece), lists_s[0, 0, levels * core])
        tile_copy(CORE, CORE, wholes, i, core_peer).start()
    for slot, there, device, exists, here, entry in far_sends:
        @pl.when(exists)
        def _():
            for i, piece in enumerate(relayed):
                stage_own(slot, span(piece), lists_s[here, 0, entry])
                for part in parts_of(i):
                    part_copy(slot, there, i, part, device).start()

    factor = math.log2(math.e) / math.sqrt(HD)

    def bias_of(parts):
        return jnp.concatenate(
            [jnp.full((1, size), jnp.where(exists, 0.0, ABSENT), jnp.float32) for size, exists in parts], axis=1)

    near_bias = bias_of([((tiles + 2) * TILE, yes), (TILE, has_low), (TILE, has_high)])
    late_bias = bias_of([(TILE, exists) for _, exists in landings])

    relays = [
        (MIRROR, MIRROR, mirror, (quarter == 0) & has_high, 1, 2, levels),
        (MIRROR, MIRROR, mirror, (quarter == 3) & has_low, 0, 2, 0),
        (RELAYED, RELAYED, across, (x == 0) & has_high & (low_corner | ((me >= 4) & (me + 8 < n))), 1, 1, levels + 1),
        (RELAYED, RELAYED, across, (x == 1) & has_low & (high_corner | ((me + 4 < n) & (me >= 8))), 0, 1, 1),
        (BELOW8, BELOW8, me + 4, has_low & has_high, 0, 4, 3),
        (ABOVE8, ABOVE8, me - 4, has_low & has_high, 1, 3, levels + 3),
    ]
    relay_down = has_low & high_corner & (to_low_end | (me + 4 >= n))
    relay_up = has_high & low_corner & (to_high_end | (me < 4))
    end_relays = [
        (END_DOWN, me - 4, relay_down, 3, levels + 1),
        (END_UP, me + 4, relay_up, 4, 1),
    ]
    relays_to_end = relay_down | relay_up

    def chosen(block_of, wanted):
        block = block_of(0)
        for tile in range(1, tiles):
            block = jnp.where(wanted == tile, block_of(tile), block)
        return block

    low = jnp.where(low_chosen, 0, own_list[0, 2])
    high = jnp.where(high_chosen, 0, own_list[0, levels + 2])
    beside = jnp.where(outer, own_list[0, 1 + levels * (1 - x)], 0)

    def early(h, carry):
        columns = pl.ds(pl.multiple_of(h * HD, HD), HD)

        def gather(kv):
            own = (k_v, v_v)[kv]
            return jnp.concatenate(
                [own[tile, :, columns] for tile in range(tiles)] + [
                    landed[CORE, kv, :, columns],
                    chosen(lambda tile: inside[kv, tile, :, columns], beside),
                    chosen(lambda tile: whole[0, kv, tile, :, columns], low),
                    chosen(lambda tile: whole[1, kv, tile, :, columns], high)], axis=0)
        scores = lax.dot_general(
            q_v[:, columns], gather(0), (((1,), (1,)), ((), ())), preferred_element_type=jnp.float32)
        scores = scores + near_bias
        peak = jnp.max(scores, axis=1, keepdims=True)
        raised = jnp.exp2((scores - peak) * factor)
        added = jnp.sum(raised, axis=1, keepdims=True)
        acc[h] = jnp.dot(raised.astype(jnp.bfloat16), gather(1), preferred_element_type=jnp.float32)
        top[h] = jnp.broadcast_to(peak, (peak.shape[0], HD))
        total[h] = jnp.broadcast_to(added, (peak.shape[0], HD))
        return carry

    def arrived(target, semaphore):
        pltpu.make_async_remote_copy(
            src_ref=target, dst_ref=target, send_sem=semaphore, recv_sem=semaphore,
            device_id={"frame": core_peer}, device_id_type=MESH).wait_recv()

    for w, (first, size) in enumerate(wholes):
        inside_piece = [r for r, piece in enumerate(relayed) if first <= piece[0] < first + size]
        for side in range(2):
            @pl.when(sides[side][1])
            def _():
                arrived(whole.at[side, :, :, :, span(wholes[w])], w_recv.at[side, w])
            @pl.when(sides[side][2])
            def _():
                end_copy(TO_LOW_END, side, w).wait_recv()

        for slot, device, exists, here, entry in end_relays:
            @pl.when(exists)
            def _():
                arrived(inside.at[:, :, :, span(wholes[w])], i_recv.at[w])
                wanted = lists_s[here, 0, entry]
                for r in inside_piece:
                    columns = span(relayed[r])
                    for kv in range(2):
                        stage[slot, kv, :, columns] = chosen(lambda tile: inside[kv, tile, :, columns], wanted)
                    for part in parts_of(r):
                        part_copy(slot, RELAYED, r, part, device).start()

        for r in inside_piece:
            columns = span(relayed[r])
            for slot, there, device, exists, side, here, entry in relays:
                @pl.when(exists)
                def _():
                    wanted = lists_s[here, 0, entry]
                    for kv in range(2):
                        stage[slot, kv, :, columns] = chosen(lambda tile: whole[side, kv, tile, :, columns], wanted)
            for part in parts_of(r):
                for slot, there, device, exists, _, _, _ in relays:
                    @pl.when(exists)
                    def _():
                        part_copy(slot, there, r, part, device).start()

        @pl.when(outer & ~relays_to_end)
        def _():
            arrived(inside.at[:, :, :, span(wholes[w])], i_recv.at[w])

        @pl.when(outer)
        def _():
            wanted = lists_s[0, 0, levels * (1 - core)]
            for r in inside_piece:
                columns = span(relayed[r])
                for kv in range(2):
                    stage[INNER, kv, :, columns] = chosen(lambda tile: inside[kv, tile, :, columns], wanted)
                for part in parts_of(r):
                    part_copy(INNER, MIRROR, r, part, core_peer).start()

        @pl.when(inner)
        def _():
            across_copy(w).wait_recv()

        tile_copy(CORE, CORE, wholes, w, core_peer).wait_recv()
        lax.fori_loop(first, first + size, early, 0)

    def landed_at(kv, columns):
        return jnp.concatenate([landed[slot, kv, :, columns] for slot, _ in landings], axis=0)

    def weigh(h, columns):
        scores = lax.dot_general(
            q_v[:, columns], landed_at(0, columns), (((1,), (1,)), ((), ())), preferred_element_type=jnp.float32)
        scores = scores + late_bias
        old = top[h][:, :1]
        peak = jnp.maximum(old, jnp.max(scores, axis=1, keepdims=True))
        raised = jnp.exp2((scores - peak) * factor)
        fade = jnp.exp2((old - peak) * factor)
        added = jnp.sum(raised, axis=1, keepdims=True) + fade * total[h][:, :1]
        return raised.astype(jnp.bfloat16), fade * acc[h], added

    def finish(columns, raised, faded, added):
        mixed = jnp.dot(raised, landed_at(1, columns), preferred_element_type=jnp.float32) + faded
        out_ref[:, columns] = (mixed / added).astype(out_ref.dtype)

    def late(h, carry):
        columns = pl.ds(pl.multiple_of(h * HD, HD), HD)
        finish(columns, *weigh(h, columns))
        return carry

    def sent(source, target, semaphore):
        pltpu.make_async_remote_copy(
            src_ref=source, dst_ref=target, send_sem=semaphore, recv_sem=semaphore,
            device_id={"frame": core_peer}, device_id_type=MESH).wait_send()

    def drain_early():
        for _, exists, here, _ in partners:
            @pl.when(exists)
            def _():
                list_copy(core_peer, here, here).wait_send()
        for kv in range(2):
            @pl.when(inner)
            def _():
                sent((k_hbm, v_hbm)[kv], inside.at[kv], i_send.at[kv])
            for side in range(2):
                @pl.when(sides[side][0])
                def _():
                    sent((k_hbm, v_hbm)[kv], whole.at[side, kv], w_send.at[side, kv])
        early_slots = [(CORE, yes), (ACROSS, outer)] + [(slot, exists) for slot, _, exists, _, _ in end_sends]
        for slot, exists in early_slots:
            @pl.when(exists)
            def _():
                sent(stage.at[slot], landed.at[CORE], t_send.at[slot])

    def drain():
        late_slots = [(INNER, outer)]
        late_slots += [(slot, exists) for slot, _, _, exists, _, _ in far_sends]
        late_slots += [(slot, exists) for slot, _, _, exists, _, _, _ in relays]
        late_slots += [(slot, exists) for slot, _, exists, _, _ in end_relays]
        for slot, exists in late_slots:
            @pl.when(exists)
            def _():
                sent(stage.at[slot], landed.at[CORE], t_send.at[slot])

    def wait_landed(r, part):
        for slot, exists in landings:
            @pl.when(exists)
            def _():
                part_copy(CORE, slot, r, part, core_peer).wait_recv()

    last = len(relayed) - 1
    for r in range(last):
        first, size = relayed[r]
        wait_landed(r, None)
        lax.fori_loop(first, first + size, late, 0)
        if r == 0:
            drain_early()
    first, size = relayed[last]
    wait_landed(last, 0)
    weighed = [weigh(h, span((h, 1))) for h in range(first, first + size)]
    drain()
    wait_landed(last, 1)
    for h, ready in zip(range(first, first + size), weighed):
        finish(span((h, 1)), *ready)


def write_out(in_ref, out_ref, sem):
    copy = pltpu.make_async_copy(in_ref, out_ref, sem)
    copy.start()
    copy.wait()


def solution(mesh):
    n = mesh.shape["frame"]

    def body(queries, key_heads, value_heads, tile_lists):
        rows, channels = queries.shape
        heads = channels // HD
        tiles = rows // TILE
        levels = tile_lists.shape[1] // 2
        far = max(levels - 4, 0)
        lists = 5 + 2 * far
        bf16, f32 = jnp.bfloat16, jnp.float32
        hbm = pl.BlockSpec(memory_space=pltpu.HBM)
        dma = pltpu.SemaphoreType.DMA
        out_slots, in_slots = OUT_NEAR + 2 * far, NEAR + 2 * far
        result = pl.pallas_call(
            functools.partial(kernel, n, levels, heads),
            out_shape=pltpu.VMEM((rows, channels), bf16),
            in_specs=[hbm, hbm, hbm, pl.BlockSpec(memory_space=pltpu.SMEM)],
            out_specs=pl.BlockSpec(memory_space=pltpu.VMEM),
            scratch_shapes=[
                pltpu.VMEM((rows, channels), bf16),
                pltpu.VMEM((tiles, TILE, channels), bf16),
                pltpu.VMEM((tiles, TILE, channels), bf16),
                pltpu.VMEM((2, 2, tiles, TILE, channels), bf16),
                pltpu.VMEM((2, tiles, TILE, channels), bf16),
                pltpu.VMEM((out_slots, 2, TILE, channels), bf16),
                pltpu.VMEM((in_slots, 2, TILE, channels), bf16),
                pltpu.SMEM((lists, 1, 2 * levels), jnp.int32),
                pltpu.VMEM((heads, rows, HD), f32),
                pltpu.VMEM((heads, rows, HD), f32),
                pltpu.VMEM((heads, rows, HD), f32),
                dma((2, 2)),
                dma((2, len(WHOLE_PIECES))),
                dma((2,)),
                dma((len(WHOLE_PIECES),)),
                dma((out_slots,)),
                dma((in_slots, len(RELAY_PIECES) + 1)),
                dma((lists,)),
                dma((lists,)),
                dma((3,)),
            ],
            compiler_params=pltpu.CompilerParams(
                collective_id=0, has_side_effects=True, vmem_limit_bytes=61 << 20
            ),
        )(
            queries,
            key_heads.reshape(tiles, TILE, channels),
            value_heads.reshape(tiles, TILE, channels),
            tile_lists,
        )
        return pl.pallas_call(
            write_out,
            out_shape=jax.ShapeDtypeStruct((rows, channels), bf16),
            in_specs=[pl.BlockSpec(memory_space=pltpu.VMEM)],
            out_specs=pl.BlockSpec(memory_space=pl.ANY),
            scratch_shapes=[dma],
            compiler_params=pltpu.CompilerParams(vmem_limit_bytes=4 << 20),
        )(result)

    in_specs = (
        P(("groups", "frame"), None),
        P(("groups", "frame"), None),
        P(("groups", "frame"), None),
        P("frame", None),
    )
    return jax.shard_map(
        body, mesh=mesh, in_specs=in_specs, out_specs=P(("groups", "frame"), None), check_vma=False
    )
```

```python
import functools
import math

import jax
import jax.numpy as jnp
from jax import lax
from jax.experimental import pallas as pl
from jax.experimental.pallas import tpu as pltpu
from jax.sharding import PartitionSpec as P

HD = 128
TILE = 128
MESH = pl.DeviceIdType.MESH
ABSENT = -1e30

WHOLE_PIECES = (4, 6, 2)
RELAY_PIECES = (4, 4, 2, 2)

CORE, MIRROR, RELAYED, BELOW8, ABOVE8 = range(5)
NEAR = 5
ACROSS, INNER, TO_LOW_END, TO_HIGH_END, END_DOWN, END_UP = range(NEAR, NEAR + 6)
OUT_NEAR = NEAR + 6


def pieces_of(sizes, heads):
    unit = heads // sum(sizes)
    pieces, first = [], 0
    for size in sizes:
        pieces.append((first, size * unit))
        first += size * unit
    return pieces


def kernel(n, levels, heads, q_hbm, k_hbm, v_hbm, own_list, out_ref,
           q_v, k_v, v_v, whole, inside, stage, landed, lists_s, top, total, acc,
           w_send, w_recv, i_send, i_recv, t_send, t_recv, l_send, l_recv, in_sem):
    me = lax.axis_index("frame")
    quarter = me % 4
    x = quarter // 2
    core = me % 2
    core_peer = me + 1 - 2 * core
    across = me + 2 - 4 * x
    mirror = me + 3 - 2 * quarter
    inner = (quarter == 1) | (quarter == 2)
    outer = (quarter == 0) | (quarter == 3)
    has_low, has_high = me >= 4, me + 4 < n
    low_corner, high_corner = quarter == 0, quarter == 3
    to_low_end, to_high_end = has_low & (me < 8), has_high & (me + 8 >= n)
    chosen_down, chosen_up = to_low_end & ~low_corner, to_high_end & ~high_corner
    low_chosen, high_chosen = (me + 4 >= n) & ~high_corner, (me < 4) & ~low_corner
    tiles = k_v.shape[0]
    far = [1 << level for level in range(4, levels)]
    yes = me >= 0
    wholes = pieces_of(WHOLE_PIECES, heads)
    relayed = pieces_of(RELAY_PIECES, heads)

    partners = [
        (core_peer, yes, 0, 0),
        (across, yes, 1, 1),
        (mirror, yes, 2, 2),
        (me - 4, has_low, 3, 4),
        (me + 4, has_high, 4, 3),
    ]
    for j, d in enumerate(far):
        partners.append((me - d, me >= d, 5 + 2 * j, 6 + 2 * j))
        partners.append((me + d, me + d < n, 6 + 2 * j, 5 + 2 * j))

    def when(exists):
        return (lambda run: run()) if exists is yes else pl.when(exists)

    barrier = pltpu.get_barrier_semaphore()
    for device, exists, _, _ in partners:
        @when(exists)
        def _():
            pl.semaphore_signal(barrier, inc=1, device_id={"frame": device}, device_id_type=MESH)
    loads = [
        pltpu.make_async_copy(source, target, in_sem.at[i])
        for i, (source, target) in enumerate(((k_hbm, k_v), (v_hbm, v_v), (q_hbm, q_v)))
    ]
    for load in loads:
        load.start()
    pl.semaphore_wait(barrier, sum(jnp.where(exists, 1, 0) for _, exists, _, _ in partners))

    def span(piece):
        return pl.ds(piece[0] * HD, piece[1] * HD)

    def whole_copy(side, i, kv):
        columns = span(wholes[i])
        return pltpu.make_async_remote_copy(
            src_ref=(k_hbm, v_hbm)[kv].at[:, :, columns], dst_ref=whole.at[side, kv, :, :, columns],
            send_sem=w_send.at[side, kv], recv_sem=w_recv.at[side, i],
            device_id={"frame": me + 4 if side == 0 else me - 4}, device_id_type=MESH)

    def inner_copy(i, kv):
        columns = span(wholes[i])
        return pltpu.make_async_remote_copy(
            src_ref=(k_hbm, v_hbm)[kv].at[:, :, columns], dst_ref=inside.at[kv, :, :, columns],
            send_sem=i_send.at[kv], recv_sem=i_recv.at[i],
            device_id={"frame": across}, device_id_type=MESH)

    def across_copy(i):
        columns = span(wholes[i])
        return pltpu.make_async_remote_copy(
            src_ref=stage.at[ACROSS, :, :, columns], dst_ref=inside.at[:, 0, :, columns],
            send_sem=t_send.at[ACROSS], recv_sem=i_recv.at[i],
            device_id={"frame": across}, device_id_type=MESH)

    def end_copy(slot, side, i):
        columns = span(wholes[i])
        return pltpu.make_async_remote_copy(
            src_ref=stage.at[slot, :, :, columns], dst_ref=whole.at[side, :, 0, :, columns],
            send_sem=t_send.at[slot], recv_sem=w_recv.at[side, i],
            device_id={"frame": me + 4 if side == 0 else me - 4}, device_id_type=MESH)

    def list_copy(device, here, there):
        return pltpu.make_async_remote_copy(
            src_ref=own_list, dst_ref=lists_s.at[there],
            send_sem=l_send.at[here], recv_sem=l_recv.at[there],
            device_id={"frame": device}, device_id_type=MESH)

    def tile_copy(slot, there, pieces, i, device):
        columns = span(pieces[i])
        return pltpu.make_async_remote_copy(
            src_ref=stage.at[slot, :, :, columns], dst_ref=landed.at[there, :, :, columns],
            send_sem=t_send.at[slot], recv_sem=t_recv.at[there, i],
            device_id={"frame": device}, device_id_type=MESH)

    def parts_of(r):
        return (0, 1) if r == len(relayed) - 1 else (None,)

    def part_copy(slot, there, r, part, device):
        columns = span(relayed[r])
        at = slice(None) if part is None else part
        i = r + (part or 0)
        return pltpu.make_async_remote_copy(
            src_ref=stage.at[slot, at, :, columns], dst_ref=landed.at[there, at, :, columns],
            send_sem=t_send.at[slot], recv_sem=t_recv.at[there, i],
            device_id={"frame": device}, device_id_type=MESH)

    sides = (
        (has_high & ~chosen_up, has_low & ~low_chosen, has_low & low_chosen),
        (has_low & ~chosen_down, has_high & ~high_chosen, has_high & high_chosen),
    )
    end_sends = [(TO_HIGH_END, 0, chosen_up, 4, 2), (TO_LOW_END, 1, chosen_down, 3, levels + 2)]

    def send_lists(chosen_partners):
        for device, exists, here, there in chosen_partners:
            @when(exists)
            def _():
                list_copy(device, here, there).start()

    def send_wholes(i):
        for side in range(2):
            @pl.when(sides[side][0])
            def _():
                for kv in range(2):
                    whole_copy(side, i, kv).start()

    def send_inner(i):
        @pl.when(inner)
        def _():
            for kv in range(2):
                inner_copy(i, kv).start()

    send_lists(partners[1:3])
    send_inner(0)
    send_lists(partners[3:])
    send_wholes(0)
    send_lists(partners[:1])
    for i in range(1, len(wholes)):
        send_inner(i)
        send_wholes(i)

    landings = [
        (MIRROR, inner | ((quarter == 0) & has_low) | ((quarter == 3) & has_high)),
        (RELAYED, ((x == 0) & has_low) | ((x == 1) & has_high)),
        (BELOW8, me >= 8),
        (ABOVE8, me + 8 < n),
    ]
    for j, d in enumerate(far):
        landings.append((NEAR + 2 * j, me >= d))
        landings.append((NEAR + 2 * j + 1, me + d < n))
    for slot, exists in landings:
        @pl.when(jnp.logical_not(exists))
        def _():
            landed[slot] = jnp.zeros(landed.shape[1:], landed.dtype)
    for side in range(2):
        @pl.when(jnp.logical_not((has_low, has_high)[side]))
        def _():
            whole[side] = jnp.zeros(whole.shape[1:], whole.dtype)

    for load in loads:
        load.wait()
    for _, exists, here, _ in partners:
        @when(exists)
        def _():
            list_copy(core_peer, here, here).wait_recv()

    def stage_own(slot, columns, wanted):
        stage[slot, 0, :, columns] = k_v[wanted, :, columns]
        stage[slot, 1, :, columns] = v_v[wanted, :, columns]

    far_sends = []
    for j, d in enumerate(far):
        far_sends.append((OUT_NEAR + 2 * j, NEAR + 2 * j, me + d, me + d < n, 6 + 2 * j, 4 + j))
        far_sends.append((OUT_NEAR + 2 * j + 1, NEAR + 2 * j + 1, me - d, me >= d, 5 + 2 * j, levels + 4 + j))

    for i, piece in enumerate(wholes):
        for slot, side, exists, here, entry in end_sends:
            @when(exists)
            def _():
                stage_own(slot, span(piece), lists_s[here, 0, entry])
                end_copy(slot, side, i).start()
        @pl.when(outer)
        def _():
            stage_own(ACROSS, span(piece), lists_s[1, 0, 1 + levels * x])
            across_copy(i).start()
        stage_own(CORE, span(piece), lists_s[0, 0, levels * core])
        tile_copy(CORE, CORE, wholes, i, core_peer).start()
    for slot, there, device, exists, here, entry in far_sends:
        @when(exists)
        def _():
            for i, piece in enumerate(relayed):
                stage_own(slot, span(piece), lists_s[here, 0, entry])
                for part in parts_of(i):
                    part_copy(slot, there, i, part, device).start()

    factor = math.log2(math.e) / math.sqrt(HD)

    def bias_of(parts):
        return jnp.concatenate(
            [jnp.full((1, size), jnp.where(exists, 0.0, ABSENT), jnp.float32) for size, exists in parts], axis=1)

    near_bias = bias_of([((tiles + 2) * TILE, yes), (TILE, has_low), (TILE, has_high)])
    late_bias = bias_of([(TILE, exists) for _, exists in landings])

    relays = [
        (MIRROR, MIRROR, mirror, (quarter == 0) & has_high, 1, 2, levels),
        (MIRROR, MIRROR, mirror, (quarter == 3) & has_low, 0, 2, 0),
        (RELAYED, RELAYED, across, (x == 0) & has_high & (low_corner | ((me >= 4) & (me + 8 < n))), 1, 1, levels + 1),
        (RELAYED, RELAYED, across, (x == 1) & has_low & (high_corner | ((me + 4 < n) & (me >= 8))), 0, 1, 1),
        (BELOW8, BELOW8, me + 4, has_low & has_high, 0, 4, 3),
        (ABOVE8, ABOVE8, me - 4, has_low & has_high, 1, 3, levels + 3),
    ]
    relay_down = has_low & high_corner & (to_low_end | (me + 4 >= n))
    relay_up = has_high & low_corner & (to_high_end | (me < 4))
    end_relays = [
        (END_DOWN, me - 4, relay_down, 3, levels + 1),
        (END_UP, me + 4, relay_up, 4, 1),
    ]
    relays_to_end = relay_down | relay_up

    def chosen(block_of, wanted):
        block = block_of(0)
        for tile in range(1, tiles):
            block = jnp.where(wanted == tile, block_of(tile), block)
        return block

    low = jnp.where(low_chosen, 0, own_list[0, 2])
    high = jnp.where(high_chosen, 0, own_list[0, levels + 2])
    beside = jnp.where(outer, own_list[0, 1 + levels * (1 - x)], 0)

    def early(h, carry):
        columns = pl.ds(pl.multiple_of(h * HD, HD), HD)

        def gather(kv):
            own = (k_v, v_v)[kv]
            return jnp.concatenate(
                [own[tile, :, columns] for tile in range(tiles)] + [
                    landed[CORE, kv, :, columns],
                    chosen(lambda tile: inside[kv, tile, :, columns], beside),
                    chosen(lambda tile: whole[0, kv, tile, :, columns], low),
                    chosen(lambda tile: whole[1, kv, tile, :, columns], high)], axis=0)
        scores = lax.dot_general(
            q_v[:, columns], gather(0), (((1,), (1,)), ((), ())), preferred_element_type=jnp.float32)
        scores = scores + near_bias
        peak = jnp.max(scores, axis=1, keepdims=True)
        raised = jnp.exp2((scores - peak) * factor)
        added = jnp.sum(raised, axis=1, keepdims=True)
        acc[h] = jnp.dot(raised.astype(jnp.bfloat16), gather(1), preferred_element_type=jnp.float32)
        top[h] = jnp.broadcast_to(peak, (peak.shape[0], HD))
        total[h] = jnp.broadcast_to(added, (peak.shape[0], HD))
        return carry

    def arrived(target, semaphore):
        pltpu.make_async_remote_copy(
            src_ref=target, dst_ref=target, send_sem=semaphore, recv_sem=semaphore,
            device_id={"frame": core_peer}, device_id_type=MESH).wait_recv()

    for w, (first, size) in enumerate(wholes):
        inside_piece = [r for r, piece in enumerate(relayed) if first <= piece[0] < first + size]
        for side in range(2):
            @pl.when(sides[side][1])
            def _():
                arrived(whole.at[side, :, :, :, span(wholes[w])], w_recv.at[side, w])
            @pl.when(sides[side][2])
            def _():
                end_copy(TO_LOW_END, side, w).wait_recv()

        for slot, device, exists, here, entry in end_relays:
            @when(exists)
            def _():
                arrived(inside.at[:, :, :, span(wholes[w])], i_recv.at[w])
                wanted = lists_s[here, 0, entry]
                for r in inside_piece:
                    columns = span(relayed[r])
                    for kv in range(2):
                        stage[slot, kv, :, columns] = chosen(lambda tile: inside[kv, tile, :, columns], wanted)
                    for part in parts_of(r):
                        part_copy(slot, RELAYED, r, part, device).start()

        for r in inside_piece:
            columns = span(relayed[r])
            for slot, there, device, exists, side, here, entry in relays:
                @when(exists)
                def _():
                    wanted = lists_s[here, 0, entry]
                    for kv in range(2):
                        stage[slot, kv, :, columns] = chosen(lambda tile: whole[side, kv, tile, :, columns], wanted)
            for part in parts_of(r):
                for slot, there, device, exists, _, _, _ in relays:
                    @when(exists)
                    def _():
                        part_copy(slot, there, r, part, device).start()

        @pl.when(outer & ~relays_to_end)
        def _():
            arrived(inside.at[:, :, :, span(wholes[w])], i_recv.at[w])

        @pl.when(outer)
        def _():
            wanted = lists_s[0, 0, levels * (1 - core)]
            for r in inside_piece:
                columns = span(relayed[r])
                for kv in range(2):
                    stage[INNER, kv, :, columns] = chosen(lambda tile: inside[kv, tile, :, columns], wanted)
                for part in parts_of(r):
                    part_copy(INNER, MIRROR, r, part, core_peer).start()

        @pl.when(inner)
        def _():
            across_copy(w).wait_recv()

        tile_copy(CORE, CORE, wholes, w, core_peer).wait_recv()
        lax.fori_loop(first, first + size, early, 0)

    def landed_at(kv, columns):
        return jnp.concatenate([landed[slot, kv, :, columns] for slot, _ in landings], axis=0)

    def weigh(h, columns):
        scores = lax.dot_general(
            q_v[:, columns], landed_at(0, columns), (((1,), (1,)), ((), ())), preferred_element_type=jnp.float32)
        scores = scores + late_bias
        old = top[h][:, :1]
        peak = jnp.maximum(old, jnp.max(scores, axis=1, keepdims=True))
        raised = jnp.exp2((scores - peak) * factor)
        fade = jnp.exp2((old - peak) * factor)
        added = jnp.sum(raised, axis=1, keepdims=True) + fade * total[h][:, :1]
        return raised.astype(jnp.bfloat16), fade * acc[h], added

    def finish(columns, raised, faded, added):
        mixed = jnp.dot(raised, landed_at(1, columns), preferred_element_type=jnp.float32) + faded
        out_ref[:, columns] = (mixed / added).astype(out_ref.dtype)

    def late(h, carry):
        columns = pl.ds(pl.multiple_of(h * HD, HD), HD)
        finish(columns, *weigh(h, columns))
        return carry

    def sent(source, target, semaphore):
        pltpu.make_async_remote_copy(
            src_ref=source, dst_ref=target, send_sem=semaphore, recv_sem=semaphore,
            device_id={"frame": core_peer}, device_id_type=MESH).wait_send()

    def drain_early():
        for _, exists, here, _ in partners:
            @when(exists)
            def _():
                list_copy(core_peer, here, here).wait_send()
        for kv in range(2):
            @pl.when(inner)
            def _():
                sent((k_hbm, v_hbm)[kv], inside.at[kv], i_send.at[kv])
            for side in range(2):
                @pl.when(sides[side][0])
                def _():
                    sent((k_hbm, v_hbm)[kv], whole.at[side, kv], w_send.at[side, kv])
        early_slots = [(CORE, yes), (ACROSS, outer)] + [(slot, exists) for slot, _, exists, _, _ in end_sends]
        for slot, exists in early_slots:
            @when(exists)
            def _():
                sent(stage.at[slot], landed.at[CORE], t_send.at[slot])

    def drain():
        late_slots = [(INNER, outer)]
        late_slots += [(slot, exists) for slot, _, _, exists, _, _ in far_sends]
        sent_by_slot = {}
        for slot, _, _, exists, _, _, _ in relays:
            sent_by_slot[slot] = sent_by_slot[slot] | exists if slot in sent_by_slot else exists
        late_slots += list(sent_by_slot.items())
        late_slots += [(slot, exists) for slot, _, exists, _, _ in end_relays]
        for slot, exists in late_slots:
            @when(exists)
            def _():
                sent(stage.at[slot], landed.at[CORE], t_send.at[slot])

    def wait_landed(r, part):
        for slot, exists in landings:
            @when(exists)
            def _():
                part_copy(CORE, slot, r, part, core_peer).wait_recv()

    last = len(relayed) - 1
    for r in range(last):
        first, size = relayed[r]
        wait_landed(r, None)
        lax.fori_loop(first, first + size, late, 0)
        if r == 0:
            drain_early()
    first, size = relayed[last]
    wait_landed(last, 0)
    weighed = [weigh(h, span((h, 1))) for h in range(first, first + size)]
    drain()
    wait_landed(last, 1)
    for h, ready in zip(range(first, first + size), weighed):
        finish(span((h, 1)), *ready)


def write_out(in_ref, out_ref, sem):
    copy = pltpu.make_async_copy(in_ref, out_ref, sem)
    copy.start()
    copy.wait()


def solution(mesh):
    n = mesh.shape["frame"]

    def body(queries, key_heads, value_heads, tile_lists):
        rows, channels = queries.shape
        heads = channels // HD
        tiles = rows // TILE
        levels = tile_lists.shape[1] // 2
        far = max(levels - 4, 0)
        lists = 5 + 2 * far
        bf16, f32 = jnp.bfloat16, jnp.float32
        hbm = pl.BlockSpec(memory_space=pltpu.HBM)
        dma = pltpu.SemaphoreType.DMA
        out_slots, in_slots = OUT_NEAR + 2 * far, NEAR + 2 * far
        result = pl.pallas_call(
            functools.partial(kernel, n, levels, heads),
            out_shape=pltpu.VMEM((rows, channels), bf16),
            in_specs=[hbm, hbm, hbm, pl.BlockSpec(memory_space=pltpu.SMEM)],
            out_specs=pl.BlockSpec(memory_space=pltpu.VMEM),
            scratch_shapes=[
                pltpu.VMEM((rows, channels), bf16),
                pltpu.VMEM((tiles, TILE, channels), bf16),
                pltpu.VMEM((tiles, TILE, channels), bf16),
                pltpu.VMEM((2, 2, tiles, TILE, channels), bf16),
                pltpu.VMEM((2, tiles, TILE, channels), bf16),
                pltpu.VMEM((out_slots, 2, TILE, channels), bf16),
                pltpu.VMEM((in_slots, 2, TILE, channels), bf16),
                pltpu.SMEM((lists, 1, 2 * levels), jnp.int32),
                pltpu.VMEM((heads, rows, HD), f32),
                pltpu.VMEM((heads, rows, HD), f32),
                pltpu.VMEM((heads, rows, HD), f32),
                dma((2, 2)),
                dma((2, len(WHOLE_PIECES))),
                dma((2,)),
                dma((len(WHOLE_PIECES),)),
                dma((out_slots,)),
                dma((in_slots, len(RELAY_PIECES) + 1)),
                dma((lists,)),
                dma((lists,)),
                dma((3,)),
            ],
            compiler_params=pltpu.CompilerParams(
                collective_id=0, has_side_effects=True, vmem_limit_bytes=61 << 20
            ),
        )(
            queries,
            key_heads.reshape(tiles, TILE, channels),
            value_heads.reshape(tiles, TILE, channels),
            tile_lists,
        )
        return pl.pallas_call(
            write_out,
            out_shape=jax.ShapeDtypeStruct((rows, channels), bf16),
            in_specs=[pl.BlockSpec(memory_space=pltpu.VMEM)],
            out_specs=pl.BlockSpec(memory_space=pl.ANY),
            scratch_shapes=[dma],
            compiler_params=pltpu.CompilerParams(vmem_limit_bytes=4 << 20),
        )(result)

    in_specs = (
        P(("groups", "frame"), None),
        P(("groups", "frame"), None),
        P(("groups", "frame"), None),
        P("frame", None),
    )
    return jax.shard_map(
        body, mesh=mesh, in_specs=in_specs, out_specs=P(("groups", "frame"), None), check_vma=False
    )
```

```python
import functools
import math

import jax
import jax.numpy as jnp
from jax import lax
from jax.experimental import pallas as pl
from jax.experimental.pallas import tpu as pltpu
from jax.sharding import PartitionSpec as P

HD = 128
TILE = 128
MESH = pl.DeviceIdType.MESH
ABSENT = -1e30

WHOLE_PIECES = (4, 4, 4)
RELAY_PIECES = (4, 4, 2, 2)

CORE, MIRROR, RELAYED, BELOW8, ABOVE8 = range(5)
NEAR = 5
ACROSS, INNER, TO_LOW_END, TO_HIGH_END, END_DOWN, END_UP = range(NEAR, NEAR + 6)
OUT_NEAR = NEAR + 6


def pieces_of(sizes, heads):
    unit = heads // sum(sizes)
    pieces, first = [], 0
    for size in sizes:
        pieces.append((first, size * unit))
        first += size * unit
    return pieces


def kernel(n, levels, heads, q_hbm, k_hbm, v_hbm, own_list, out_ref,
           q_v, k_v, v_v, whole, inside, stage, landed, lists_s, top, total, acc,
           w_send, w_recv, i_send, i_recv, t_send, t_recv, l_send, l_recv, in_sem):
    me = lax.axis_index("frame")
    quarter = me % 4
    x = quarter // 2
    core = me % 2
    core_peer = me + 1 - 2 * core
    across = me + 2 - 4 * x
    mirror = me + 3 - 2 * quarter
    inner = (quarter == 1) | (quarter == 2)
    outer = (quarter == 0) | (quarter == 3)
    has_low, has_high = me >= 4, me + 4 < n
    low_corner, high_corner = quarter == 0, quarter == 3
    to_low_end, to_high_end = has_low & (me < 8), has_high & (me + 8 >= n)
    chosen_down, chosen_up = to_low_end & ~low_corner, to_high_end & ~high_corner
    low_chosen, high_chosen = (me + 4 >= n) & ~high_corner, (me < 4) & ~low_corner
    tiles = k_v.shape[0]
    far = [1 << level for level in range(4, levels)]
    yes = me >= 0
    wholes = pieces_of(WHOLE_PIECES, heads)
    relayed = pieces_of(RELAY_PIECES, heads)

    partners = [
        (core_peer, yes, 0, 0),
        (across, yes, 1, 1),
        (mirror, yes, 2, 2),
        (me - 4, has_low, 3, 4),
        (me + 4, has_high, 4, 3),
    ]
    for j, d in enumerate(far):
        partners.append((me - d, me >= d, 5 + 2 * j, 6 + 2 * j))
        partners.append((me + d, me + d < n, 6 + 2 * j, 5 + 2 * j))

    barrier = pltpu.get_barrier_semaphore()
    for device, exists, _, _ in partners:
        @pl.when(exists)
        def _():
            pl.semaphore_signal(barrier, inc=1, device_id={"frame": device}, device_id_type=MESH)
    loads = [
        pltpu.make_async_copy(source, target, in_sem.at[i])
        for i, (source, target) in enumerate(((k_hbm, k_v), (v_hbm, v_v), (q_hbm, q_v)))
    ]
    for load in loads:
        load.start()
    pl.semaphore_wait(barrier, sum(jnp.where(exists, 1, 0) for _, exists, _, _ in partners))

    def span(piece):
        return pl.ds(piece[0] * HD, piece[1] * HD)

    def whole_copy(side, i, kv):
        columns = span(wholes[i])
        return pltpu.make_async_remote_copy(
            src_ref=(k_hbm, v_hbm)[kv].at[:, :, columns], dst_ref=whole.at[side, kv, :, :, columns],
            send_sem=w_send.at[side, kv], recv_sem=w_recv.at[side, i],
            device_id={"frame": me + 4 if side == 0 else me - 4}, device_id_type=MESH)

    def inner_copy(i, kv):
        columns = span(wholes[i])
        return pltpu.make_async_remote_copy(
            src_ref=(k_hbm, v_hbm)[kv].at[:, :, columns], dst_ref=inside.at[kv, :, :, columns],
            send_sem=i_send.at[kv], recv_sem=i_recv.at[i],
            device_id={"frame": across}, device_id_type=MESH)

    def across_copy(i):
        columns = span(wholes[i])
        return pltpu.make_async_remote_copy(
            src_ref=stage.at[ACROSS, :, :, columns], dst_ref=inside.at[:, 0, :, columns],
            send_sem=t_send.at[ACROSS], recv_sem=i_recv.at[i],
            device_id={"frame": across}, device_id_type=MESH)

    def end_copy(slot, side, i):
        columns = span(wholes[i])
        return pltpu.make_async_remote_copy(
            src_ref=stage.at[slot, :, :, columns], dst_ref=whole.at[side, :, 0, :, columns],
            send_sem=t_send.at[slot], recv_sem=w_recv.at[side, i],
            device_id={"frame": me + 4 if side == 0 else me - 4}, device_id_type=MESH)

    def list_copy(device, here, there):
        return pltpu.make_async_remote_copy(
            src_ref=own_list, dst_ref=lists_s.at[there],
            send_sem=l_send.at[here], recv_sem=l_recv.at[there],
            device_id={"frame": device}, device_id_type=MESH)

    def tile_copy(slot, there, pieces, i, device):
        columns = span(pieces[i])
        return pltpu.make_async_remote_copy(
            src_ref=stage.at[slot, :, :, columns], dst_ref=landed.at[there, :, :, columns],
            send_sem=t_send.at[slot], recv_sem=t_recv.at[there, i],
            device_id={"frame": device}, device_id_type=MESH)

    def parts_of(r):
        return (0, 1) if r == len(relayed) - 1 else (None,)

    def part_copy(slot, there, r, part, device):
        columns = span(relayed[r])
        at = slice(None) if part is None else part
        i = r + (part or 0)
        return pltpu.make_async_remote_copy(
            src_ref=stage.at[slot, at, :, columns], dst_ref=landed.at[there, at, :, columns],
            send_sem=t_send.at[slot], recv_sem=t_recv.at[there, i],
            device_id={"frame": device}, device_id_type=MESH)

    sides = (
        (has_high & ~chosen_up, has_low & ~low_chosen, has_low & low_chosen),
        (has_low & ~chosen_down, has_high & ~high_chosen, has_high & high_chosen),
    )
    end_sends = [(TO_HIGH_END, 0, chosen_up, 4, 2), (TO_LOW_END, 1, chosen_down, 3, levels + 2)]

    def send_lists(chosen_partners):
        for device, exists, here, there in chosen_partners:
            @pl.when(exists)
            def _():
                list_copy(device, here, there).start()

    def send_wholes(i):
        for side in range(2):
            @pl.when(sides[side][0])
            def _():
                for kv in range(2):
                    whole_copy(side, i, kv).start()

    def send_inner(i):
        @pl.when(inner)
        def _():
            for kv in range(2):
                inner_copy(i, kv).start()

    send_lists(partners[1:3])
    send_inner(0)
    send_lists(partners[3:])
    send_wholes(0)
    send_lists(partners[:1])
    for i in range(1, len(wholes)):
        send_inner(i)
        send_wholes(i)

    landings = [
        (MIRROR, inner | ((quarter == 0) & has_low) | ((quarter == 3) & has_high)),
        (RELAYED, ((x == 0) & has_low) | ((x == 1) & has_high)),
        (BELOW8, me >= 8),
        (ABOVE8, me + 8 < n),
    ]
    for j, d in enumerate(far):
        landings.append((NEAR + 2 * j, me >= d))
        landings.append((NEAR + 2 * j + 1, me + d < n))
    for slot, exists in landings:
        @pl.when(jnp.logical_not(exists))
        def _():
            landed[slot] = jnp.zeros(landed.shape[1:], landed.dtype)
    for side in range(2):
        @pl.when(jnp.logical_not((has_low, has_high)[side]))
        def _():
            whole[side] = jnp.zeros(whole.shape[1:], whole.dtype)

    for load in loads:
        load.wait()
    for _, exists, here, _ in partners:
        @pl.when(exists)
        def _():
            list_copy(core_peer, here, here).wait_recv()

    def stage_own(slot, columns, wanted):
        stage[slot, 0, :, columns] = k_v[wanted, :, columns]
        stage[slot, 1, :, columns] = v_v[wanted, :, columns]

    far_sends = []
    for j, d in enumerate(far):
        far_sends.append((OUT_NEAR + 2 * j, NEAR + 2 * j, me + d, me + d < n, 6 + 2 * j, 4 + j))
        far_sends.append((OUT_NEAR + 2 * j + 1, NEAR + 2 * j + 1, me - d, me >= d, 5 + 2 * j, levels + 4 + j))

    for i, piece in enumerate(wholes):
        for slot, side, exists, here, entry in end_sends:
            @pl.when(exists)
            def _():
                stage_own(slot, span(piece), lists_s[here, 0, entry])
                end_copy(slot, side, i).start()
        @pl.when(outer)
        def _():
            stage_own(ACROSS, span(piece), lists_s[1, 0, 1 + levels * x])
            across_copy(i).start()
        stage_own(CORE, span(piece), lists_s[0, 0, levels * core])
        tile_copy(CORE, CORE, wholes, i, core_peer).start()
    for slot, there, device, exists, here, entry in far_sends:
        @pl.when(exists)
        def _():
            for i, piece in enumerate(relayed):
                stage_own(slot, span(piece), lists_s[here, 0, entry])
                for part in parts_of(i):
                    part_copy(slot, there, i, part, device).start()

    factor = math.log2(math.e) / math.sqrt(HD)

    def bias_of(parts):
        return jnp.concatenate(
            [jnp.full((1, size), jnp.where(exists, 0.0, ABSENT), jnp.float32) for size, exists in parts], axis=1)

    near_bias = bias_of([((tiles + 2) * TILE, yes), (TILE, has_low), (TILE, has_high)])
    late_bias = bias_of([(TILE, exists) for _, exists in landings])

    relays = [
        (MIRROR, MIRROR, mirror, (quarter == 0) & has_high, 1, 2, levels),
        (MIRROR, MIRROR, mirror, (quarter == 3) & has_low, 0, 2, 0),
        (RELAYED, RELAYED, across, (x == 0) & has_high & (low_corner | ((me >= 4) & (me + 8 < n))), 1, 1, levels + 1),
        (RELAYED, RELAYED, across, (x == 1) & has_low & (high_corner | ((me + 4 < n) & (me >= 8))), 0, 1, 1),
        (BELOW8, BELOW8, me + 4, has_low & has_high, 0, 4, 3),
        (ABOVE8, ABOVE8, me - 4, has_low & has_high, 1, 3, levels + 3),
    ]
    relay_down = has_low & high_corner & (to_low_end | (me + 4 >= n))
    relay_up = has_high & low_corner & (to_high_end | (me < 4))
    end_relays = [
        (END_DOWN, me - 4, relay_down, 3, levels + 1),
        (END_UP, me + 4, relay_up, 4, 1),
    ]
    relays_to_end = relay_down | relay_up

    def chosen(block_of, wanted):
        block = block_of(0)
        for tile in range(1, tiles):
            block = jnp.where(wanted == tile, block_of(tile), block)
        return block

    low = jnp.where(low_chosen, 0, own_list[0, 2])
    high = jnp.where(high_chosen, 0, own_list[0, levels + 2])
    beside = jnp.where(outer, own_list[0, 1 + levels * (1 - x)], 0)

    def early(h, carry):
        columns = pl.ds(pl.multiple_of(h * HD, HD), HD)

        def gather(kv):
            own = (k_v, v_v)[kv]
            return jnp.concatenate(
                [own[tile, :, columns] for tile in range(tiles)] + [
                    landed[CORE, kv, :, columns],
                    chosen(lambda tile: inside[kv, tile, :, columns], beside),
                    chosen(lambda tile: whole[0, kv, tile, :, columns], low),
                    chosen(lambda tile: whole[1, kv, tile, :, columns], high)], axis=0)
        scores = lax.dot_general(
            q_v[:, columns], gather(0), (((1,), (1,)), ((), ())), preferred_element_type=jnp.float32)
        scores = scores + near_bias
        peak = jnp.max(scores, axis=1, keepdims=True)
        raised = jnp.exp2((scores - peak) * factor)
        added = jnp.sum(raised, axis=1, keepdims=True)
        acc[h] = jnp.dot(raised.astype(jnp.bfloat16), gather(1), preferred_element_type=jnp.float32)
        top[h] = jnp.broadcast_to(peak, (peak.shape[0], HD))
        total[h] = jnp.broadcast_to(added, (peak.shape[0], HD))
        return carry

    def arrived(target, semaphore):
        pltpu.make_async_remote_copy(
            src_ref=target, dst_ref=target, send_sem=semaphore, recv_sem=semaphore,
            device_id={"frame": core_peer}, device_id_type=MESH).wait_recv()

    for w, (first, size) in enumerate(wholes):
        inside_piece = [r for r, piece in enumerate(relayed) if first <= piece[0] < first + size]
        for side in range(2):
            @pl.when(sides[side][1])
            def _():
                arrived(whole.at[side, :, :, :, span(wholes[w])], w_recv.at[side, w])
            @pl.when(sides[side][2])
            def _():
                end_copy(TO_LOW_END, side, w).wait_recv()

        for slot, device, exists, here, entry in end_relays:
            @pl.when(exists)
            def _():
                arrived(inside.at[:, :, :, span(wholes[w])], i_recv.at[w])
                wanted = lists_s[here, 0, entry]
                for r in inside_piece:
                    columns = span(relayed[r])
                    for kv in range(2):
                        stage[slot, kv, :, columns] = chosen(lambda tile: inside[kv, tile, :, columns], wanted)
                    for part in parts_of(r):
                        part_copy(slot, RELAYED, r, part, device).start()

        for r in inside_piece:
            columns = span(relayed[r])
            for slot, there, device, exists, side, here, entry in relays:
                @pl.when(exists)
                def _():
                    wanted = lists_s[here, 0, entry]
                    for kv in range(2):
                        stage[slot, kv, :, columns] = chosen(lambda tile: whole[side, kv, tile, :, columns], wanted)
            for part in parts_of(r):
                for slot, there, device, exists, _, _, _ in relays:
                    @pl.when(exists)
                    def _():
                        part_copy(slot, there, r, part, device).start()

        @pl.when(outer & ~relays_to_end)
        def _():
            arrived(inside.at[:, :, :, span(wholes[w])], i_recv.at[w])

        @pl.when(outer)
        def _():
            wanted = lists_s[0, 0, levels * (1 - core)]
            for r in inside_piece:
                columns = span(relayed[r])
                for kv in range(2):
                    stage[INNER, kv, :, columns] = chosen(lambda tile: inside[kv, tile, :, columns], wanted)
                for part in parts_of(r):
                    part_copy(INNER, MIRROR, r, part, core_peer).start()

        @pl.when(inner)
        def _():
            across_copy(w).wait_recv()

        tile_copy(CORE, CORE, wholes, w, core_peer).wait_recv()
        lax.fori_loop(first, first + size, early, 0)

    def landed_at(kv, columns):
        return jnp.concatenate([landed[slot, kv, :, columns] for slot, _ in landings], axis=0)

    def weigh(h, columns):
        scores = lax.dot_general(
            q_v[:, columns], landed_at(0, columns), (((1,), (1,)), ((), ())), preferred_element_type=jnp.float32)
        scores = scores + late_bias
        old = top[h][:, :1]
        peak = jnp.maximum(old, jnp.max(scores, axis=1, keepdims=True))
        raised = jnp.exp2((scores - peak) * factor)
        fade = jnp.exp2((old - peak) * factor)
        added = jnp.sum(raised, axis=1, keepdims=True) + fade * total[h][:, :1]
        return raised.astype(jnp.bfloat16), fade * acc[h], added

    def finish(columns, raised, faded, added):
        mixed = jnp.dot(raised, landed_at(1, columns), preferred_element_type=jnp.float32) + faded
        out_ref[:, columns] = (mixed / added).astype(out_ref.dtype)

    def late(h, carry):
        columns = pl.ds(pl.multiple_of(h * HD, HD), HD)
        finish(columns, *weigh(h, columns))
        return carry

    def sent(source, target, semaphore):
        pltpu.make_async_remote_copy(
            src_ref=source, dst_ref=target, send_sem=semaphore, recv_sem=semaphore,
            device_id={"frame": core_peer}, device_id_type=MESH).wait_send()

    def drain_early():
        for _, exists, here, _ in partners:
            @pl.when(exists)
            def _():
                list_copy(core_peer, here, here).wait_send()
        for kv in range(2):
            @pl.when(inner)
            def _():
                sent((k_hbm, v_hbm)[kv], inside.at[kv], i_send.at[kv])
            for side in range(2):
                @pl.when(sides[side][0])
                def _():
                    sent((k_hbm, v_hbm)[kv], whole.at[side, kv], w_send.at[side, kv])
        early_slots = [(CORE, yes), (ACROSS, outer)] + [(slot, exists) for slot, _, exists, _, _ in end_sends]
        for slot, exists in early_slots:
            @pl.when(exists)
            def _():
                sent(stage.at[slot], landed.at[CORE], t_send.at[slot])

    def drain():
        late_slots = [(INNER, outer)]
        late_slots += [(slot, exists) for slot, _, _, exists, _, _ in far_sends]
        late_slots += [(slot, exists) for slot, _, _, exists, _, _, _ in relays]
        late_slots += [(slot, exists) for slot, _, exists, _, _ in end_relays]
        for slot, exists in late_slots:
            @pl.when(exists)
            def _():
                sent(stage.at[slot], landed.at[CORE], t_send.at[slot])

    def wait_landed(r, part):
        for slot, exists in landings:
            @pl.when(exists)
            def _():
                part_copy(CORE, slot, r, part, core_peer).wait_recv()

    last = len(relayed) - 1
    for r in range(last):
        first, size = relayed[r]
        wait_landed(r, None)
        lax.fori_loop(first, first + size, late, 0)
        if r == 0:
            drain_early()
    first, size = relayed[last]
    wait_landed(last, 0)
    weighed = [weigh(h, span((h, 1))) for h in range(first, first + size)]
    drain()
    wait_landed(last, 1)
    for h, ready in zip(range(first, first + size), weighed):
        finish(span((h, 1)), *ready)


def solution(mesh):
    n = mesh.shape["frame"]

    def body(queries, key_heads, value_heads, tile_lists):
        rows, channels = queries.shape
        heads = channels // HD
        tiles = rows // TILE
        levels = tile_lists.shape[1] // 2
        far = max(levels - 4, 0)
        lists = 5 + 2 * far
        bf16, f32 = jnp.bfloat16, jnp.float32
        hbm = pl.BlockSpec(memory_space=pltpu.HBM)
        dma = pltpu.SemaphoreType.DMA
        out_slots, in_slots = OUT_NEAR + 2 * far, NEAR + 2 * far
        return pl.pallas_call(
            functools.partial(kernel, n, levels, heads),
            out_shape=pltpu.VMEM((rows, channels), bf16),
            in_specs=[hbm, hbm, hbm, pl.BlockSpec(memory_space=pltpu.SMEM)],
            out_specs=pl.BlockSpec(memory_space=pltpu.VMEM),
            scratch_shapes=[
                pltpu.VMEM((rows, channels), bf16),
                pltpu.VMEM((tiles, TILE, channels), bf16),
                pltpu.VMEM((tiles, TILE, channels), bf16),
                pltpu.VMEM((2, 2, tiles, TILE, channels), bf16),
                pltpu.VMEM((2, tiles, TILE, channels), bf16),
                pltpu.VMEM((out_slots, 2, TILE, channels), bf16),
                pltpu.VMEM((in_slots, 2, TILE, channels), bf16),
                pltpu.SMEM((lists, 1, 2 * levels), jnp.int32),
                pltpu.VMEM((heads, rows, HD), f32),
                pltpu.VMEM((heads, rows, HD), f32),
                pltpu.VMEM((heads, rows, HD), f32),
                dma((2, 2)),
                dma((2, len(WHOLE_PIECES))),
                dma((2,)),
                dma((len(WHOLE_PIECES),)),
                dma((out_slots,)),
                dma((in_slots, len(RELAY_PIECES) + 1)),
                dma((lists,)),
                dma((lists,)),
                dma((3,)),
            ],
            compiler_params=pltpu.CompilerParams(
                collective_id=0, has_side_effects=True, vmem_limit_bytes=61 << 20
            ),
        )(
            queries,
            key_heads.reshape(tiles, TILE, channels),
            value_heads.reshape(tiles, TILE, channels),
            tile_lists,
        )
    in_specs = (
        P(("groups", "frame"), None),
        P(("groups", "frame"), None),
        P(("groups", "frame"), None),
        P("frame", None),
    )
    return jax.shard_map(
        body, mesh=mesh, in_specs=in_specs, out_specs=P(("groups", "frame"), None), check_vma=False
    )
```

```python
import functools
import math

import jax
import jax.numpy as jnp
from jax import lax
from jax.experimental import pallas as pl
from jax.experimental.pallas import tpu as pltpu
from jax.sharding import PartitionSpec as P

HD = 128
TILE = 128
MESH = pl.DeviceIdType.MESH
ABSENT = -1e30

WHOLE_PIECES = (4, 4, 4)
RELAY_PIECES = (4, 4, 2, 2)

CORE, MIRROR, RELAYED, BELOW8, ABOVE8 = range(5)
NEAR = 5
ACROSS, INNER, TO_LOW_END, TO_HIGH_END, END_DOWN, END_UP = range(NEAR, NEAR + 6)
OUT_NEAR = NEAR + 6


def pieces_of(sizes, heads):
    unit = heads // sum(sizes)
    pieces, first = [], 0
    for size in sizes:
        pieces.append((first, size * unit))
        first += size * unit
    return pieces


def kernel(n, levels, heads, q_hbm, k_hbm, v_hbm, own_list, out_ref,
           q_v, k_v, v_v, whole, inside, stage, landed, lists_s, top, total, acc,
           w_send, w_recv, i_send, i_recv, t_send, t_recv, l_send, l_recv, in_sem):
    me = lax.axis_index("frame")
    quarter = me % 4
    x = quarter // 2
    core = me % 2
    core_peer = me + 1 - 2 * core
    across = me + 2 - 4 * x
    mirror = me + 3 - 2 * quarter
    inner = (quarter == 1) | (quarter == 2)
    outer = (quarter == 0) | (quarter == 3)
    has_low, has_high = me >= 4, me + 4 < n
    low_corner, high_corner = quarter == 0, quarter == 3
    to_low_end, to_high_end = has_low & (me < 8), has_high & (me + 8 >= n)
    chosen_down, chosen_up = to_low_end & ~low_corner, to_high_end & ~high_corner
    low_chosen, high_chosen = (me + 4 >= n) & ~high_corner, (me < 4) & ~low_corner
    tiles = k_v.shape[0]
    far = [1 << level for level in range(4, levels)]
    yes = me >= 0
    wholes = pieces_of(WHOLE_PIECES, heads)
    relayed = pieces_of(RELAY_PIECES, heads)

    partners = [
        (core_peer, yes, 0, 0),
        (across, yes, 1, 1),
        (mirror, yes, 2, 2),
        (me - 4, has_low, 3, 4),
        (me + 4, has_high, 4, 3),
    ]
    for j, d in enumerate(far):
        partners.append((me - d, me >= d, 5 + 2 * j, 6 + 2 * j))
        partners.append((me + d, me + d < n, 6 + 2 * j, 5 + 2 * j))

    barrier = pltpu.get_barrier_semaphore()
    for device, exists, _, _ in partners:
        @pl.when(exists)
        def _():
            pl.semaphore_signal(barrier, inc=1, device_id={"frame": device}, device_id_type=MESH)
    loads = [
        pltpu.make_async_copy(source, target, in_sem.at[i])
        for i, (source, target) in enumerate(((k_hbm, k_v), (v_hbm, v_v), (q_hbm, q_v)))
    ]
    for load in loads:
        load.start()
    pl.semaphore_wait(barrier, sum(jnp.where(exists, 1, 0) for _, exists, _, _ in partners))

    def span(piece):
        return pl.ds(piece[0] * HD, piece[1] * HD)

    def whole_copy(side, i, kv):
        columns = span(wholes[i])
        return pltpu.make_async_remote_copy(
            src_ref=(k_hbm, v_hbm)[kv].at[:, :, columns], dst_ref=whole.at[side, kv, :, :, columns],
            send_sem=w_send.at[side, kv], recv_sem=w_recv.at[side, i],
            device_id={"frame": me + 4 if side == 0 else me - 4}, device_id_type=MESH)

    def inner_copy(i, kv):
        columns = span(wholes[i])
        return pltpu.make_async_remote_copy(
            src_ref=(k_hbm, v_hbm)[kv].at[:, :, columns], dst_ref=inside.at[kv, :, :, columns],
            send_sem=i_send.at[kv], recv_sem=i_recv.at[i],
            device_id={"frame": across}, device_id_type=MESH)

    def across_copy(i):
        columns = span(wholes[i])
        return pltpu.make_async_remote_copy(
            src_ref=stage.at[ACROSS, :, :, columns], dst_ref=inside.at[:, 0, :, columns],
            send_sem=t_send.at[ACROSS], recv_sem=i_recv.at[i],
            device_id={"frame": across}, device_id_type=MESH)

    def end_copy(slot, side, i):
        columns = span(wholes[i])
        return pltpu.make_async_remote_copy(
            src_ref=stage.at[slot, :, :, columns], dst_ref=whole.at[side, :, 0, :, columns],
            send_sem=t_send.at[slot], recv_sem=w_recv.at[side, i],
            device_id={"frame": me + 4 if side == 0 else me - 4}, device_id_type=MESH)

    def list_copy(device, here, there):
        return pltpu.make_async_remote_copy(
            src_ref=own_list, dst_ref=lists_s.at[there],
            send_sem=l_send.at[here], recv_sem=l_recv.at[there],
            device_id={"frame": device}, device_id_type=MESH)

    def tile_copy(slot, there, pieces, i, device):
        columns = span(pieces[i])
        return pltpu.make_async_remote_copy(
            src_ref=stage.at[slot, :, :, columns], dst_ref=landed.at[there, :, :, columns],
            send_sem=t_send.at[slot], recv_sem=t_recv.at[there, i],
            device_id={"frame": device}, device_id_type=MESH)

    def parts_of(r):
        return (0, 1) if r == len(relayed) - 1 else (None,)

    def part_copy(slot, there, r, part, device):
        columns = span(relayed[r])
        at = slice(None) if part is None else part
        i = r + (part or 0)
        return pltpu.make_async_remote_copy(
            src_ref=stage.at[slot, at, :, columns], dst_ref=landed.at[there, at, :, columns],
            send_sem=t_send.at[slot], recv_sem=t_recv.at[there, i],
            device_id={"frame": device}, device_id_type=MESH)

    sides = (
        (has_high & ~chosen_up, has_low & ~low_chosen, has_low & low_chosen),
        (has_low & ~chosen_down, has_high & ~high_chosen, has_high & high_chosen),
    )
    end_sends = [(TO_HIGH_END, 0, chosen_up, 4, 2), (TO_LOW_END, 1, chosen_down, 3, levels + 2)]

    def send_lists(chosen_partners):
        for device, exists, here, there in chosen_partners:
            @pl.when(exists)
            def _():
                list_copy(device, here, there).start()

    def send_wholes(i):
        for side in range(2):
            @pl.when(sides[side][0])
            def _():
                for kv in range(2):
                    whole_copy(side, i, kv).start()

    def send_inner(i):
        @pl.when(inner)
        def _():
            for kv in range(2):
                inner_copy(i, kv).start()

    send_lists(partners[1:3])
    send_inner(0)
    send_lists(partners[3:])
    send_wholes(0)
    send_lists(partners[:1])
    for i in range(1, len(wholes)):
        send_inner(i)
        send_wholes(i)

    landings = [
        (MIRROR, inner | ((quarter == 0) & has_low) | ((quarter == 3) & has_high)),
        (RELAYED, ((x == 0) & has_low) | ((x == 1) & has_high)),
        (BELOW8, me >= 8),
        (ABOVE8, me + 8 < n),
    ]
    for j, d in enumerate(far):
        landings.append((NEAR + 2 * j, me >= d))
        landings.append((NEAR + 2 * j + 1, me + d < n))
    for slot, exists in landings:
        @pl.when(jnp.logical_not(exists))
        def _():
            landed[slot] = jnp.zeros(landed.shape[1:], landed.dtype)
    for side in range(2):
        @pl.when(jnp.logical_not((has_low, has_high)[side]))
        def _():
            whole[side] = jnp.zeros(whole.shape[1:], whole.dtype)

    for load in loads:
        load.wait()
    for _, exists, here, _ in partners:
        @pl.when(exists)
        def _():
            list_copy(core_peer, here, here).wait_recv()

    def stage_own(slot, columns, wanted):
        stage[slot, 0, :, columns] = k_v[wanted, :, columns]
        stage[slot, 1, :, columns] = v_v[wanted, :, columns]

    far_sends = []
    for j, d in enumerate(far):
        far_sends.append((OUT_NEAR + 2 * j, NEAR + 2 * j, me + d, me + d < n, 6 + 2 * j, 4 + j))
        far_sends.append((OUT_NEAR + 2 * j + 1, NEAR + 2 * j + 1, me - d, me >= d, 5 + 2 * j, levels + 4 + j))

    for i, piece in enumerate(wholes):
        for slot, side, exists, here, entry in end_sends:
            @pl.when(exists)
            def _():
                stage_own(slot, span(piece), lists_s[here, 0, entry])
                end_copy(slot, side, i).start()
        @pl.when(outer)
        def _():
            stage_own(ACROSS, span(piece), lists_s[1, 0, 1 + levels * x])
            across_copy(i).start()
        stage_own(CORE, span(piece), lists_s[0, 0, levels * core])
        tile_copy(CORE, CORE, wholes, i, core_peer).start()
    for slot, there, device, exists, here, entry in far_sends:
        @pl.when(exists)
        def _():
            for i, piece in enumerate(relayed):
                stage_own(slot, span(piece), lists_s[here, 0, entry])
                for part in parts_of(i):
                    part_copy(slot, there, i, part, device).start()

    factor = math.log2(math.e) / math.sqrt(HD)

    def bias_of(parts):
        return jnp.concatenate(
            [jnp.full((1, size), jnp.where(exists, 0.0, ABSENT), jnp.float32) for size, exists in parts], axis=1)

    near_bias = bias_of([((tiles + 2) * TILE, yes), (TILE, has_low), (TILE, has_high)])
    late_bias = bias_of([(TILE, exists) for _, exists in landings])

    relays = [
        (BELOW8, BELOW8, me + 4, has_low & has_high, 0, 4, 3),
        (ABOVE8, ABOVE8, me - 4, has_low & has_high, 1, 3, levels + 3),
        (RELAYED, RELAYED, across, (x == 0) & has_high & (low_corner | ((me >= 4) & (me + 8 < n))), 1, 1, levels + 1),
        (RELAYED, RELAYED, across, (x == 1) & has_low & (high_corner | ((me + 4 < n) & (me >= 8))), 0, 1, 1),
        (MIRROR, MIRROR, mirror, (quarter == 0) & has_high, 1, 2, levels),
        (MIRROR, MIRROR, mirror, (quarter == 3) & has_low, 0, 2, 0),
    ]
    relay_down = has_low & high_corner & (to_low_end | (me + 4 >= n))
    relay_up = has_high & low_corner & (to_high_end | (me < 4))
    end_relays = [
        (END_DOWN, me - 4, relay_down, 3, levels + 1),
        (END_UP, me + 4, relay_up, 4, 1),
    ]
    relays_to_end = relay_down | relay_up

    def chosen(block_of, wanted):
        block = block_of(0)
        for tile in range(1, tiles):
            block = jnp.where(wanted == tile, block_of(tile), block)
        return block

    low = jnp.where(low_chosen, 0, own_list[0, 2])
    high = jnp.where(high_chosen, 0, own_list[0, levels + 2])
    beside = jnp.where(outer, own_list[0, 1 + levels * (1 - x)], 0)

    def early(h, carry):
        columns = pl.ds(pl.multiple_of(h * HD, HD), HD)

        def gather(kv):
            own = (k_v, v_v)[kv]
            return jnp.concatenate(
                [own[tile, :, columns] for tile in range(tiles)] + [
                    landed[CORE, kv, :, columns],
                    chosen(lambda tile: inside[kv, tile, :, columns], beside),
                    chosen(lambda tile: whole[0, kv, tile, :, columns], low),
                    chosen(lambda tile: whole[1, kv, tile, :, columns], high)], axis=0)
        scores = lax.dot_general(
            q_v[:, columns], gather(0), (((1,), (1,)), ((), ())), preferred_element_type=jnp.float32)
        scores = scores + near_bias
        peak = jnp.max(scores, axis=1, keepdims=True)
        raised = jnp.exp2((scores - peak) * factor)
        added = jnp.sum(raised, axis=1, keepdims=True)
        acc[h] = jnp.dot(raised.astype(jnp.bfloat16), gather(1), preferred_element_type=jnp.float32)
        top[h] = jnp.broadcast_to(peak, (peak.shape[0], HD))
        total[h] = jnp.broadcast_to(added, (peak.shape[0], HD))
        return carry

    def arrived(target, semaphore):
        pltpu.make_async_remote_copy(
            src_ref=target, dst_ref=target, send_sem=semaphore, recv_sem=semaphore,
            device_id={"frame": core_peer}, device_id_type=MESH).wait_recv()

    for w, (first, size) in enumerate(wholes):
        inside_piece = [r for r, piece in enumerate(relayed) if first <= piece[0] < first + size]
        for side in range(2):
            @pl.when(sides[side][1])
            def _():
                arrived(whole.at[side, :, :, :, span(wholes[w])], w_recv.at[side, w])
            @pl.when(sides[side][2])
            def _():
                end_copy(TO_LOW_END, side, w).wait_recv()

        for slot, device, exists, here, entry in end_relays:
            @pl.when(exists)
            def _():
                arrived(inside.at[:, :, :, span(wholes[w])], i_recv.at[w])
                wanted = lists_s[here, 0, entry]
                for r in inside_piece:
                    columns = span(relayed[r])
                    for kv in range(2):
                        stage[slot, kv, :, columns] = chosen(lambda tile: inside[kv, tile, :, columns], wanted)
                    for part in parts_of(r):
                        part_copy(slot, RELAYED, r, part, device).start()

        for r in inside_piece:
            columns = span(relayed[r])
            for slot, there, device, exists, side, here, entry in relays:
                @pl.when(exists)
                def _():
                    wanted = lists_s[here, 0, entry]
                    for kv in range(2):
                        stage[slot, kv, :, columns] = chosen(lambda tile: whole[side, kv, tile, :, columns], wanted)
            for part in parts_of(r):
                for slot, there, device, exists, _, _, _ in relays:
                    @pl.when(exists)
                    def _():
                        part_copy(slot, there, r, part, device).start()

        @pl.when(outer & ~relays_to_end)
        def _():
            arrived(inside.at[:, :, :, span(wholes[w])], i_recv.at[w])

        @pl.when(outer)
        def _():
            wanted = lists_s[0, 0, levels * (1 - core)]
            for r in inside_piece:
                columns = span(relayed[r])
                for kv in range(2):
                    stage[INNER, kv, :, columns] = chosen(lambda tile: inside[kv, tile, :, columns], wanted)
                for part in parts_of(r):
                    part_copy(INNER, MIRROR, r, part, core_peer).start()

        @pl.when(inner)
        def _():
            across_copy(w).wait_recv()

        tile_copy(CORE, CORE, wholes, w, core_peer).wait_recv()
        lax.fori_loop(first, first + size, early, 0)

    def landed_at(kv, columns):
        return jnp.concatenate([landed[slot, kv, :, columns] for slot, _ in landings], axis=0)

    def weigh(h, columns):
        scores = lax.dot_general(
            q_v[:, columns], landed_at(0, columns), (((1,), (1,)), ((), ())), preferred_element_type=jnp.float32)
        scores = scores + late_bias
        old = top[h][:, :1]
        peak = jnp.maximum(old, jnp.max(scores, axis=1, keepdims=True))
        raised = jnp.exp2((scores - peak) * factor)
        fade = jnp.exp2((old - peak) * factor)
        added = jnp.sum(raised, axis=1, keepdims=True) + fade * total[h][:, :1]
        return raised.astype(jnp.bfloat16), fade * acc[h], added

    def finish(columns, raised, faded, added):
        mixed = jnp.dot(raised, landed_at(1, columns), preferred_element_type=jnp.float32) + faded
        out_ref[:, columns] = (mixed / added).astype(out_ref.dtype)

    def late(h, carry):
        columns = pl.ds(pl.multiple_of(h * HD, HD), HD)
        finish(columns, *weigh(h, columns))
        return carry

    def sent(source, target, semaphore):
        pltpu.make_async_remote_copy(
            src_ref=source, dst_ref=target, send_sem=semaphore, recv_sem=semaphore,
            device_id={"frame": core_peer}, device_id_type=MESH).wait_send()

    def drain_early():
        for _, exists, here, _ in partners:
            @pl.when(exists)
            def _():
                list_copy(core_peer, here, here).wait_send()
        for kv in range(2):
            @pl.when(inner)
            def _():
                sent((k_hbm, v_hbm)[kv], inside.at[kv], i_send.at[kv])
            for side in range(2):
                @pl.when(sides[side][0])
                def _():
                    sent((k_hbm, v_hbm)[kv], whole.at[side, kv], w_send.at[side, kv])
        early_slots = [(CORE, yes), (ACROSS, outer)] + [(slot, exists) for slot, _, exists, _, _ in end_sends]
        for slot, exists in early_slots:
            @pl.when(exists)
            def _():
                sent(stage.at[slot], landed.at[CORE], t_send.at[slot])

    def drain():
        late_slots = [(INNER, outer)]
        late_slots += [(slot, exists) for slot, _, _, exists, _, _ in far_sends]
        late_slots += [(slot, exists) for slot, _, _, exists, _, _, _ in relays]
        late_slots += [(slot, exists) for slot, _, exists, _, _ in end_relays]
        for slot, exists in late_slots:
            @pl.when(exists)
            def _():
                sent(stage.at[slot], landed.at[CORE], t_send.at[slot])

    def wait_landed(r, part):
        for slot, exists in landings:
            @pl.when(exists)
            def _():
                part_copy(CORE, slot, r, part, core_peer).wait_recv()

    last = len(relayed) - 1
    for r in range(last):
        first, size = relayed[r]
        wait_landed(r, None)
        lax.fori_loop(first, first + size, late, 0)
        if r == 0:
            drain_early()
    first, size = relayed[last]
    wait_landed(last, 0)
    weighed = [weigh(h, span((h, 1))) for h in range(first, first + size)]
    drain()
    wait_landed(last, 1)
    for h, ready in zip(range(first, first + size), weighed):
        finish(span((h, 1)), *ready)


def write_out(in_ref, out_ref, sem):
    copy = pltpu.make_async_copy(in_ref, out_ref, sem)
    copy.start()
    copy.wait()


def solution(mesh):
    n = mesh.shape["frame"]

    def body(queries, key_heads, value_heads, tile_lists):
        rows, channels = queries.shape
        heads = channels // HD
        tiles = rows // TILE
        levels = tile_lists.shape[1] // 2
        far = max(levels - 4, 0)
        lists = 5 + 2 * far
        bf16, f32 = jnp.bfloat16, jnp.float32
        hbm = pl.BlockSpec(memory_space=pltpu.HBM)
        dma = pltpu.SemaphoreType.DMA
        out_slots, in_slots = OUT_NEAR + 2 * far, NEAR + 2 * far
        result = pl.pallas_call(
            functools.partial(kernel, n, levels, heads),
            out_shape=pltpu.VMEM((rows, channels), bf16),
            in_specs=[hbm, hbm, hbm, pl.BlockSpec(memory_space=pltpu.SMEM)],
            out_specs=pl.BlockSpec(memory_space=pltpu.VMEM),
            scratch_shapes=[
                pltpu.VMEM((rows, channels), bf16),
                pltpu.VMEM((tiles, TILE, channels), bf16),
                pltpu.VMEM((tiles, TILE, channels), bf16),
                pltpu.VMEM((2, 2, tiles, TILE, channels), bf16),
                pltpu.VMEM((2, tiles, TILE, channels), bf16),
                pltpu.VMEM((out_slots, 2, TILE, channels), bf16),
                pltpu.VMEM((in_slots, 2, TILE, channels), bf16),
                pltpu.SMEM((lists, 1, 2 * levels), jnp.int32),
                pltpu.VMEM((heads, rows, HD), f32),
                pltpu.VMEM((heads, rows, HD), f32),
                pltpu.VMEM((heads, rows, HD), f32),
                dma((2, 2)),
                dma((2, len(WHOLE_PIECES))),
                dma((2,)),
                dma((len(WHOLE_PIECES),)),
                dma((out_slots,)),
                dma((in_slots, len(RELAY_PIECES) + 1)),
                dma((lists,)),
                dma((lists,)),
                dma((3,)),
            ],
            compiler_params=pltpu.CompilerParams(
                collective_id=0, has_side_effects=True, vmem_limit_bytes=61 << 20
            ),
        )(
            queries,
            key_heads.reshape(tiles, TILE, channels),
            value_heads.reshape(tiles, TILE, channels),
            tile_lists,
        )
        return pl.pallas_call(
            write_out,
            out_shape=jax.ShapeDtypeStruct((rows, channels), bf16),
            in_specs=[pl.BlockSpec(memory_space=pltpu.VMEM)],
            out_specs=pl.BlockSpec(memory_space=pl.ANY),
            scratch_shapes=[dma],
            compiler_params=pltpu.CompilerParams(vmem_limit_bytes=4 << 20),
        )(result)

    in_specs = (
        P(("groups", "frame"), None),
        P(("groups", "frame"), None),
        P(("groups", "frame"), None),
        P("frame", None),
    )
    return jax.shard_map(
        body, mesh=mesh, in_specs=in_specs, out_specs=P(("groups", "frame"), None), check_vma=False
    )
```

```python
import functools
import math

import jax
import jax.numpy as jnp
from jax import lax
from jax.experimental import pallas as pl
from jax.experimental.pallas import tpu as pltpu
from jax.sharding import PartitionSpec as P

HD = 128
TILE = 128
MESH = pl.DeviceIdType.MESH
ABSENT = -1e30

WHOLE_PIECES = (4, 4, 4)
RELAY_PIECES = (4, 4, 2, 2)

CORE, MIRROR, RELAYED, BELOW8, ABOVE8 = range(5)
NEAR = 5
ACROSS, INNER, TO_LOW_END, TO_HIGH_END, END_DOWN, END_UP = range(NEAR, NEAR + 6)
OUT_NEAR = NEAR + 6


def pieces_of(sizes, heads):
    unit = heads // sum(sizes)
    pieces, first = [], 0
    for size in sizes:
        pieces.append((first, size * unit))
        first += size * unit
    return pieces


def kernel(n, levels, heads, q_hbm, k_hbm, v_hbm, own_list, out_ref,
           q_v, k_v, v_v, whole, inside, stage, landed, lists_s, top, total, acc,
           w_send, w_recv, i_send, i_recv, t_send, t_recv, l_send, l_recv, in_sem):
    me = lax.axis_index("frame")
    quarter = me % 4
    x = quarter // 2
    core = me % 2
    core_peer = me + 1 - 2 * core
    across = me + 2 - 4 * x
    mirror = me + 3 - 2 * quarter
    inner = (quarter == 1) | (quarter == 2)
    outer = (quarter == 0) | (quarter == 3)
    has_low, has_high = me >= 4, me + 4 < n
    low_corner, high_corner = quarter == 0, quarter == 3
    to_low_end, to_high_end = has_low & (me < 8), has_high & (me + 8 >= n)
    chosen_down, chosen_up = to_low_end & ~low_corner, to_high_end & ~high_corner
    low_chosen, high_chosen = (me + 4 >= n) & ~high_corner, (me < 4) & ~low_corner
    tiles = k_v.shape[0]
    far = [1 << level for level in range(4, levels)]
    yes = me >= 0
    wholes = pieces_of(WHOLE_PIECES, heads)
    relayed = pieces_of(RELAY_PIECES, heads)

    partners = [
        (core_peer, yes, 0, 0),
        (across, yes, 1, 1),
        (mirror, yes, 2, 2),
        (me - 4, has_low, 3, 4),
        (me + 4, has_high, 4, 3),
    ]
    for j, d in enumerate(far):
        partners.append((me - d, me >= d, 5 + 2 * j, 6 + 2 * j))
        partners.append((me + d, me + d < n, 6 + 2 * j, 5 + 2 * j))

    def when(exists):
        return (lambda run: run()) if exists is yes else pl.when(exists)

    barrier = pltpu.get_barrier_semaphore()
    for device, exists, _, _ in partners:
        @when(exists)
        def _():
            pl.semaphore_signal(barrier, inc=1, device_id={"frame": device}, device_id_type=MESH)
    loads = [
        pltpu.make_async_copy(source, target, in_sem.at[i])
        for i, (source, target) in enumerate(((k_hbm, k_v), (v_hbm, v_v), (q_hbm, q_v)))
    ]
    for load in loads:
        load.start()
    pl.semaphore_wait(barrier, sum(jnp.where(exists, 1, 0) for _, exists, _, _ in partners))

    def span(piece):
        return pl.ds(piece[0] * HD, piece[1] * HD)

    def whole_copy(side, i, kv):
        columns = span(wholes[i])
        return pltpu.make_async_remote_copy(
            src_ref=(k_hbm, v_hbm)[kv].at[:, :, columns], dst_ref=whole.at[side, kv, :, :, columns],
            send_sem=w_send.at[side, kv], recv_sem=w_recv.at[side, i],
            device_id={"frame": me + 4 if side == 0 else me - 4}, device_id_type=MESH)

    def inner_copy(i, kv):
        columns = span(wholes[i])
        return pltpu.make_async_remote_copy(
            src_ref=(k_hbm, v_hbm)[kv].at[:, :, columns], dst_ref=inside.at[kv, :, :, columns],
            send_sem=i_send.at[kv], recv_sem=i_recv.at[i],
            device_id={"frame": across}, device_id_type=MESH)

    def across_copy(i):
        columns = span(wholes[i])
        return pltpu.make_async_remote_copy(
            src_ref=stage.at[ACROSS, :, :, columns], dst_ref=inside.at[:, 0, :, columns],
            send_sem=t_send.at[ACROSS], recv_sem=i_recv.at[i],
            device_id={"frame": across}, device_id_type=MESH)

    def end_copy(slot, side, i):
        columns = span(wholes[i])
        return pltpu.make_async_remote_copy(
            src_ref=stage.at[slot, :, :, columns], dst_ref=whole.at[side, :, 0, :, columns],
            send_sem=t_send.at[slot], recv_sem=w_recv.at[side, i],
            device_id={"frame": me + 4 if side == 0 else me - 4}, device_id_type=MESH)

    def list_copy(device, here, there):
        return pltpu.make_async_remote_copy(
            src_ref=own_list, dst_ref=lists_s.at[there],
            send_sem=l_send.at[here], recv_sem=l_recv.at[there],
            device_id={"frame": device}, device_id_type=MESH)

    def tile_copy(slot, there, pieces, i, device):
        columns = span(pieces[i])
        return pltpu.make_async_remote_copy(
            src_ref=stage.at[slot, :, :, columns], dst_ref=landed.at[there, :, :, columns],
            send_sem=t_send.at[slot], recv_sem=t_recv.at[there, i],
            device_id={"frame": device}, device_id_type=MESH)

    def parts_of(r):
        return (0, 1) if r == len(relayed) - 1 else (None,)

    def part_copy(slot, there, r, part, device):
        columns = span(relayed[r])
        at = slice(None) if part is None else part
        i = r + (part or 0)
        return pltpu.make_async_remote_copy(
            src_ref=stage.at[slot, at, :, columns], dst_ref=landed.at[there, at, :, columns],
            send_sem=t_send.at[slot], recv_sem=t_recv.at[there, i],
            device_id={"frame": device}, device_id_type=MESH)

    sides = (
        (has_high & ~chosen_up, has_low & ~low_chosen, has_low & low_chosen),
        (has_low & ~chosen_down, has_high & ~high_chosen, has_high & high_chosen),
    )
    end_sends = [(TO_HIGH_END, 0, chosen_up, 4, 2), (TO_LOW_END, 1, chosen_down, 3, levels + 2)]

    def send_lists(chosen_partners):
        for device, exists, here, there in chosen_partners:
            @when(exists)
            def _():
                list_copy(device, here, there).start()

    def send_wholes(i):
        for side in range(2):
            @pl.when(sides[side][0])
            def _():
                for kv in range(2):
                    whole_copy(side, i, kv).start()

    def send_inner(i):
        @pl.when(inner)
        def _():
            for kv in range(2):
                inner_copy(i, kv).start()

    send_lists(partners[1:3])
    send_inner(0)
    send_lists(partners[3:])
    send_wholes(0)
    send_lists(partners[:1])
    for i in range(1, len(wholes)):
        send_inner(i)
        send_wholes(i)

    landings = [
        (MIRROR, inner | ((quarter == 0) & has_low) | ((quarter == 3) & has_high)),
        (RELAYED, ((x == 0) & has_low) | ((x == 1) & has_high)),
        (BELOW8, me >= 8),
        (ABOVE8, me + 8 < n),
    ]
    for j, d in enumerate(far):
        landings.append((NEAR + 2 * j, me >= d))
        landings.append((NEAR + 2 * j + 1, me + d < n))
    for slot, exists in landings:
        @pl.when(jnp.logical_not(exists))
        def _():
            landed[slot] = jnp.zeros(landed.shape[1:], landed.dtype)
    for side in range(2):
        @pl.when(jnp.logical_not((has_low, has_high)[side]))
        def _():
            whole[side] = jnp.zeros(whole.shape[1:], whole.dtype)

    for load in loads:
        load.wait()
    for _, exists, here, _ in partners:
        @when(exists)
        def _():
            list_copy(core_peer, here, here).wait_recv()

    def stage_own(slot, columns, wanted):
        stage[slot, 0, :, columns] = k_v[wanted, :, columns]
        stage[slot, 1, :, columns] = v_v[wanted, :, columns]

    far_sends = []
    for j, d in enumerate(far):
        far_sends.append((OUT_NEAR + 2 * j, NEAR + 2 * j, me + d, me + d < n, 6 + 2 * j, 4 + j))
        far_sends.append((OUT_NEAR + 2 * j + 1, NEAR + 2 * j + 1, me - d, me >= d, 5 + 2 * j, levels + 4 + j))

    for i, piece in enumerate(wholes):
        for slot, side, exists, here, entry in end_sends:
            @when(exists)
            def _():
                stage_own(slot, span(piece), lists_s[here, 0, entry])
                end_copy(slot, side, i).start()
        @pl.when(outer)
        def _():
            stage_own(ACROSS, span(piece), lists_s[1, 0, 1 + levels * x])
            across_copy(i).start()
        stage_own(CORE, span(piece), lists_s[0, 0, levels * core])
        tile_copy(CORE, CORE, wholes, i, core_peer).start()
    for slot, there, device, exists, here, entry in far_sends:
        @when(exists)
        def _():
            for i, piece in enumerate(relayed):
                stage_own(slot, span(piece), lists_s[here, 0, entry])
                for part in parts_of(i):
                    part_copy(slot, there, i, part, device).start()

    factor = math.log2(math.e) / math.sqrt(HD)

    def bias_of(parts):
        return jnp.concatenate(
            [jnp.full((1, size), jnp.where(exists, 0.0, ABSENT), jnp.float32) for size, exists in parts], axis=1)

    near_bias = bias_of([((tiles + 2) * TILE, yes), (TILE, has_low), (TILE, has_high)])
    late_bias = bias_of([(TILE, exists) for _, exists in landings])

    relays = [
        (MIRROR, MIRROR, mirror, (quarter == 0) & has_high, 1, 2, levels),
        (MIRROR, MIRROR, mirror, (quarter == 3) & has_low, 0, 2, 0),
        (RELAYED, RELAYED, across, (x == 0) & has_high & (low_corner | ((me >= 4) & (me + 8 < n))), 1, 1, levels + 1),
        (RELAYED, RELAYED, across, (x == 1) & has_low & (high_corner | ((me + 4 < n) & (me >= 8))), 0, 1, 1),
        (BELOW8, BELOW8, me + 4, has_low & has_high, 0, 4, 3),
        (ABOVE8, ABOVE8, me - 4, has_low & has_high, 1, 3, levels + 3),
    ]
    relay_down = has_low & high_corner & (to_low_end | (me + 4 >= n))
    relay_up = has_high & low_corner & (to_high_end | (me < 4))
    end_relays = [
        (END_DOWN, me - 4, relay_down, 3, levels + 1),
        (END_UP, me + 4, relay_up, 4, 1),
    ]
    relays_to_end = relay_down | relay_up

    def chosen(block_of, wanted):
        block = block_of(0)
        for tile in range(1, tiles):
            block = jnp.where(wanted == tile, block_of(tile), block)
        return block

    low = jnp.where(low_chosen, 0, own_list[0, 2])
    high = jnp.where(high_chosen, 0, own_list[0, levels + 2])
    beside = jnp.where(outer, own_list[0, 1 + levels * (1 - x)], 0)

    def early(h, carry):
        columns = pl.ds(pl.multiple_of(h * HD, HD), HD)

        def gather(kv):
            own = (k_v, v_v)[kv]
            return jnp.concatenate(
                [own[tile, :, columns] for tile in range(tiles)] + [
                    landed[CORE, kv, :, columns],
                    chosen(lambda tile: inside[kv, tile, :, columns], beside),
                    chosen(lambda tile: whole[0, kv, tile, :, columns], low),
                    chosen(lambda tile: whole[1, kv, tile, :, columns], high)], axis=0)
        scores = lax.dot_general(
            q_v[:, columns], gather(0), (((1,), (1,)), ((), ())), preferred_element_type=jnp.float32)
        scores = scores + near_bias
        peak = jnp.max(scores, axis=1, keepdims=True)
        raised = jnp.exp2((scores - peak) * factor)
        added = jnp.sum(raised, axis=1, keepdims=True)
        acc[h] = jnp.dot(raised.astype(jnp.bfloat16), gather(1), preferred_element_type=jnp.float32)
        top[h] = jnp.broadcast_to(peak, (peak.shape[0], HD))
        total[h] = jnp.broadcast_to(added, (peak.shape[0], HD))
        return carry

    def arrived(target, semaphore):
        pltpu.make_async_remote_copy(
            src_ref=target, dst_ref=target, send_sem=semaphore, recv_sem=semaphore,
            device_id={"frame": core_peer}, device_id_type=MESH).wait_recv()

    for w, (first, size) in enumerate(wholes):
        inside_piece = [r for r, piece in enumerate(relayed) if first <= piece[0] < first + size]
        for side in range(2):
            @pl.when(sides[side][1])
            def _():
                arrived(whole.at[side, :, :, :, span(wholes[w])], w_recv.at[side, w])
            @pl.when(sides[side][2])
            def _():
                end_copy(TO_LOW_END, side, w).wait_recv()

        for slot, device, exists, here, entry in end_relays:
            @when(exists)
            def _():
                arrived(inside.at[:, :, :, span(wholes[w])], i_recv.at[w])
                wanted = lists_s[here, 0, entry]
                for r in inside_piece:
                    columns = span(relayed[r])
                    for kv in range(2):
                        stage[slot, kv, :, columns] = chosen(lambda tile: inside[kv, tile, :, columns], wanted)
                    for part in parts_of(r):
                        part_copy(slot, RELAYED, r, part, device).start()

        for r in inside_piece:
            columns = span(relayed[r])
            for slot, there, device, exists, side, here, entry in relays:
                @when(exists)
                def _():
                    wanted = lists_s[here, 0, entry]
                    for kv in range(2):
                        stage[slot, kv, :, columns] = chosen(lambda tile: whole[side, kv, tile, :, columns], wanted)
            for part in parts_of(r):
                for slot, there, device, exists, _, _, _ in relays:
                    @when(exists)
                    def _():
                        part_copy(slot, there, r, part, device).start()

        @pl.when(outer & ~relays_to_end)
        def _():
            arrived(inside.at[:, :, :, span(wholes[w])], i_recv.at[w])

        @pl.when(outer)
        def _():
            wanted = lists_s[0, 0, levels * (1 - core)]
            for r in inside_piece:
                columns = span(relayed[r])
                for kv in range(2):
                    stage[INNER, kv, :, columns] = chosen(lambda tile: inside[kv, tile, :, columns], wanted)
                for part in parts_of(r):
                    part_copy(INNER, MIRROR, r, part, core_peer).start()

        @pl.when(inner)
        def _():
            across_copy(w).wait_recv()

        tile_copy(CORE, CORE, wholes, w, core_peer).wait_recv()
        lax.fori_loop(first, first + size, early, 0)

    def landed_at(kv, columns):
        return jnp.concatenate([landed[slot, kv, :, columns] for slot, _ in landings], axis=0)

    def weigh(h, columns):
        scores = lax.dot_general(
            q_v[:, columns], landed_at(0, columns), (((1,), (1,)), ((), ())), preferred_element_type=jnp.float32)
        scores = scores + late_bias
        old = top[h][:, :1]
        peak = jnp.maximum(old, jnp.max(scores, axis=1, keepdims=True))
        raised = jnp.exp2((scores - peak) * factor)
        fade = jnp.exp2((old - peak) * factor)
        added = jnp.sum(raised, axis=1, keepdims=True) + fade * total[h][:, :1]
        return raised.astype(jnp.bfloat16), fade * acc[h], added

    def finish(columns, raised, faded, added):
        mixed = jnp.dot(raised, landed_at(1, columns), preferred_element_type=jnp.float32) + faded
        out_ref[:, columns] = (mixed / added).astype(out_ref.dtype)

    def late(h, carry):
        columns = pl.ds(pl.multiple_of(h * HD, HD), HD)
        finish(columns, *weigh(h, columns))
        return carry

    def sent(source, target, semaphore):
        pltpu.make_async_remote_copy(
            src_ref=source, dst_ref=target, send_sem=semaphore, recv_sem=semaphore,
            device_id={"frame": core_peer}, device_id_type=MESH).wait_send()

    def drain_early():
        for _, exists, here, _ in partners:
            @when(exists)
            def _():
                list_copy(core_peer, here, here).wait_send()
        for kv in range(2):
            @pl.when(inner)
            def _():
                sent((k_hbm, v_hbm)[kv], inside.at[kv], i_send.at[kv])
            for side in range(2):
                @pl.when(sides[side][0])
                def _():
                    sent((k_hbm, v_hbm)[kv], whole.at[side, kv], w_send.at[side, kv])
        early_slots = [(CORE, yes), (ACROSS, outer)] + [(slot, exists) for slot, _, exists, _, _ in end_sends]
        for slot, exists in early_slots:
            @when(exists)
            def _():
                sent(stage.at[slot], landed.at[CORE], t_send.at[slot])

    def drain():
        late_slots = [(INNER, outer)]
        late_slots += [(slot, exists) for slot, _, _, exists, _, _ in far_sends]
        late_slots += [(slot, exists) for slot, _, _, exists, _, _, _ in relays]
        late_slots += [(slot, exists) for slot, _, exists, _, _ in end_relays]
        for slot, exists in late_slots:
            @when(exists)
            def _():
                sent(stage.at[slot], landed.at[CORE], t_send.at[slot])

    def wait_landed(r, part):
        for slot, exists in landings:
            @when(exists)
            def _():
                part_copy(CORE, slot, r, part, core_peer).wait_recv()

    last = len(relayed) - 1
    for r in range(last):
        first, size = relayed[r]
        wait_landed(r, None)
        lax.fori_loop(first, first + size, late, 0)
        if r == 0:
            drain_early()
    first, size = relayed[last]
    wait_landed(last, 0)
    weighed = [weigh(h, span((h, 1))) for h in range(first, first + size)]
    drain()
    wait_landed(last, 1)
    for h, ready in zip(range(first, first + size), weighed):
        finish(span((h, 1)), *ready)


def write_out(in_ref, out_ref, sem):
    copy = pltpu.make_async_copy(in_ref, out_ref, sem)
    copy.start()
    copy.wait()


def solution(mesh):
    n = mesh.shape["frame"]

    def body(queries, key_heads, value_heads, tile_lists):
        rows, channels = queries.shape
        heads = channels // HD
        tiles = rows // TILE
        levels = tile_lists.shape[1] // 2
        far = max(levels - 4, 0)
        lists = 5 + 2 * far
        bf16, f32 = jnp.bfloat16, jnp.float32
        hbm = pl.BlockSpec(memory_space=pltpu.HBM)
        dma = pltpu.SemaphoreType.DMA
        out_slots, in_slots = OUT_NEAR + 2 * far, NEAR + 2 * far
        result = pl.pallas_call(
            functools.partial(kernel, n, levels, heads),
            out_shape=pltpu.VMEM((rows, channels), bf16),
            in_specs=[hbm, hbm, hbm, pl.BlockSpec(memory_space=pltpu.SMEM)],
            out_specs=pl.BlockSpec(memory_space=pltpu.VMEM),
            scratch_shapes=[
                pltpu.VMEM((rows, channels), bf16),
                pltpu.VMEM((tiles, TILE, channels), bf16),
                pltpu.VMEM((tiles, TILE, channels), bf16),
                pltpu.VMEM((2, 2, tiles, TILE, channels), bf16),
                pltpu.VMEM((2, tiles, TILE, channels), bf16),
                pltpu.VMEM((out_slots, 2, TILE, channels), bf16),
                pltpu.VMEM((in_slots, 2, TILE, channels), bf16),
                pltpu.SMEM((lists, 1, 2 * levels), jnp.int32),
                pltpu.VMEM((heads, rows, HD), f32),
                pltpu.VMEM((heads, rows, HD), f32),
                pltpu.VMEM((heads, rows, HD), f32),
                dma((2, 2)),
                dma((2, len(WHOLE_PIECES))),
                dma((2,)),
                dma((len(WHOLE_PIECES),)),
                dma((out_slots,)),
                dma((in_slots, len(RELAY_PIECES) + 1)),
                dma((lists,)),
                dma((lists,)),
                dma((3,)),
            ],
            compiler_params=pltpu.CompilerParams(
                collective_id=0, has_side_effects=True, vmem_limit_bytes=61 << 20
            ),
        )(
            queries,
            key_heads.reshape(tiles, TILE, channels),
            value_heads.reshape(tiles, TILE, channels),
            tile_lists,
        )
        return pl.pallas_call(
            write_out,
            out_shape=jax.ShapeDtypeStruct((rows, channels), bf16),
            in_specs=[pl.BlockSpec(memory_space=pltpu.VMEM)],
            out_specs=pl.BlockSpec(memory_space=pl.ANY),
            scratch_shapes=[dma],
            compiler_params=pltpu.CompilerParams(vmem_limit_bytes=4 << 20),
        )(result)

    in_specs = (
        P(("groups", "frame"), None),
        P(("groups", "frame"), None),
        P(("groups", "frame"), None),
        P("frame", None),
    )
    return jax.shard_map(
        body, mesh=mesh, in_specs=in_specs, out_specs=P(("groups", "frame"), None), check_vma=False
    )
```
